512 devices in a mesh: dp: 128 (over z, x, core), rep: 4 (over y).
Axes of the slice: x: 4, y: 4, z: 16, core: 2. Of those that a mesh axis runs over, the one named last changes fastest.
Arguments:
- gradient: bfloat16 [128, 4, 1024, 1024], P('dp', 'rep'), may hold values from -512 to 512
- owner_list: int32 [256, 1], replicated, may hold values from 0 to 127, as said below
- step_count: int32 [1], replicated, may hold values from 1 to 29
- master: float32 [128, 4, 4096], P('dp', None, 'rep'), may hold values from -3 to 3
- first_moment: float32 [128, 4, 4096], P('dp', None, 'rep'), may hold values from -6 to 6
- second_moment: float32 [128, 4, 4096], P('dp', None, 'rep'), may hold values from 0.25 to 4
Outputs:
- weights: bfloat16 [1024, 1024], replicated
- new_master: float32 [128, 4, 4096], P('dp', None, 'rep')
- new_first: float32 [128, 4, 4096], P('dp', None, 'rep')
- new_second: float32 [128, 4, 4096], P('dp', None, 'rep')
The draws below stay inside these ranges and needn't reach their ends.
Inputs may be any that keep to these rules, and one draw needn't show every extreme that they name: `owner_list`: every index along dp owns at least one block and at most 4; some index owns exactly 4.
All inputs are finite; a program needn't handle non-finite values.
Results may differ from the reference program's by a relative error of at most 0.0004.
Values may be sent and summed in bfloat16 or wider, within the bound.
A program may use at most 64 MiB of HBM per device.

```python
import math
import jax
import jax.numpy as jnp
from jax import lax

D = 1024
BROW = 4
ROWS = 1024
NBLK = 256
MOST = 4
BW = 4096
N_DP = 128
N_REP = 4


def owner_draw(key):
    keys = jax.random.split(jax.random.fold_in(key, 101), 3)
    group_count = N_DP // 4
    middle = jax.random.randint(keys[0], (group_count,), 1, MOST - 1)
    pattern = jnp.stack([jnp.full((group_count,), MOST, jnp.int32), middle.astype(jnp.int32), (MOST - 1 - middle).astype(jnp.int32), jnp.ones((group_count,), jnp.int32)], axis=1).reshape(N_DP)
    order = jax.random.permutation(keys[1], N_DP)
    counts = jnp.zeros((N_DP,), jnp.int32).at[order].set(pattern)
    ends = jnp.cumsum(counts)
    places = jnp.arange(NBLK, dtype=jnp.int32)
    sequence = jnp.sum((ends[None, :] <= places[:, None]).astype(jnp.int32), axis=1).astype(jnp.int32)
    shuffle = jax.random.permutation(keys[2], NBLK)
    return sequence[shuffle]


def draw_owner_list(key, part):
    return owner_draw(key)[:, None]


def hot_column(key):
    hot_keys = jax.random.split(jax.random.fold_in(key, 29), 3)
    hot_index = 2 * jax.random.randint(hot_keys[0], (), 0, D // 2) + 1
    hot_sign = jnp.where(jax.random.bernoulli(hot_keys[1]), 1.0, -1.0).astype(jnp.float32)
    hot_rows = jnp.exp(jnp.log(10.0) * jax.random.uniform(hot_keys[2], (ROWS, 1), jnp.float32))
    col_hit = (jnp.arange(D, dtype=jnp.int32) == hot_index).astype(jnp.float32)[None, :]
    return hot_sign * hot_rows * col_hit


def draw_gradient(key, part):
    owners = owner_draw(key)
    keys = jax.random.split(jax.random.fold_in(key, 17), 4)
    base = jax.random.normal(keys[0], (N_DP, N_REP, ROWS, D), jnp.float32)
    row_scale = jnp.exp(jnp.log(10.0) * jax.random.uniform(keys[1], (ROWS, 1), jnp.float32))
    col_scale = jnp.exp(jnp.log(4.0) * jax.random.uniform(keys[2], (1, D), jnp.float32))
    device_rise = jnp.power(3.0, jnp.arange(N_DP, dtype=jnp.float32) / max(N_DP - 1, 1))
    shuffled = jax.random.permutation(keys[3], NBLK)
    device_ids = jnp.arange(N_DP * N_REP, dtype=jnp.int32).reshape(N_DP, N_REP)
    target = shuffled[device_ids % NBLK]
    row_block = jnp.arange(ROWS, dtype=jnp.int32) // BROW
    replica_count = jnp.float32(N_DP * N_REP)
    spike_level = 2.0 * jnp.sqrt(replica_count)
    spiked = jnp.where(row_block[None, None, :] == target[:, :, None], spike_level, 1.0)[:, :, :, None]
    owner_frac = owners.astype(jnp.float32) / max(N_DP - 1, 1)
    hot_plane = hot_column(key)
    amplitude = 0.02
    ratio = amplitude / 0.5
    owner_amp = jnp.power(3.0, owner_frac)[row_block][:, None]
    hot_amp = ratio * jnp.sqrt(32.0 * jnp.float32(D) / replica_count)
    values = amplitude * base * row_scale * col_scale * owner_amp[None, None] * device_rise[:, None, None, None] * spiked + hot_amp * hot_plane[None, None]
    return jnp.clip(values, -512.0, 512.0).astype(jnp.bfloat16)


def shard_levels(stream_key, shape, shards, smallest, high):
    loudness, own = 1.0, jax.random.fold_in(stream_key, 6)
    for axis_at, shards_of in shards:
        heights = jnp.exp(jax.random.uniform(jax.random.fold_in(own, axis_at), (shards_of,), jnp.float32, smallest / len(shards), high / len(shards)))
        loudness = loudness * jnp.repeat(heights, shape[axis_at] // shards_of).reshape([-1 if axis == axis_at else 1 for axis in range(len(shape))])
    return loudness


def bell_draw(own_key, extent, spread, most, cuts=(), kind=jnp.bfloat16):
    result = jax.random.normal(own_key, extent, jnp.float32) * spread
    if len(cuts) > 0:
        result = shard_levels(own_key, extent, cuts, -0.22, 0.18) * result
    return jnp.clip(result, min=-most, max=most).astype(kind)


def setup_inputs(seed: int = 0) -> dict:
    streams_of = jax.random.split(jax.random.key(seed), 7)
    return {
        "gradient": draw_gradient(jax.random.fold_in(streams_of[6], 71), 0),
        "owner_list": draw_owner_list(jax.random.fold_in(streams_of[6], 71), 0),
        "step_count": jax.random.randint(streams_of[2], (1,), 1, 30).astype(jnp.int32),
        "master": bell_draw(streams_of[3], (N_DP, MOST, BW), 0.5, 3.0, ((0, 128), (2, 4)), jnp.float32),
        "first_moment": bell_draw(streams_of[4], (N_DP, MOST, BW), 1.0, 6.0, ((0, 128), (2, 4)), jnp.float32),
        "second_moment": jnp.clip(jnp.exp(math.log(4.0) - 2.7725887 * jax.random.uniform(streams_of[5], (N_DP, MOST, BW), jnp.float32) ** shard_levels(streams_of[5], (N_DP, MOST, BW), ((0, 128), (2, 4)), -0.2, 0.2)), 0.25, 4.0),
    }


def add_replica(carry, piece):
    return (carry + lax.optimization_barrier(jnp.sum(piece.astype(jnp.float32), axis=0)), None)

def reference(gradient, owner_list, step_count, master, first_moment, second_moment):
    summed, _ = lax.scan(add_replica, jnp.zeros((ROWS, D), jnp.float32), gradient)
    owner_of = owner_list[:, 0].astype(jnp.int32)
    block_ids = jnp.arange(NBLK, dtype=jnp.int32)
    earlier = (owner_of[:, None] == owner_of[None, :]) & (block_ids[None, :] < block_ids[:, None])
    slot_rank = lax.optimization_barrier(jnp.sum(earlier.astype(jnp.int32), axis=1))
    owner_hit = (owner_of[:, None] == jnp.arange(N_DP, dtype=jnp.int32)[None, :]).astype(jnp.float32)
    slot_hit = (slot_rank[:, None] == jnp.arange(MOST, dtype=jnp.int32)[None, :]).astype(jnp.float32)
    hits = owner_hit[:, :, None] * slot_hit[:, None, :]
    filled = (lax.optimization_barrier(jnp.sum(hits, axis=0)) > 0.5)[:, :, None]
    squares_total = jnp.sum(summed * summed)
    limit = jnp.sqrt(jnp.float32(ROWS * D))
    scale = limit / jnp.maximum(jnp.sqrt(squares_total), limit)
    blocks = summed.reshape(NBLK, BW)
    placed = jnp.einsum('bos,bw->osw', hits, blocks, precision=lax.Precision.HIGHEST)
    clipped = scale * placed
    new_first = jnp.where(filled, 0.9 * first_moment + 0.1 * clipped, 0.0)
    new_second = jnp.where(filled, 0.95 * second_moment + 0.05 * clipped * clipped, 0.0)
    step_value = step_count[0].astype(jnp.float32)
    first_fix = 1.0 - jnp.power(jnp.float32(0.9), step_value)
    second_fix = 1.0 - jnp.power(jnp.float32(0.95), step_value)
    update = new_first / first_fix / (jnp.sqrt(new_second / second_fix) + 1e-08)
    new_master = jnp.where(filled, master * (1.0 - 0.1 * 0.1) - 0.1 * update, 0.0)
    rows_back = jnp.einsum('bos,osw->bw', hits, new_master, precision=lax.Precision.HIGHEST)
    weights = rows_back.reshape(ROWS, D).astype(jnp.bfloat16)
    return (weights, new_master, new_first, new_second)
```

```python
import functools

import jax
import jax.numpy as jnp
from jax import lax
from jax.experimental import pallas as pl
from jax.experimental.pallas import tpu as pltpu
from jax.sharding import PartitionSpec as P

MESH = pl.DeviceIdType.MESH
F32 = jnp.float32
BF16 = jnp.bfloat16
HIGH = lax.Precision.HIGHEST
NZ = 16
NFLOW = 4
NSEM = 256


def flip1(v):
    return v + 1 - 2 * (v % 2)


def flip2(v):
    return (v + 2) % 4


def flip3(v):
    return 3 - v


def integer_power(base, count):
    result = jnp.ones((1, 1), F32)
    factor = jnp.float32(base)
    for bit in range(5):
        result = jnp.where((count // (2**bit)) % 2 == 1, result * factor, result)
        factor = factor * factor
    return result


def adam(total, master, first, second, scale, first_fix, second_fix):
    clipped = scale * total
    new_first = 0.9 * first + 0.1 * clipped
    new_second = 0.95 * second + 0.05 * clipped * clipped
    update = new_first / first_fix / (jnp.sqrt(new_second / second_fix) + 1e-08)
    new_master = master * (1.0 - 0.1 * 0.1) - 0.1 * update
    return new_master, new_first, new_second


def kernel(
    grad,
    owner_ref,
    step_ref,
    master_ref,
    first_ref,
    second_ref,
    w_out,
    nm_out,
    nf_out,
    ns_out,
    own_half,
    core_in,
    rows_f32,
    part,
    in1,
    in2,
    in3,
    in4,
    zsend,
    zin,
    sums,
    squares,
    sel_out,
    sel_in,
    opt_out,
    opt_in,
    opt_all,
    onehot,
    w_part,
    w_rows,
    local_sem,
    send_sem,
    recv_sem,
):
    d = lax.axis_index("dp")
    y = lax.axis_index("rep")
    z = d // 8
    w = d % 8
    x = w // 2
    c = d % 2
    slab = c * 4 + x

    def dev(zz, xx, cc, yy):
        return (zz * 8 + xx * 2 + cc, yy)

    counter = [0]

    def remote(src, dst, device):
        i = counter[0]
        counter[0] += 1
        return pltpu.make_async_remote_copy(
            src_ref=src,
            dst_ref=dst,
            send_sem=send_sem.at[i],
            recv_sem=recv_sem.at[i],
            device_id=device,
            device_id_type=MESH,
        )

    sent = []

    def start(copy):
        copy.start()
        sent.append(copy)
        return copy

    partner = dev(z, x, 1 - c, y)

    local = []
    for f in range(NFLOW):
        local.append(
            pltpu.make_async_copy(
                grad.at[pl.ds(256 * f, 256), pl.ds(pl.multiple_of(512 * c, 512), 512)],
                own_half.at[f],
                local_sem.at[f],
            )
        )
        local[f].start()

    barrier = pltpu.get_barrier_semaphore()
    q = (y * 4 + x) * 2 + c

    def slab_peer(o):
        p = (q + o) % 32
        return dev(z, (p // 2) % 4, p % 2, p // 8)

    for o in range(1, 32):
        pl.semaphore_signal(barrier, inc=1, device_id=slab_peer(o), device_id_type=MESH)
    for o in range(1, NZ):
        pl.semaphore_signal(
            barrier, inc=1, device_id=dev((z + o) % NZ, x, c, y), device_id_type=MESH
        )
    pl.semaphore_wait(barrier, 31 + NZ - 1)

    core_copies = []
    for f in range(NFLOW):
        core_copies.append(
            start(
                remote(
                    grad.at[
                        pl.ds(256 * f, 256), pl.ds(pl.multiple_of(512 * (1 - c), 512), 512)
                    ],
                    core_in.at[f],
                    partner,
                )
            )
        )

    def opt_cols(k):
        return (
            master_ref[0, :, 128 * k : 128 * k + 128],
            first_ref[0, :, 128 * k : 128 * k + 128],
            second_ref[0, :, 128 * k : 128 * k + 128],
        )

    for k in range(8):
        for a, piece in enumerate(opt_cols(k)):
            opt_out[k, a] = piece
    opt_copies = []
    for o in range(1, 8):
        wt = (w + o) % 8
        xt = wt // 2
        ct = wt % 2
        opt_copies.append(
            start(remote(opt_out.at[ct * 4 + xt], opt_in.at[o], dev(z, xt, ct, y)))
        )
    opt_in[0] = opt_out[slab]

    flows = []
    for f in range(NFLOW):
        along_x = f % 2 == 0
        s0, s1 = (flip1, flip3) if f < 2 else (flip3, flip1)
        c1, c2 = (x, y) if along_x else (y, x)
        peer_x = lambda v: dev(z, v, c, y)
        peer_y = lambda v: dev(z, x, c, v)
        peer1, peer2 = (peer_x, peer_y) if along_x else (peer_y, peer_x)
        flows.append((along_x, s0, s1, c1, c2, peer1, peer2))

    step1 = []
    for f in range(NFLOW):
        along_x, s0, s1, c1, c2, peer1, peer2 = flows[f]
        local[f].wait()
        core_copies[f].wait_recv()
        for kx in range(4):
            cols = slice(128 * kx, 128 * kx + 128)
            rows_f32[kx] = own_half[f, :, cols].astype(F32) + core_in[f, :, cols].astype(F32)
            for r in range(4):
                i, j = (kx, r) if along_x else (r, kx)
                part[f, i, j] = rows_f32[kx, pl.ds(r, 64, stride=4), :]
        p = s0(c1)
        a = start(remote(part.at[f, flip2(c1)], in1.at[f, 0], peer1(p)))
        b = start(remote(part.at[f, p], in1.at[f, 1], peer1(p)))
        step1.append((a, b))

    for o in range(1, 8):
        opt_copies[o - 1].wait_recv()
    for o in range(8):
        ws = (w + 8 - o) % 8
        for a in range(3):
            opt_all[z, a, pl.ds(ws * 4, 4), :] = opt_in[o, a]
    ring_r = []
    ring_l = []

    def ring_step(s):
        if s > 1:
            ring_r[s - 2].wait_recv()
            if s - 2 < len(ring_l):
                ring_l[s - 2].wait_recv()
        if s <= 8:
            at = (z + NZ - s + 1) % NZ
            ring_r.append(start(remote(opt_all.at[at], opt_all.at[at], dev((z + 1) % NZ, x, c, y))))
        if s <= 7:
            at = (z + s - 1) % NZ
            ring_l.append(
                start(remote(opt_all.at[at], opt_all.at[at], dev((z + NZ - 1) % NZ, x, c, y)))
            )

    ring_step(1)

    owner_col = jnp.broadcast_to(owner_ref[...], (256, 256))
    row_id = lax.broadcasted_iota(jnp.int32, (256, 256), 0)
    col_id = lax.broadcasted_iota(jnp.int32, (256, 256), 1)
    owner_row = jnp.sum(jnp.where(row_id == col_id, owner_col, 0), axis=0, keepdims=True)
    same = owner_col == owner_row
    rank_col = jnp.sum(
        jnp.where(same & (col_id < row_id), 1.0, 0.0), axis=1, keepdims=True
    ).astype(jnp.int32)
    rank_row = jnp.sum(jnp.where(same & (row_id < col_id), 1, 0), axis=0, keepdims=True)
    pos_col = owner_ref[...] * 4 + rank_col
    pos_row = owner_row * 4 + rank_row
    onehot[...] = (pos_col == lax.broadcasted_iota(jnp.int32, (256, 512), 1)).astype(F32)
    chosen = (
        pos_row == z * 32 + lax.broadcasted_iota(jnp.int32, (32, 256), 0)
    ).astype(F32)
    mine = (pos_row == d * 4 + lax.broadcasted_iota(jnp.int32, (4, 256), 0)).astype(F32)
    filled = jnp.sum(mine, axis=1, keepdims=True) > 0.5

    step2 = []
    for f in range(NFLOW):
        along_x, s0, s1, c1, c2, peer1, peer2 = flows[f]
        qq = s1(c1)
        step1[f][0].wait_recv()
        part[f, qq] = part[f, qq] + in1[f, 0]
        step2.append(start(remote(part.at[f, qq], in2.at[f], peer1(qq))))
    ring_step(2)
    step3 = []
    for f in range(NFLOW):
        along_x, s0, s1, c1, c2, peer1, peer2 = flows[f]
        p = s0(c2)
        step1[f][1].wait_recv()
        step2[f].wait_recv()
        part[f, c1] = part[f, c1] + in1[f, 1] + in2[f]
        a = start(remote(part.at[f, c1, flip2(c2)], in3.at[f, 0], peer2(p)))
        b = start(remote(part.at[f, c1, p], in3.at[f, 1], peer2(p)))
        step3.append((a, b))
        if f % 2 == 1:
            ring_step(3 + f // 2)
    step4 = []
    for f in range(NFLOW):
        along_x, s0, s1, c1, c2, peer1, peer2 = flows[f]
        qq = s1(c2)
        step3[f][0].wait_recv()
        part[f, c1, qq] = part[f, c1, qq] + in3[f, 0]
        step4.append(start(remote(part.at[f, c1, qq], in4.at[f], peer2(qq))))
    ring_step(5)
    for f in range(NFLOW):
        along_x, s0, s1, c1, c2, peer1, peer2 = flows[f]
        step3[f][1].wait_recv()
        step4[f].wait_recv()
        total = part[f, c1, c2] + in3[f, 1] + in4[f]
        for k in range(4):
            zsend[4 * f + k] = total[16 * k : 16 * k + 16]

    order = [8, 7, 9, 6, 10, 5, 11, 4, 12, 3, 13, 2, 14, 1, 15]
    zcopies = []
    for o in order:
        to = (z + o) % NZ
        zcopies.append(start(remote(zsend.at[to], zin.at[o], dev(to, x, c, y))))
    ring_step(6)
    ring_step(7)
    ring_step(8)
    for copy in zcopies:
        copy.wait_recv()
    zin[0] = zsend[z]
    sums[z] = jnp.sum(zin[...], axis=0)
    gathers = []
    for o in order:
        to = (z + o) % NZ
        gathers.append(start(remote(sums.at[z], sums.at[z], dev(to, x, c, y))))
    ring_step(9)
    states = []
    for a in range(3):
        table = opt_all[:, a].reshape(512, 128)
        states.append(jnp.dot(onehot[...], table, precision=HIGH, preferred_element_type=F32))
    for copy in gathers:
        copy.wait_recv()

    summed = sums[...].reshape(256, 128)
    squares[q] = jnp.sum((summed * summed).reshape(32, 8, 128), axis=0)
    norms = []
    for o in range(1, 32):
        norms.append(start(remote(squares.at[q], squares.at[q], slab_peer(o))))
    picked = jnp.dot(chosen, summed, precision=HIGH, preferred_element_type=F32)
    for k in range(8):
        sel_out[k] = picked[4 * k : 4 * k + 4]
    sel_copies = []
    for o in range(1, 8):
        wt = (w + o) % 8
        sel_copies.append(
            start(remote(sel_out.at[wt], sel_in.at[slab], dev(z, wt // 2, wt % 2, y)))
        )
    sel_in[slab] = sel_out[w]

    count = jnp.full((1, 1), step_ref[0], jnp.int32)
    first_fix = 1.0 - integer_power(0.9, count)
    second_fix = 1.0 - integer_power(0.95, count)
    for copy in norms:
        copy.wait_recv()
    squares_total = jnp.sum(jnp.sum(squares[...], axis=0), keepdims=True)
    limit = jnp.float32(1024.0)
    scale = limit / jnp.maximum(jnp.sqrt(squares_total), limit)
    new_slab, _, _ = adam(summed, *states, scale, first_fix, second_fix)
    rounded = new_slab.astype(BF16)

    ag = []
    for f in range(NFLOW):
        along_x, s0, s1, c1, c2, peer1, peer2 = flows[f]
        w_part[c, f, c1, c2] = rounded[64 * f : 64 * f + 64]
        p, qq = s0(c2), s1(c2)
        own = w_part.at[c, f, c1, c2]
        a = start(remote(own, own, peer2(qq)))
        b = start(remote(own, own, peer2(p)))
        ag.append((a, b))
    third = []
    for f in range(NFLOW):
        along_x, s0, s1, c1, c2, peer1, peer2 = flows[f]
        p, qq = s0(c2), s1(c2)
        ag[f][0].wait_recv()
        got = w_part.at[c, f, c1, qq]
        third.append(start(remote(got, got, peer2(p))))

    core_w = []

    def to_partner(piece):
        core_w.append(start(remote(piece, piece, partner)))

    wide = []
    for f in range(NFLOW):
        along_x, s0, s1, c1, c2, peer1, peer2 = flows[f]
        p, qq = s0(c1), s1(c1)
        ag[f][1].wait_recv()
        third[f].wait_recv()
        own = w_part.at[c, f, c1]
        a = start(remote(own, own, peer1(qq)))
        b = start(remote(own, own, peer1(p)))
        wide.append((a, b))
        to_partner(own)

    for copy in sel_copies:
        copy.wait_recv()
    for k in range(8):
        cols = slice(128 * k, 128 * k + 128)
        parts = adam(sel_in[k], *opt_cols(k), scale, first_fix, second_fix)
        for out, value in zip((nm_out, nf_out, ns_out), parts):
            out[0, :, cols] = jnp.where(filled, value, 0.0)

    last = []
    for f in range(NFLOW):
        along_x, s0, s1, c1, c2, peer1, peer2 = flows[f]
        p, qq = s0(c1), s1(c1)
        wide[f][0].wait_recv()
        got = w_part.at[c, f, qq]
        last.append(start(remote(got, got, peer1(p))))
        to_partner(got)
    for f in range(NFLOW):
        along_x, s0, s1, c1, c2, peer1, peer2 = flows[f]
        wide[f][1].wait_recv()
        to_partner(w_part.at[c, f, s0(c1)])
        last[f].wait_recv()
        to_partner(w_part.at[c, f, flip2(c1)])

    def assemble(f, kx, half):
        along_x = flows[f][0]
        for r in range(4):
            i, j = (kx, r) if along_x else (r, kx)
            w_rows[kx, pl.ds(r, 64, stride=4), :] = w_part[half, f, i, j].astype(F32)
        at = pl.multiple_of(512 * half + 128 * kx, 128)
        w_out[pl.ds(256 * f, 256), pl.ds(at, 128)] = w_rows[kx].astype(BF16)

    for f in range(NFLOW):
        for kx in range(4):
            assemble(f, kx, c)
    for copy in core_w:
        copy.wait_recv()
    for f in range(NFLOW):
        for kx in range(4):
            assemble(f, kx, 1 - c)
    for copy in sent:
        copy.wait_send()


def local_step(gradient, owner_list, step_count, master, first_moment, second_moment):
    vmem = pl.BlockSpec(memory_space=pltpu.VMEM)
    state = jax.ShapeDtypeStruct(master.shape, F32)
    return pl.pallas_call(
        kernel,
        out_shape=(jax.ShapeDtypeStruct((1024, 1024), BF16), state, state, state),
        in_specs=[
            pl.BlockSpec(memory_space=pl.ANY),
            vmem,
            pl.BlockSpec(memory_space=pltpu.SMEM),
            vmem,
            vmem,
            vmem,
        ],
        out_specs=(vmem, vmem, vmem, vmem),
        scratch_shapes=[
            pltpu.VMEM((NFLOW, 256, 512), BF16),
            pltpu.VMEM((NFLOW, 256, 512), BF16),
            pltpu.VMEM((4, 256, 128), F32),
            pltpu.VMEM((NFLOW, 4, 4, 64, 128), F32),
            pltpu.VMEM((NFLOW, 2, 4, 64, 128), F32),
            pltpu.VMEM((NFLOW, 4, 64, 128), F32),
            pltpu.VMEM((NFLOW, 2, 64, 128), F32),
            pltpu.VMEM((NFLOW, 64, 128), F32),
            pltpu.VMEM((NZ, 16, 128), F32),
            pltpu.VMEM((NZ, 16, 128), F32),
            pltpu.VMEM((NZ, 16, 128), F32),
            pltpu.VMEM((32, 8, 128), F32),
            pltpu.VMEM((8, 4, 128), F32),
            pltpu.VMEM((8, 4, 128), F32),
            pltpu.VMEM((8, 3, 4, 128), F32),
            pltpu.VMEM((8, 3, 4, 128), F32),
            pltpu.VMEM((NZ, 3, 32, 128), F32),
            pltpu.VMEM((256, 512), F32),
            pltpu.VMEM((2, NFLOW, 4, 4, 64, 128), BF16),
            pltpu.VMEM((4, 256, 128), F32),
            pltpu.SemaphoreType.DMA((NFLOW,)),
            pltpu.SemaphoreType.DMA((NSEM,)),
            pltpu.SemaphoreType.DMA((NSEM,)),
        ],
        compiler_params=pltpu.CompilerParams(collective_id=0, has_side_effects=True),
        name="adam_step",
    )(
        gradient.reshape(gradient.shape[2:]),
        owner_list,
        step_count,
        master,
        first_moment,
        second_moment,
    )


def solution(mesh):
    owned = P("dp", None, "rep")
    return jax.shard_map(
        local_step,
        mesh=mesh,
        in_specs=(P("dp", "rep", None, None), P(), P(), owned, owned, owned),
        out_specs=(P(), owned, owned, owned),
        check_vma=False,
    )
```

```python
import jax
import jax.numpy as jnp
from jax import lax
from jax.experimental import pallas as pl
from jax.experimental.pallas import tpu as pltpu
from jax.sharding import PartitionSpec as P

MESH = pl.DeviceIdType.MESH
F32 = jnp.float32
BF16 = jnp.bfloat16
HIGH = lax.Precision.HIGHEST
NZ = 16
FLOWS = (0, 2, 1, 3)


def flip1(v):
    return v + 1 - 2 * (v % 2)


def flip2(v):
    return (v + 2) % 4


def flip3(v):
    return 3 - v


def integer_power(base, count):
    result = jnp.ones((1, 1), F32)
    factor = jnp.float32(base)
    for bit in range(5):
        result = jnp.where((count // (2**bit)) % 2 == 1, result * factor, result)
        factor = factor * factor
    return result


def corrections(step_ref):
    count = jnp.full((1, 1), step_ref[0], jnp.int32)
    return 1.0 - integer_power(0.9, count), 1.0 - integer_power(0.95, count)


def adam(total, master, first, second, scale, first_fix, second_fix):
    clipped = scale * total
    new_first = 0.9 * first + 0.1 * clipped
    new_second = 0.95 * second + 0.05 * clipped * clipped
    update = new_first / first_fix / (jnp.sqrt(new_second / second_fix) + 1e-08)
    new_master = master * (1.0 - 0.1 * 0.1) - 0.1 * update
    return new_master, new_first, new_second


def reduce_kernel(
    grad,
    owner_ref,
    step_ref,
    master_ref,
    first_ref,
    second_ref,
    w_all,
    small,
    g,
    gy,
    tmp,
    in1x,
    in1y,
    core_out,
    core_in,
    part,
    in2,
    in3,
    zsend,
    zin,
    sums,
    sq1,
    sq2,
    sel_out,
    opt_out,
    opt_in,
    opt_all,
    onehot,
    w_part,
    load_sem,
    step1_sem,
    core_sem,
    step2_sem,
    dim2_sem,
    opt_sem,
    ring_sem,
    z_sem,
    norm_sem,
    ag2_sem,
    ag1_sem,
    out_sem,
    send_sem,
):
    d = lax.axis_index("dp")
    y = lax.axis_index("rep")
    z = d // 8
    w = d % 8
    x = w // 2
    c = d % 2
    slab = c * 4 + x

    def dev(zz, xx, cc, yy):
        return (zz * 8 + xx * 2 + cc, yy)

    def remote(src, dst, send, recv, device):
        copy = pltpu.make_async_remote_copy(
            src_ref=src,
            dst_ref=dst,
            send_sem=send,
            recv_sem=recv,
            device_id=device,
            device_id_type=MESH,
        )
        copy.start()
        return copy

    def drain(ref, sem):
        pltpu.make_async_copy(ref, ref, sem).wait()

    partner = dev(z, x, 1 - c, y)

    loads = {}
    for f in (1, 3, 0, 2):
        loads[f] = pltpu.make_async_copy(
            grad.at[pl.ds(256 * f, 256)], g.at[pl.ds(256 * f, 256)], load_sem.at[f]
        )
        loads[f].start()

    def xc_peer(o):
        t = (w + o) % 8
        return dev(z, t // 2, t % 2, y)

    right = dev((z + 1) % NZ, x, c, y)
    left = dev((z + NZ - 1) % NZ, x, c, y)

    barrier = pltpu.get_barrier_semaphore()
    near = [xc_peer(o) for o in range(1, 8)]
    near += [dev(z, x, c, (y + o) % 4) for o in range(1, 4)] + [right, left]
    for device in near:
        pl.semaphore_signal(barrier, inc=1, device_id=device, device_id_type=MESH)

    states_in = (master_ref, first_ref, second_ref)
    for k in range(8):
        for a in range(3):
            opt_out[k, a] = states_in[a][0, :, 128 * k : 128 * k + 128]

    pl.semaphore_wait(barrier, len(near))

    for o in range(1, 8):
        t = (w + o) % 8
        remote(
            opt_out.at[(t % 2) * 4 + t // 2], opt_in.at[o], send_sem.at[0], opt_sem.at[0], xc_peer(o)
        )
    opt_in[0] = opt_out[slab]

    flows = []
    for f in range(4):
        along_x = f % 2 == 0
        s0, s1 = (flip1, flip3) if f < 2 else (flip3, flip1)
        c1, c2 = (x, y) if along_x else (y, x)
        peer_x = lambda v: dev(z, v, c, y)
        peer_y = lambda v: dev(z, x, c, v)
        peer1, peer2 = (peer_x, peer_y) if along_x else (peer_y, peer_x)
        flows.append((along_x, s0(c1), s1(c1), c1, c2, peer1, peer2))

    def column(core, k):
        return pl.ds(pl.multiple_of(512 * core + 128 * k, 128), 128)

    step1 = {}

    def send_step1(f):
        along_x, p, qq, c1, c2, peer1, peer2 = flows[f]
        h = f // 2
        for k in range(4):
            index = flip2(c1) if k < 2 else p
            core = 1 - c if k % 2 == 0 else c
            if along_x:
                src = grad.at[pl.ds(256 * f, 256), column(core, index)]
                dst = in1x.at[h, k]
            else:
                src = gy.at[h, index, core]
                dst = in1y.at[h, k]
            step1[f, k] = remote(
                src, dst, send_sem.at[1 if along_x else 2], step1_sem.at[f, k], peer1(p)
            )

    send_step1(0)
    send_step1(2)
    for f in (1, 3):
        loads[f].wait()
        for k in range(8):
            tmp[k % 2] = g[256 * f : 256 * f + 256, 128 * k : 128 * k + 128].astype(F32)
            for r in range(4):
                gy[f // 2, r, k // 4, k % 4] = tmp[k % 2, pl.ds(r, 64, stride=4), :].astype(BF16)
        send_step1(f)

    drain(opt_in.at[pl.ds(1, 7)], opt_sem.at[0])
    for o in range(8):
        ws = (w + 8 - o) % 8
        for a in range(3):
            opt_all[z, a, pl.ds(ws * 4, 4), :] = opt_in[o, a]
    ring_r = []
    ring_l = []

    def ring_step():
        s = len(ring_r) + 1
        if s > 9:
            return
        if s > 1:
            ring_r[s - 2].wait_recv()
            if s - 2 < 7:
                ring_l[s - 2].wait_recv()
        if s <= 8:
            at = opt_all.at[(z + NZ - s + 1) % NZ]
            ring_r.append(remote(at, at, send_sem.at[3], ring_sem.at[0, s - 1], right))
        else:
            ring_r.append(None)
        if s <= 7:
            at = opt_all.at[(z + s - 1) % NZ]
            ring_l.append(remote(at, at, send_sem.at[3], ring_sem.at[1, s - 1], left))

    ring_step()
    loads[0].wait()
    loads[2].wait()

    def pair_sum(f, k, put):
        along_x, p, qq, c1, c2, peer1, peer2 = flows[f]
        h = f // 2
        index = qq if k < 2 else c1
        core = 1 - c if k % 2 == 0 else c
        step1[f, k].wait_recv()
        if along_x:
            own = g[256 * f : 256 * f + 256, column(core, index)]
            tmp[h] = own.astype(F32) + in1x[h, k].astype(F32)
            for r in range(4):
                put(r, tmp[h, pl.ds(r, 64, stride=4), :])
        else:
            for j in range(4):
                put(j, gy[h, index, core, j].astype(F32) + in1y[h, k, j].astype(F32))

    core = {}

    def to_core(f, half):
        def put(j, value):
            core_out[f, half, j] = value

        pair_sum(f, 2 * half, put)
        core[f, half] = remote(
            core_out.at[f, half],
            core_in.at[f, half],
            send_sem.at[4],
            core_sem.at[f, half],
            partner,
        )

    def keep(f, half):
        index = flows[f][2] if half == 0 else flows[f][3]

        def put(j, value):
            part[f, index, j] = value

        pair_sum(f, 2 * half + 1, put)

    step2 = {}
    for f in FLOWS:
        to_core(f, 0)
    for f in FLOWS:
        keep(f, 0)
    ring_step()
    for f in FLOWS:
        along_x, p, qq, c1, c2, peer1, peer2 = flows[f]
        core[f, 0].wait_recv()
        part[f, qq] = part[f, qq] + core_in[f, 0]
        step2[f] = remote(
            part.at[f, qq], in2.at[f], send_sem.at[5], step2_sem.at[f], peer1(qq)
        )
    for f in FLOWS:
        to_core(f, 1)
    ring_step()

    row_id = lax.broadcasted_iota(jnp.int32, (256, 256), 0)
    col_id = lax.broadcasted_iota(jnp.int32, (256, 256), 1)
    owner_row = jnp.broadcast_to(owner_ref[...].astype(F32), (256, 256))
    owner_col = jnp.sum(jnp.where(row_id == col_id, owner_row, 0.0), axis=1, keepdims=True)
    same = owner_col == owner_row
    rank_col = jnp.sum(jnp.where(same & (col_id < row_id), 1.0, 0.0), axis=1, keepdims=True)
    rank_row = jnp.sum(jnp.where(same & (row_id < col_id), 1.0, 0.0), axis=0, keepdims=True)
    pos_col = (owner_col * 4.0 + rank_col).astype(jnp.int32)
    pos_row = (owner_ref[...].astype(F32) * 4.0 + rank_row).astype(jnp.int32)
    onehot[...] = (pos_col == lax.broadcasted_iota(jnp.int32, (256, 512), 1)).astype(F32)
    chosen = (pos_row == z * 32 + lax.broadcasted_iota(jnp.int32, (32, 256), 0)).astype(F32)
    mine = (pos_row == d * 4 + lax.broadcasted_iota(jnp.int32, (4, 256), 0)).astype(F32)
    small[9] = jnp.broadcast_to(jnp.sum(mine, axis=1, keepdims=True), (4, 128))

    for f in FLOWS:
        keep(f, 1)
    ring_step()
    for f in FLOWS:
        along_x, p, qq, c1, c2, peer1, peer2 = flows[f]
        core[f, 1].wait_recv()
        step2[f].wait_recv()
        part[f, c1] = part[f, c1] + core_in[f, 1] + in2[f]
        for o in (2, 1, 3):
            to = (c2 + o) % 4
            remote(
                part.at[f, c1, to], in3.at[f, o - 1], send_sem.at[6], dim2_sem.at[f], peer2(to)
            )
    ring_step()
    ring_step()
    for f in FLOWS:
        along_x, p, qq, c1, c2, peer1, peer2 = flows[f]
        drain(in3.at[f], dim2_sem.at[f])
        total = part[f, c1, c2] + in3[f, 0] + in3[f, 1] + in3[f, 2]
        for k in range(4):
            zsend[4 * f + k] = total[16 * k : 16 * k + 16]
    ring_step()
    ring_step()
    ring_step()

    order = [8, 7, 9, 6, 10, 5, 11, 4, 12, 3, 13, 2, 14, 1, 15]
    for o in order:
        to = (z + o) % NZ
        remote(zsend.at[to], zin.at[o], send_sem.at[7], z_sem.at[0], dev(to, x, c, y))
    zin[0] = zsend[z]
    states = []
    for a in range(3):
        table = opt_all[:, a].reshape(512, 128)
        states.append(jnp.dot(onehot[...], table, precision=HIGH, preferred_element_type=F32))
    first_fix, second_fix = corrections(step_ref)
    drain(zin.at[pl.ds(1, 15)], z_sem.at[0])
    sums[z] = jnp.sum(zin[...], axis=0)
    for o in order:
        to = (z + o) % NZ
        remote(sums.at[z], sums.at[z], send_sem.at[8], z_sem.at[1], dev(to, x, c, y))
    drain(sums.at[pl.ds(0, 15)], z_sem.at[1])

    summed = sums[...].reshape(256, 128)
    sq1[w] = jnp.sum((summed * summed).reshape(32, 8, 128), axis=0)
    for o in range(1, 8):
        remote(sq1.at[w], sq1.at[w], send_sem.at[9], norm_sem.at[0], xc_peer(o))
    picked = jnp.dot(chosen, summed, precision=HIGH, preferred_element_type=F32)
    for k in range(8):
        sel_out[k] = picked[4 * k : 4 * k + 4]
    drain(sq1.at[pl.ds(0, 7)], norm_sem.at[0])
    sq2[y] = jnp.sum(sq1[...], axis=0)
    for o in (2, 1, 3):
        remote(sq2.at[y], sq2.at[y], send_sem.at[10], norm_sem.at[1], dev(z, x, c, (y + o) % 4))
    for o in range(1, 8):
        remote(
            sel_out.at[(w + o) % 8], small.at[slab], send_sem.at[11], norm_sem.at[2], xc_peer(o)
        )
    small[slab] = sel_out[w]
    drain(sq2.at[pl.ds(0, 3)], norm_sem.at[1])
    squares_total = jnp.sum(jnp.sum(sq2[...], axis=0), keepdims=True)
    limit = jnp.float32(1024.0)
    scale = limit / jnp.maximum(jnp.sqrt(squares_total), limit)
    rounded = adam(summed, *states, scale, first_fix, second_fix)[0].astype(BF16)

    for f in FLOWS:
        along_x, p, qq, c1, c2, peer1, peer2 = flows[f]
        w_part[f, c1, c2] = rounded[64 * f : 64 * f + 64]
        own = w_part.at[f, c1, c2]
        for o in (2, 1, 3):
            remote(own, own, send_sem.at[12], ag2_sem.at[f], peer2((c2 + o) % 4))
    small[8] = jnp.broadcast_to(scale, (4, 128))

    def give(f, index):
        piece = w_part.at[f, index]
        remote(piece, w_all.at[c, f, index], send_sem.at[14], out_sem.at[0], partner)
        pltpu.make_async_copy(piece, w_all.at[c, f, index], out_sem.at[1]).start()

    wide = {}
    for f in FLOWS:
        along_x, p, qq, c1, c2, peer1, peer2 = flows[f]
        drain(w_part.at[f, c1, pl.ds(0, 3)], ag2_sem.at[f])
        own = w_part.at[f, c1]
        wide[f, 0] = remote(own, own, send_sem.at[13], ag1_sem.at[f, 0], peer1(qq))
        wide[f, 1] = remote(own, own, send_sem.at[13], ag1_sem.at[f, 1], peer1(p))
        give(f, c1)
    for f in FLOWS:
        along_x, p, qq, c1, c2, peer1, peer2 = flows[f]
        wide[f, 0].wait_recv()
        got = w_part.at[f, qq]
        wide[f, 2] = remote(got, got, send_sem.at[13], ag1_sem.at[f, 2], peer1(p))
        give(f, qq)
    for f in FLOWS:
        wide[f, 1].wait_recv()
        give(f, flows[f][1])
    for f in FLOWS:
        wide[f, 2].wait_recv()
        give(f, flip2(flows[f][3]))

    drain(small.at[pl.ds(0, 7)], norm_sem.at[2])
    drain(opt_in.at[pl.ds(1, 7)], send_sem.at[0])
    drain(in1x, send_sem.at[1])
    drain(in1y, send_sem.at[2])
    drain(opt_all.at[pl.ds(0, 15)], send_sem.at[3])
    drain(core_out, send_sem.at[4])
    drain(in2, send_sem.at[5])
    drain(in3, send_sem.at[6])
    drain(zin.at[pl.ds(1, 15)], send_sem.at[7])
    drain(sums.at[pl.ds(0, 15)], send_sem.at[8])
    drain(sq1.at[pl.ds(0, 7)], send_sem.at[9])
    drain(sq2.at[pl.ds(0, 3)], send_sem.at[10])
    drain(sel_out.at[pl.ds(0, 7)], send_sem.at[11])
    drain(w_part.at[0, pl.ds(0, 3)], send_sem.at[12])
    drain(w_part.at[pl.ds(0, 3)], send_sem.at[13])
    drain(w_part, send_sem.at[14])
    drain(w_part, out_sem.at[1])
    drain(w_all.at[1 - c], out_sem.at[0])


def result_kernel(
    w_ref, small, step_ref, master_ref, first_ref, second_ref, w_out, nm_out, nf_out, ns_out, tmp
):
    f = pl.program_id(0)

    def assemble(along_x):
        for core in range(2):
            for k in range(4):
                for r in range(4):
                    i, j = (k, r) if along_x else (r, k)
                    tmp[k, pl.ds(r, 64, stride=4), :] = w_ref[core, 0, i, j].astype(F32)
                at = 512 * core + 128 * k
                w_out[:, at : at + 128] = tmp[k].astype(BF16)

    @pl.when(f % 2 == 0)
    def _():
        assemble(True)

    @pl.when(f % 2 == 1)
    def _():
        assemble(False)

    @pl.when(f == 0)
    def _():
        scale = small[8, :1, :1]
        filled = small[9] > 0.5
        fixes = corrections(step_ref)
        for k in range(8):
            cols = slice(128 * k, 128 * k + 128)
            olds = (master_ref[0, :, cols], first_ref[0, :, cols], second_ref[0, :, cols])
            parts = adam(small[k], *olds, scale, *fixes)
            for out, value in zip((nm_out, nf_out, ns_out), parts):
                out[0, :, cols] = jnp.where(filled, value, 0.0)


def local_step(gradient, owner_list, step_count, master, first_moment, second_moment):
    vmem = pl.BlockSpec(memory_space=pltpu.VMEM)
    smem = pl.BlockSpec(memory_space=pltpu.SMEM)
    anywhere = pl.BlockSpec(memory_space=pl.ANY)
    dma = pltpu.SemaphoreType.DMA
    w_all, small = pl.pallas_call(
        reduce_kernel,
        out_shape=(
            jax.ShapeDtypeStruct((2, 4, 4, 4, 64, 128), BF16),
            jax.ShapeDtypeStruct((10, 4, 128), F32),
        ),
        in_specs=[anywhere, vmem, smem, vmem, vmem, vmem],
        out_specs=(anywhere, vmem),
        scratch_shapes=[
            pltpu.VMEM((1024, 1024), BF16),
            pltpu.VMEM((2, 4, 2, 4, 64, 128), BF16),
            pltpu.VMEM((2, 256, 128), F32),
            pltpu.VMEM((2, 4, 256, 128), BF16),
            pltpu.VMEM((2, 4, 4, 64, 128), BF16),
            pltpu.VMEM((4, 2, 4, 64, 128), F32),
            pltpu.VMEM((4, 2, 4, 64, 128), F32),
            pltpu.VMEM((4, 4, 4, 64, 128), F32),
            pltpu.VMEM((4, 4, 64, 128), F32),
            pltpu.VMEM((4, 3, 64, 128), F32),
            pltpu.VMEM((NZ, 16, 128), F32),
            pltpu.VMEM((NZ, 16, 128), F32),
            pltpu.VMEM((NZ, 16, 128), F32),
            pltpu.VMEM((8, 8, 128), F32),
            pltpu.VMEM((4, 8, 128), F32),
            pltpu.VMEM((8, 4, 128), F32),
            pltpu.VMEM((8, 3, 4, 128), F32),
            pltpu.VMEM((8, 3, 4, 128), F32),
            pltpu.VMEM((NZ, 3, 32, 128), F32),
            pltpu.VMEM((256, 512), F32),
            pltpu.VMEM((4, 4, 4, 64, 128), BF16),
            dma((4,)),
            dma((4, 4)),
            dma((4, 2)),
            dma((4,)),
            dma((4,)),
            dma((1,)),
            dma((2, 8)),
            dma((2,)),
            dma((3,)),
            dma((4,)),
            dma((4, 3)),
            dma((2,)),
            dma((15,)),
        ],
        compiler_params=pltpu.CompilerParams(collective_id=0, has_side_effects=True),
        name="adam_reduce",
    )(
        gradient.reshape(gradient.shape[2:]),
        owner_list.reshape(1, owner_list.shape[0]),
        step_count,
        master,
        first_moment,
        second_moment,
    )
    state = jax.ShapeDtypeStruct(master.shape, F32)
    state_block = pl.BlockSpec(master.shape, lambda f: (0, 0, 0))
    return pl.pallas_call(
        result_kernel,
        grid=(4,),
        out_shape=(jax.ShapeDtypeStruct((1024, 1024), BF16), state, state, state),
        in_specs=[
            pl.BlockSpec((2, 1, 4, 4, 64, 128), lambda f: (0, f, 0, 0, 0, 0)),
            pl.BlockSpec((10, 4, 128), lambda f: (0, 0, 0)),
            smem,
            state_block,
            state_block,
            state_block,
        ],
        out_specs=(pl.BlockSpec((256, 1024), lambda f: (f, 0)), state_block, state_block, state_block),
        scratch_shapes=[pltpu.VMEM((4, 256, 128), F32)],
        name="adam_results",
    )(w_all, small, step_count, master, first_moment, second_moment)


def solution(mesh):
    owned = P("dp", None, "rep")
    return jax.shard_map(
        local_step,
        mesh=mesh,
        in_specs=(P("dp", "rep", None, None), P(), P(), owned, owned, owned),
        out_specs=(P(), owned, owned, owned),
        check_vma=False,
    )
```

```python
import jax
import jax.numpy as jnp
from jax import lax
from jax.experimental import pallas as pl
from jax.experimental.pallas import tpu as pltpu
from jax.sharding import PartitionSpec as P

MESH = pl.DeviceIdType.MESH
F32 = jnp.float32
BF16 = jnp.bfloat16
HIGH = lax.Precision.HIGHEST
NZ = 16
FLOWS = (0, 2, 1, 3)


def flip1(v):
    return v + 1 - 2 * (v % 2)


def flip2(v):
    return (v + 2) % 4


def flip3(v):
    return 3 - v


def integer_power(base, count):
    result = jnp.ones((1, 1), F32)
    factor = jnp.float32(base)
    for bit in range(5):
        result = jnp.where((count // (2**bit)) % 2 == 1, result * factor, result)
        factor = factor * factor
    return result


def corrections(step_ref):
    count = jnp.full((1, 1), step_ref[0], jnp.int32)
    return 1.0 - integer_power(0.9, count), 1.0 - integer_power(0.95, count)


def adam(total, master, first, second, scale, first_fix, second_fix):
    clipped = scale * total
    new_first = 0.9 * first + 0.1 * clipped
    new_second = 0.95 * second + 0.05 * clipped * clipped
    update = new_first / first_fix / (jnp.sqrt(new_second / second_fix) + 1e-08)
    new_master = master * (1.0 - 0.1 * 0.1) - 0.1 * update
    return new_master, new_first, new_second


def reduce_kernel(
    grad,
    owner_ref,
    step_ref,
    master_ref,
    first_ref,
    second_ref,
    w_all,
    small,
    g,
    gy,
    tmp,
    in1x,
    in1y,
    core_out,
    core_in,
    part,
    in2,
    in3,
    zsend,
    zin,
    sums,
    sq1,
    sq2,
    sel_out,
    opt_out,
    opt_in,
    opt_all,
    onehot,
    w_part,
    load_sem,
    step1_sem,
    core_sem,
    step2_sem,
    dim2_sem,
    opt_sem,
    ring_sem,
    z_sem,
    norm_sem,
    ag2_sem,
    ag1_sem,
    out_sem,
    send_sem,
    token_sem,
):
    d = lax.axis_index("dp")
    y = lax.axis_index("rep")
    z = d // 8
    w = d % 8
    x = w // 2
    c = d % 2
    slab = c * 4 + x

    def dev(zz, xx, cc, yy):
        return (zz * 8 + xx * 2 + cc, yy)

    def remote(src, dst, send, recv, device):
        copy = pltpu.make_async_remote_copy(
            src_ref=src,
            dst_ref=dst,
            send_sem=send,
            recv_sem=recv,
            device_id=device,
            device_id_type=MESH,
        )
        copy.start()
        return copy

    def drain(ref, sem):
        pltpu.make_async_copy(ref, ref, sem).wait()

    partner = dev(z, x, 1 - c, y)

    loads = {}
    for f in (1, 3, 0, 2):
        loads[f] = pltpu.make_async_copy(
            grad.at[pl.ds(256 * f, 256)], g.at[pl.ds(256 * f, 256)], load_sem.at[f]
        )
        loads[f].start()

    def xc_peer(o):
        t = (w + o) % 8
        return dev(z, t // 2, t % 2, y)

    right = dev((z + 1) % NZ, x, c, y)
    left = dev((z + NZ - 1) % NZ, x, c, y)

    barrier = pltpu.get_barrier_semaphore()
    near = [xc_peer(o) for o in range(1, 8)]
    near += [dev(z, x, c, (y + o) % 4) for o in range(1, 4)] + [right, left]
    for device in near:
        pl.semaphore_signal(barrier, inc=1, device_id=device, device_id_type=MESH)

    states_in = (master_ref, first_ref, second_ref)
    for k in range(8):
        for a in range(3):
            opt_out[k, a] = states_in[a][0, :, 128 * k : 128 * k + 128]

    pl.semaphore_wait(barrier, len(near))

    for o in range(1, 8):
        t = (w + o) % 8
        remote(
            opt_out.at[(t % 2) * 4 + t // 2], opt_in.at[o], send_sem.at[0], opt_sem.at[0], xc_peer(o)
        )
    opt_in[0] = opt_out[slab]

    flows = []
    for f in range(4):
        along_x = f % 2 == 0
        s0, s1 = (flip1, flip3) if f < 2 else (flip3, flip1)
        c1, c2 = (x, y) if along_x else (y, x)
        peer_x = lambda v: dev(z, v, c, y)
        peer_y = lambda v: dev(z, x, c, v)
        peer1, peer2 = (peer_x, peer_y) if along_x else (peer_y, peer_x)
        flows.append((along_x, s0(c1), s1(c1), c1, c2, peer1, peer2))

    def column(core, k):
        return pl.ds(pl.multiple_of(512 * core + 128 * k, 128), 128)

    step1 = {}

    def send_step1(f):
        along_x, p, qq, c1, c2, peer1, peer2 = flows[f]
        h = f // 2
        for k in range(4):
            index = flip2(c1) if k < 2 else p
            core = 1 - c if k % 2 == 0 else c
            if along_x:
                src = grad.at[pl.ds(256 * f, 256), column(core, index)]
                dst = in1x.at[h, k]
            else:
                src = gy.at[h, index, core]
                dst = in1y.at[h, k]
            step1[f, k] = remote(
                src, dst, send_sem.at[1 if along_x else 2], step1_sem.at[f, k], peer1(p)
            )

    send_step1(0)
    send_step1(2)
    for f in (1, 3):
        loads[f].wait()
        for k in range(8):
            tmp[k % 2] = g[256 * f : 256 * f + 256, 128 * k : 128 * k + 128].astype(F32)
            for r in range(4):
                gy[f // 2, r, k // 4, k % 4] = tmp[k % 2, pl.ds(r, 64, stride=4), :].astype(BF16)
        send_step1(f)

    drain(opt_in.at[pl.ds(1, 7)], opt_sem.at[0])
    for o in range(8):
        ws = (w + 8 - o) % 8
        for a in range(3):
            opt_all[z, a, pl.ds(ws * 4, 4), :] = opt_in[o, a]
    ring_r = []
    ring_l = []

    def token(i, distance):
        for to in ((z + distance) % NZ, (z + NZ - distance) % NZ):
            pl.semaphore_signal(
                token_sem.at[i], inc=1, device_id=dev(to, x, c, y), device_id_type=MESH
            )

    def ring_step():
        s = len(ring_r) + 1
        if s > 9:
            return
        if s > 1:
            ring_r[s - 2].wait_recv()
            if s - 2 < 7:
                ring_l[s - 2].wait_recv()
        if s <= 8:
            at = opt_all.at[(z + NZ - s + 1) % NZ]
            ring_r.append(remote(at, at, send_sem.at[3], ring_sem.at[0, s - 1], right))
        else:
            ring_r.append(None)
        if s <= 7:
            at = opt_all.at[(z + s - 1) % NZ]
            ring_l.append(remote(at, at, send_sem.at[3], ring_sem.at[1, s - 1], left))

    ring_step()
    loads[0].wait()
    loads[2].wait()

    def pair_sum(f, k, put):
        along_x, p, qq, c1, c2, peer1, peer2 = flows[f]
        h = f // 2
        index = qq if k < 2 else c1
        core = 1 - c if k % 2 == 0 else c
        step1[f, k].wait_recv()
        if along_x:
            own = g[256 * f : 256 * f + 256, column(core, index)]
            tmp[h] = own.astype(F32) + in1x[h, k].astype(F32)
            for r in range(4):
                put(r, tmp[h, pl.ds(r, 64, stride=4), :])
        else:
            for j in range(4):
                put(j, gy[h, index, core, j].astype(F32) + in1y[h, k, j].astype(F32))

    core = {}

    def to_core(f, half):
        def put(j, value):
            core_out[f, half, j] = value

        pair_sum(f, 2 * half, put)
        core[f, half] = remote(
            core_out.at[f, half],
            core_in.at[f, half],
            send_sem.at[4],
            core_sem.at[f, half],
            partner,
        )

    def keep(f, half):
        index = flows[f][2] if half == 0 else flows[f][3]

        def put(j, value):
            part[f, index, j] = value

        pair_sum(f, 2 * half + 1, put)

    step2 = {}
    for f in FLOWS:
        to_core(f, 0)
    for f in FLOWS:
        keep(f, 0)
    for f in FLOWS:
        along_x, p, qq, c1, c2, peer1, peer2 = flows[f]
        core[f, 0].wait_recv()
        part[f, qq] = part[f, qq] + core_in[f, 0]
        step2[f] = remote(
            part.at[f, qq], in2.at[f], send_sem.at[5], step2_sem.at[f], peer1(qq)
        )
    for f in FLOWS:
        to_core(f, 1)
    ring_step()
    token(0, 2)

    row_id = lax.broadcasted_iota(jnp.int32, (256, 256), 0)
    col_id = lax.broadcasted_iota(jnp.int32, (256, 256), 1)
    owner_row = jnp.broadcast_to(owner_ref[...].astype(F32), (256, 256))
    owner_col = jnp.sum(jnp.where(row_id == col_id, owner_row, 0.0), axis=1, keepdims=True)
    same = owner_col == owner_row
    rank_col = jnp.sum(jnp.where(same & (col_id < row_id), 1.0, 0.0), axis=1, keepdims=True)
    rank_row = jnp.sum(jnp.where(same & (row_id < col_id), 1.0, 0.0), axis=0, keepdims=True)
    pos_col = (owner_col * 4.0 + rank_col).astype(jnp.int32)
    pos_row = (owner_ref[...].astype(F32) * 4.0 + rank_row).astype(jnp.int32)
    onehot[...] = (pos_col == lax.broadcasted_iota(jnp.int32, (256, 512), 1)).astype(F32)
    chosen = (pos_row == z * 32 + lax.broadcasted_iota(jnp.int32, (32, 256), 0)).astype(F32)
    mine = (pos_row == d * 4 + lax.broadcasted_iota(jnp.int32, (4, 256), 0)).astype(F32)
    small[9] = jnp.broadcast_to(jnp.sum(mine, axis=1, keepdims=True), (4, 128))

    for f in FLOWS:
        keep(f, 1)
    for f in FLOWS:
        along_x, p, qq, c1, c2, peer1, peer2 = flows[f]
        core[f, 1].wait_recv()
        step2[f].wait_recv()
        part[f, c1] = part[f, c1] + core_in[f, 1] + in2[f]
        for o in (2, 1, 3):
            to = (c2 + o) % 4
            remote(
                part.at[f, c1, to], in3.at[f, o - 1], send_sem.at[6], dim2_sem.at[f], peer2(to)
            )
    ring_step()
    pl.semaphore_wait(token_sem.at[0], 2)
    token(1, 4)
    for f in FLOWS:
        along_x, p, qq, c1, c2, peer1, peer2 = flows[f]
        drain(in3.at[f], dim2_sem.at[f])
        total = part[f, c1, c2] + in3[f, 0] + in3[f, 1] + in3[f, 2]
        for k in range(4):
            zsend[4 * f + k] = total[16 * k : 16 * k + 16]
    pl.semaphore_wait(token_sem.at[1], 2)

    order = [8, 7, 9, 6, 10, 5, 11, 4, 12, 3, 13, 2, 14, 1, 15]
    for o in order:
        to = (z + o) % NZ
        remote(zsend.at[to], zin.at[o], send_sem.at[7], z_sem.at[0], dev(to, x, c, y))
    zin[0] = zsend[z]
    first_fix, second_fix = corrections(step_ref)
    ring_step()
    ring_step()
    drain(zin.at[pl.ds(1, 15)], z_sem.at[0])
    sums[z] = jnp.sum(zin[...], axis=0)
    for o in order:
        to = (z + o) % NZ
        remote(sums.at[z], sums.at[z], send_sem.at[8], z_sem.at[1], dev(to, x, c, y))
    ring_step()
    ring_step()
    drain(sums.at[pl.ds(0, 15)], z_sem.at[1])

    summed = sums[...].reshape(256, 128)
    sq1[w] = jnp.sum((summed * summed).reshape(32, 8, 128), axis=0)
    for o in range(1, 8):
        remote(sq1.at[w], sq1.at[w], send_sem.at[9], norm_sem.at[0], xc_peer(o))
    picked = jnp.dot(chosen, summed, precision=HIGH, preferred_element_type=F32)
    for k in range(8):
        sel_out[k] = picked[4 * k : 4 * k + 4]
    ring_step()
    drain(sq1.at[pl.ds(0, 7)], norm_sem.at[0])
    sq2[y] = jnp.sum(sq1[...], axis=0)
    for o in (2, 1, 3):
        remote(sq2.at[y], sq2.at[y], send_sem.at[10], norm_sem.at[1], dev(z, x, c, (y + o) % 4))
    for o in range(1, 8):
        remote(
            sel_out.at[(w + o) % 8], small.at[slab], send_sem.at[11], norm_sem.at[2], xc_peer(o)
        )
    small[slab] = sel_out[w]
    ring_step()
    states = []
    for a in range(3):
        table = opt_all[:, a].reshape(512, 128)
        states.append(jnp.dot(onehot[...], table, precision=HIGH, preferred_element_type=F32))
    drain(sq2.at[pl.ds(0, 3)], norm_sem.at[1])
    squares_total = jnp.sum(jnp.sum(sq2[...], axis=0), keepdims=True)
    limit = jnp.float32(1024.0)
    scale = limit / jnp.maximum(jnp.sqrt(squares_total), limit)
    rounded = adam(summed, *states, scale, first_fix, second_fix)[0].astype(BF16)

    def forward(f, j):
        along_x, p, qq, c1, c2, peer1, peer2 = flows[f]
        piece = w_part.at[f, c1, j]
        remote(piece, piece, send_sem.at[13], ag1_sem.at[f, 0], peer1(qq))
        remote(piece, piece, send_sem.at[13], ag1_sem.at[f, 1], peer1(p))

    ag2 = {}
    for f in FLOWS:
        along_x, p, qq, c1, c2, peer1, peer2 = flows[f]
        w_part[f, c1, c2] = rounded[64 * f : 64 * f + 64]
        own = w_part.at[f, c1, c2]
        for o in (2, 1, 3):
            ag2[f, o] = remote(
                own, own, send_sem.at[12], ag2_sem.at[f, o - 1], peer2((c2 + o) % 4)
            )
    for f in FLOWS:
        forward(f, flows[f][4])
    small[8] = jnp.broadcast_to(scale, (4, 128))

    def give(f, index):
        piece = w_part.at[f, index]
        remote(piece, w_all.at[c, f, index], send_sem.at[14], out_sem.at[0], partner)
        pltpu.make_async_copy(piece, w_all.at[c, f, index], out_sem.at[1]).start()

    for o in (1, 3, 2):
        for f in FLOWS:
            ag2[f, o].wait_recv()
            forward(f, (flows[f][4] + 4 - o) % 4)
    for f in FLOWS:
        give(f, flows[f][3])
    for f in FLOWS:
        along_x, p, qq, c1, c2, peer1, peer2 = flows[f]
        got = w_part.at[f, qq]
        drain(got, ag1_sem.at[f, 0])
        remote(got, got, send_sem.at[13], ag1_sem.at[f, 2], peer1(p))
        give(f, qq)
    for f in FLOWS:
        got = w_part.at[f, flows[f][1]]
        drain(got, ag1_sem.at[f, 1])
        give(f, flows[f][1])
    for f in FLOWS:
        got = w_part.at[f, flip2(flows[f][3])]
        drain(got, ag1_sem.at[f, 2])
        give(f, flip2(flows[f][3]))

    drain(small.at[pl.ds(0, 7)], norm_sem.at[2])
    drain(opt_in.at[pl.ds(1, 7)], send_sem.at[0])
    drain(in1x, send_sem.at[1])
    drain(in1y, send_sem.at[2])
    drain(opt_all.at[pl.ds(0, 15)], send_sem.at[3])
    drain(core_out, send_sem.at[4])
    drain(in2, send_sem.at[5])
    drain(in3, send_sem.at[6])
    drain(zin.at[pl.ds(1, 15)], send_sem.at[7])
    drain(sums.at[pl.ds(0, 15)], send_sem.at[8])
    drain(sq1.at[pl.ds(0, 7)], send_sem.at[9])
    drain(sq2.at[pl.ds(0, 3)], send_sem.at[10])
    drain(sel_out.at[pl.ds(0, 7)], send_sem.at[11])
    drain(w_part.at[0, pl.ds(0, 3)], send_sem.at[12])
    drain(w_part.at[pl.ds(0, 3)], send_sem.at[13])
    drain(w_part, send_sem.at[14])
    drain(w_part, out_sem.at[1])
    drain(w_all.at[1 - c], out_sem.at[0])


def result_kernel(
    w_all,
    small,
    step_ref,
    master_ref,
    first_ref,
    second_ref,
    w_out,
    nm_out,
    nf_out,
    ns_out,
    w_in,
    rows,
    tmp,
    in_sem,
    out_sem,
):
    loads = {}
    for f in range(4):
        for core in range(2):
            loads[f, core] = pltpu.make_async_copy(
                w_all.at[core, f], w_in.at[core, f], in_sem.at[f, core]
            )
            loads[f, core].start()
    scale = small[8, :1, :1]
    filled = small[9] > 0.5
    fixes = corrections(step_ref)
    for k in range(8):
        cols = slice(128 * k, 128 * k + 128)
        olds = (master_ref[0, :, cols], first_ref[0, :, cols], second_ref[0, :, cols])
        parts = adam(small[k], *olds, scale, *fixes)
        for out, value in zip((nm_out, nf_out, ns_out), parts):
            out[0, :, cols] = jnp.where(filled, value, 0.0)
    stores = []
    for f in range(4):
        for core in range(2):
            loads[f, core].wait()
            for k in range(4):
                for r in range(4):
                    i, j = (k, r) if f % 2 == 0 else (r, k)
                    tmp[k, pl.ds(r, 64, stride=4), :] = w_in[core, f, i, j].astype(F32)
                at = 512 * core + 128 * k
                rows[f, :, at : at + 128] = tmp[k].astype(BF16)
        stores.append(
            pltpu.make_async_copy(rows.at[f], w_out.at[pl.ds(256 * f, 256)], out_sem.at[f])
        )
        stores[f].start()
    for store in stores:
        store.wait()


def local_step(gradient, owner_list, step_count, master, first_moment, second_moment):
    vmem = pl.BlockSpec(memory_space=pltpu.VMEM)
    smem = pl.BlockSpec(memory_space=pltpu.SMEM)
    anywhere = pl.BlockSpec(memory_space=pl.ANY)
    dma = pltpu.SemaphoreType.DMA
    w_all, small = pl.pallas_call(
        reduce_kernel,
        out_shape=(
            jax.ShapeDtypeStruct((2, 4, 4, 4, 64, 128), BF16),
            jax.ShapeDtypeStruct((10, 4, 128), F32),
        ),
        in_specs=[anywhere, vmem, smem, vmem, vmem, vmem],
        out_specs=(anywhere, vmem),
        scratch_shapes=[
            pltpu.VMEM((1024, 1024), BF16),
            pltpu.VMEM((2, 4, 2, 4, 64, 128), BF16),
            pltpu.VMEM((2, 256, 128), F32),
            pltpu.VMEM((2, 4, 256, 128), BF16),
            pltpu.VMEM((2, 4, 4, 64, 128), BF16),
            pltpu.VMEM((4, 2, 4, 64, 128), F32),
            pltpu.VMEM((4, 2, 4, 64, 128), F32),
            pltpu.VMEM((4, 4, 4, 64, 128), F32),
            pltpu.VMEM((4, 4, 64, 128), F32),
            pltpu.VMEM((4, 3, 64, 128), F32),
            pltpu.VMEM((NZ, 16, 128), F32),
            pltpu.VMEM((NZ, 16, 128), F32),
            pltpu.VMEM((NZ, 16, 128), F32),
            pltpu.VMEM((8, 8, 128), F32),
            pltpu.VMEM((4, 8, 128), F32),
            pltpu.VMEM((8, 4, 128), F32),
            pltpu.VMEM((8, 3, 4, 128), F32),
            pltpu.VMEM((8, 3, 4, 128), F32),
            pltpu.VMEM((NZ, 3, 32, 128), F32),
            pltpu.VMEM((256, 512), F32),
            pltpu.VMEM((4, 4, 4, 64, 128), BF16),
            dma((4,)),
            dma((4, 4)),
            dma((4, 2)),
            dma((4,)),
            dma((4,)),
            dma((1,)),
            dma((2, 8)),
            dma((2,)),
            dma((3,)),
            dma((4, 3)),
            dma((4, 3)),
            dma((2,)),
            dma((15,)),
            pltpu.SemaphoreType.REGULAR((2,)),
        ],
        compiler_params=pltpu.CompilerParams(collective_id=0, has_side_effects=True),
        name="adam_reduce",
    )(
        gradient.reshape(gradient.shape[2:]),
        owner_list.reshape(1, owner_list.shape[0]),
        step_count,
        master,
        first_moment,
        second_moment,
    )
    state = jax.ShapeDtypeStruct(master.shape, F32)
    return pl.pallas_call(
        result_kernel,
        out_shape=(jax.ShapeDtypeStruct((1024, 1024), BF16), state, state, state),
        in_specs=[anywhere, vmem, smem, vmem, vmem, vmem],
        out_specs=(anywhere, vmem, vmem, vmem),
        scratch_shapes=[
            pltpu.VMEM((2, 4, 4, 4, 64, 128), BF16),
            pltpu.VMEM((4, 256, 1024), BF16),
            pltpu.VMEM((4, 256, 128), F32),
            dma((4, 2)),
            dma((4,)),
        ],
        name="adam_results",
    )(w_all, small, step_count, master, first_moment, second_moment)


def solution(mesh):
    owned = P("dp", None, "rep")
    return jax.shard_map(
        local_step,
        mesh=mesh,
        in_specs=(P("dp", "rep", None, None), P(), P(), owned, owned, owned),
        out_specs=(P(), owned, owned, owned),
        check_vma=False,
    )
```

```python
import jax
import jax.numpy as jnp
from jax import lax
from jax.experimental import pallas as pl
from jax.experimental.pallas import tpu as pltpu
from jax.sharding import PartitionSpec as P

MESH = pl.DeviceIdType.MESH
F32 = jnp.float32
BF16 = jnp.bfloat16
HIGH = lax.Precision.HIGHEST
NZ = 16
FLOWS = (0, 2, 1, 3)
GATHERED = [(d, None) for d in range(-7, 8) if d] + [(-8, 0), (8, 1)]


def flip1(v):
    return v + 1 - 2 * (v % 2)


def flip2(v):
    return (v + 2) % 4


def flip3(v):
    return 3 - v


def integer_power(base, count):
    result = jnp.ones((1, 1), F32)
    factor = jnp.float32(base)
    for bit in range(5):
        result = jnp.where((count // (2**bit)) % 2 == 1, result * factor, result)
        factor = factor * factor
    return result


def corrections(step_ref):
    count = jnp.full((1, 1), step_ref[0], jnp.int32)
    return 1.0 - integer_power(0.9, count), 1.0 - integer_power(0.95, count)


def adam(total, master, first, second, scale, first_fix, second_fix):
    clipped = scale * total
    new_first = 0.9 * first + 0.1 * clipped
    new_second = 0.95 * second + 0.05 * clipped * clipped
    update = new_first / first_fix / (jnp.sqrt(new_second / second_fix) + 1e-08)
    new_master = master * (1.0 - 0.1 * 0.1) - 0.1 * update
    return new_master, new_first, new_second


def reduce_kernel(
    grad,
    owner_hbm,
    step_ref,
    master_hbm,
    first_hbm,
    second_hbm,
    w_all,
    small_hbm,
    owner_ref,
    state_in,
    small,
    g,
    gy,
    tmp,
    in1x,
    in1y,
    core_out,
    core_in,
    part,
    in2,
    in3,
    zsend,
    zin,
    sums,
    squares,
    sel_out,
    opt_out,
    opt_in,
    opt_all,
    onehot,
    w_part,
    load_sem,
    step1_sem,
    core_sem,
    step2_sem,
    dim2_sem,
    opt_sem,
    gather_sem,
    z_sem,
    norm_sem,
    ag2_sem,
    ag1_sem,
    out_sem,
    send_sem,
    token_sem,
):
    d = lax.axis_index("dp")
    y = lax.axis_index("rep")
    z = d // 8
    w = d % 8
    x = w // 2
    c = d % 2
    slab = c * 4 + x
    q = y * 8 + w

    def dev(zz, xx, cc, yy):
        return (zz * 8 + xx * 2 + cc, yy)

    def remote(src, dst, send, recv, device):
        copy = pltpu.make_async_remote_copy(
            src_ref=src,
            dst_ref=dst,
            send_sem=send,
            recv_sem=recv,
            device_id=device,
            device_id_type=MESH,
        )
        copy.start()
        return copy

    def drain(ref, sem):
        pltpu.make_async_copy(ref, ref, sem).wait()

    partner = dev(z, x, 1 - c, y)

    inputs = []
    for i, (src, dst) in enumerate(
        (
            (master_hbm, state_in.at[0]),
            (first_hbm, state_in.at[1]),
            (second_hbm, state_in.at[2]),
            (owner_hbm, owner_ref),
        )
    ):
        inputs.append(pltpu.make_async_copy(src, dst, load_sem.at[4 + i]))
        inputs[i].start()
    loads = {}
    for f in (1, 3, 0, 2):
        loads[f] = pltpu.make_async_copy(
            grad.at[pl.ds(256 * f, 256)], g.at[pl.ds(256 * f, 256)], load_sem.at[f]
        )
        loads[f].start()

    def xc_peer(o):
        t = (w + o) % 8
        return dev(z, t // 2, t % 2, y)

    right = dev((z + 1) % NZ, x, c, y)
    left = dev((z + NZ - 1) % NZ, x, c, y)

    barrier = pltpu.get_barrier_semaphore()
    near = [xc_peer(o) for o in range(1, 8)]
    near += [dev(z, x, c, (y + o) % 4) for o in range(1, 4)] + [right, left]
    for device in near:
        pl.semaphore_signal(barrier, inc=1, device_id=device, device_id_type=MESH)

    for copy in inputs:
        copy.wait()
    for k in range(8):
        for a in range(3):
            opt_out[k % 4, k // 4, a] = state_in[a, 0, :, 128 * k : 128 * k + 128]

    def token(i, distance):
        for to in ((z + distance) % NZ, (z + NZ - distance) % NZ):
            pl.semaphore_signal(
                token_sem.at[i], inc=1, device_id=dev(to, x, c, y), device_id_type=MESH
            )

    pl.semaphore_wait(barrier, len(near))
    token(0, 1)

    for o in range(1, 4):
        xt = (x + o) % 4
        remote(opt_out.at[xt], opt_in.at[w], send_sem.at[0], opt_sem.at[0], dev(z, xt, 1, y))

    @pl.when(c == 0)
    def _():
        remote(opt_out.at[x], opt_in.at[w], send_sem.at[0], opt_sem.at[0], partner)

    @pl.when(c == 1)
    def _():
        opt_in[w] = opt_out[x]

    flows = []
    for f in range(4):
        along_x = f % 2 == 0
        s0, s1 = (flip1, flip3) if f < 2 else (flip3, flip1)
        c1, c2 = (x, y) if along_x else (y, x)
        peer_x = lambda v: dev(z, v, c, y)
        peer_y = lambda v: dev(z, x, c, v)
        peer1, peer2 = (peer_x, peer_y) if along_x else (peer_y, peer_x)
        flows.append((along_x, s0(c1), s1(c1), c1, c2, peer1, peer2))

    def column(core, k):
        return pl.ds(pl.multiple_of(512 * core + 128 * k, 128), 128)

    step1 = {}

    def send_step1(f):
        along_x, p, qq, c1, c2, peer1, peer2 = flows[f]
        h = f // 2
        for k in range(4):
            index = flip2(c1) if k < 2 else p
            core = 1 - c if k % 2 == 0 else c
            if along_x:
                src = grad.at[pl.ds(256 * f, 256), column(core, index)]
                dst = in1x.at[h, k]
            else:
                src = gy.at[h, index, core]
                dst = in1y.at[h, k]
            step1[f, k] = remote(
                src, dst, send_sem.at[1 if along_x else 2], step1_sem.at[f, k], peer1(p)
            )

    send_step1(0)
    send_step1(2)
    for f in (1, 3):
        loads[f].wait()
        for k in range(8):
            tmp[k % 2] = g[256 * f : 256 * f + 256, 128 * k : 128 * k + 128].astype(F32)
            for r in range(4):
                gy[f // 2, r, k // 4, k % 4] = tmp[k % 2, pl.ds(r, 64, stride=4), :].astype(BF16)
        send_step1(f)

    pl.semaphore_wait(token_sem.at[0], 2)
    token(1, 2)

    def pass_state(d, t, half=None):
        src = opt_all.at[(z + d + NZ) % NZ]
        if half is not None:
            src = src.at[:, :, pl.ds(16 * half, 16)]
        sem = gather_sem.at[GATHERED.index((d - t, half))]
        remote(src, src, send_sem.at[3], sem, dev((z + t + NZ) % NZ, x, c, y))

    def hand_over(d):
        src = opt_all.at[(z + d + NZ) % NZ, 0]
        remote(src, src, send_sem.at[10], opt_sem.at[1], partner)

    def take_state(*ds):
        for d in ds:
            if d == 8:
                for half in range(2):
                    drain(
                        opt_all.at[0, :, :, pl.ds(0, 16)],
                        gather_sem.at[GATHERED.index((8 * half * 2 - 8, half))],
                    )
            else:
                drain(opt_all.at[0], gather_sem.at[GATHERED.index((d, None))])

    def relay(s):
        for d in (-s, s):
            take_state(d)
            if s < 7:
                pass_state(d, 1 if d < 0 else -1)
            else:
                pass_state(d, 1 if d < 0 else -1, (d + 7) // 14)
        hand_over(-s)
        hand_over(s)

    pl.semaphore_wait(token_sem.at[1], 2)
    token(2, 4)

    @pl.when(c == 1)
    def _():
        drain(opt_in.at[pl.ds(0, 7)], opt_sem.at[0])
        for ws in range(8):
            for side in range(2):
                for a in range(3):
                    opt_all[z, side, a, 4 * ws : 4 * ws + 4] = opt_in[ws, side, a]
        for t in (1, -1, 4, -4):
            pass_state(0, t)
        hand_over(0)

    loads[0].wait()
    loads[2].wait()

    def pair_sum(f, k, put):
        along_x, p, qq, c1, c2, peer1, peer2 = flows[f]
        h = f // 2
        index = qq if k < 2 else c1
        core = 1 - c if k % 2 == 0 else c
        step1[f, k].wait_recv()
        if along_x:
            own = g[256 * f : 256 * f + 256, column(core, index)]
            tmp[h] = own.astype(F32) + in1x[h, k].astype(F32)
            for r in range(4):
                put(r, tmp[h, pl.ds(r, 64, stride=4), :])
        else:
            for j in range(4):
                put(j, gy[h, index, core, j].astype(F32) + in1y[h, k, j].astype(F32))

    core = {}

    def to_core(f, half):
        def put(j, value):
            core_out[f, half, j] = value

        pair_sum(f, 2 * half, put)
        core[f, half] = remote(
            core_out.at[f, half],
            core_in.at[f, half],
            send_sem.at[4],
            core_sem.at[f, half],
            partner,
        )

    def keep(f, half):
        index = flows[f][2] if half == 0 else flows[f][3]

        def put(j, value):
            part[f, index, j] = value

        pair_sum(f, 2 * half + 1, put)

    step2 = {}
    for f in FLOWS:
        to_core(f, 0)
    for f in FLOWS:
        keep(f, 0)
    for f in FLOWS:
        along_x, p, qq, c1, c2, peer1, peer2 = flows[f]
        core[f, 0].wait_recv()
        part[f, qq] = part[f, qq] + core_in[f, 0]
        step2[f] = remote(
            part.at[f, qq], in2.at[f], send_sem.at[5], step2_sem.at[f], peer1(qq)
        )
    @pl.when(c == 1)
    def _():
        relay(1)

    for f in FLOWS:
        to_core(f, 1)

    row_id = lax.broadcasted_iota(jnp.int32, (256, 256), 0)
    col_id = lax.broadcasted_iota(jnp.int32, (256, 256), 1)
    owner_row = jnp.broadcast_to(owner_ref[...].astype(F32), (256, 256))
    owner_col = jnp.sum(jnp.where(row_id == col_id, owner_row, 0.0), axis=1, keepdims=True)
    same = owner_col == owner_row
    rank_col = jnp.sum(jnp.where(same & (col_id < row_id), 1.0, 0.0), axis=1, keepdims=True)
    rank_row = jnp.sum(jnp.where(same & (row_id < col_id), 1.0, 0.0), axis=0, keepdims=True)
    pos_col = (owner_col * 4.0 + rank_col).astype(jnp.int32)
    pos_row = (owner_ref[...].astype(F32) * 4.0 + rank_row).astype(jnp.int32)
    onehot[...] = (pos_col == lax.broadcasted_iota(jnp.int32, (256, 512), 1)).astype(F32)
    chosen = (pos_row == z * 32 + lax.broadcasted_iota(jnp.int32, (32, 256), 0)).astype(F32)
    mine = (pos_row == d * 4 + lax.broadcasted_iota(jnp.int32, (4, 256), 0)).astype(F32)
    small[9] = jnp.broadcast_to(jnp.sum(mine, axis=1, keepdims=True), (4, 128))

    for f in FLOWS:
        keep(f, 1)
    for f in FLOWS:
        along_x, p, qq, c1, c2, peer1, peer2 = flows[f]
        core[f, 1].wait_recv()
        step2[f].wait_recv()
        part[f, c1] = part[f, c1] + core_in[f, 1] + in2[f]
        for o in (2, 1, 3):
            to = (c2 + o) % 4
            remote(
                part.at[f, c1, to], in3.at[f, o - 1], send_sem.at[6], dim2_sem.at[f], peer2(to)
            )
        if f == 0:

            @pl.when(c == 1)
            def _():
                for d in (-4, 4):
                    take_state(d)
                    pass_state(d, 1 if d < 0 else -1)
                    pass_state(d, -1 if d < 0 else 1)
                    hand_over(d)

    for f in FLOWS:
        along_x, p, qq, c1, c2, peer1, peer2 = flows[f]
        drain(in3.at[f], dim2_sem.at[f])
        total = part[f, c1, c2] + in3[f, 0] + in3[f, 1] + in3[f, 2]
        for k in range(4):
            zsend[4 * f + k] = total[16 * k : 16 * k + 16]
    pl.semaphore_wait(token_sem.at[2], 2)

    order = [8, 7, 9, 6, 10, 5, 11, 4, 12, 3, 13, 2, 14, 1, 15]
    for o in order:
        to = (z + o) % NZ
        remote(zsend.at[to], zin.at[o], send_sem.at[7], z_sem.at[0], dev(to, x, c, y))
    zin[0] = zsend[z]

    @pl.when(c == 1)
    def _():
        relay(5)
        relay(6)

    first_fix, second_fix = corrections(step_ref)
    drain(zin.at[pl.ds(1, 15)], z_sem.at[0])
    sums[z] = jnp.sum(zin[...], axis=0)
    for o in order:
        to = (z + o) % NZ
        remote(sums.at[z], sums.at[z], send_sem.at[8], z_sem.at[1], dev(to, x, c, y))

    @pl.when(c == 1)
    def _():
        for d in (-2, 2, -3, 3):
            take_state(d)
            hand_over(d)
        relay(7)
        take_state(8)
        hand_over(8)

    drain(sums.at[pl.ds(0, 15)], z_sem.at[1])

    summed = sums[...].reshape(256, 128)
    squares[q] = jnp.sum(summed * summed, axis=0, keepdims=True)
    for o in range(1, 32):
        t = (q + o) % 32
        remote(
            squares.at[q],
            squares.at[q],
            send_sem.at[9],
            norm_sem.at[0],
            dev(z, (t // 2) % 4, t % 2, t // 8),
        )
    picked = jnp.dot(chosen, summed, precision=HIGH, preferred_element_type=F32)
    for k in range(8):
        sel_out[k] = picked[4 * k : 4 * k + 4]
    for o in range(1, 8):
        remote(
            sel_out.at[(w + o) % 8], small.at[slab], send_sem.at[11], norm_sem.at[1], xc_peer(o)
        )
    small[slab] = sel_out[w]

    @pl.when(c == 0)
    def _():
        drain(opt_all.at[pl.ds(0, 8)], opt_sem.at[1])

    states = []
    for a in range(3):
        table = opt_all[:, c, a].reshape(512, 128)
        states.append(jnp.dot(onehot[...], table, precision=HIGH, preferred_element_type=F32))
    drain(squares.at[pl.ds(0, 31)], norm_sem.at[0])
    squares_total = jnp.sum(jnp.sum(squares[...], axis=0), keepdims=True)
    limit = jnp.float32(1024.0)
    scale = limit / jnp.maximum(jnp.sqrt(squares_total), limit)
    rounded = adam(summed, *states, scale, first_fix, second_fix)[0].astype(BF16)

    def forward(f, j):
        along_x, p, qq, c1, c2, peer1, peer2 = flows[f]
        piece = w_part.at[f, c1, j]
        remote(piece, piece, send_sem.at[13], ag1_sem.at[f, 0], peer1(qq))
        remote(piece, piece, send_sem.at[13], ag1_sem.at[f, 1], peer1(p))

    ag2 = {}
    for f in FLOWS:
        along_x, p, qq, c1, c2, peer1, peer2 = flows[f]
        w_part[f, c1, c2] = rounded[64 * f : 64 * f + 64]
        own = w_part.at[f, c1, c2]
        for o in (2, 1, 3):
            ag2[f, o] = remote(
                own, own, send_sem.at[12], ag2_sem.at[f, o - 1], peer2((c2 + o) % 4)
            )
    for f in FLOWS:
        forward(f, flows[f][4])
    small[8] = jnp.broadcast_to(scale, (4, 128))

    def give(f, index):
        piece = w_part.at[f, index]
        remote(piece, w_all.at[c, f, index], send_sem.at[14], out_sem.at[0], partner)
        pltpu.make_async_copy(piece, w_all.at[c, f, index], out_sem.at[1]).start()

    for o in (1, 3, 2):
        for f in FLOWS:
            ag2[f, o].wait_recv()
            forward(f, (flows[f][4] + 4 - o) % 4)
    for f in FLOWS:
        give(f, flows[f][3])
    drain(small.at[pl.ds(0, 7)], norm_sem.at[1])
    small_copy = pltpu.make_async_copy(small, small_hbm, out_sem.at[2])
    small_copy.start()
    for f in FLOWS:
        along_x, p, qq, c1, c2, peer1, peer2 = flows[f]
        got = w_part.at[f, qq]
        drain(got, ag1_sem.at[f, 0])
        remote(got, got, send_sem.at[13], ag1_sem.at[f, 2], peer1(p))
        give(f, qq)
    for f in FLOWS:
        got = w_part.at[f, flows[f][1]]
        drain(got, ag1_sem.at[f, 1])
        give(f, flows[f][1])
    for f in FLOWS:
        got = w_part.at[f, flip2(flows[f][3])]
        drain(got, ag1_sem.at[f, 2])
        give(f, flip2(flows[f][3]))

    small_copy.wait()

    @pl.when(c == 0)
    def _():
        drain(opt_out, send_sem.at[0])

    @pl.when(c == 1)
    def _():
        drain(opt_out.at[pl.ds(0, 3)], send_sem.at[0])
        drain(opt_all.at[pl.ds(0, 15)], send_sem.at[3])
        drain(opt_all.at[pl.ds(0, 8)], send_sem.at[10])

    drain(in1x, send_sem.at[1])
    drain(in1y, send_sem.at[2])
    drain(core_out, send_sem.at[4])
    drain(in2, send_sem.at[5])
    drain(in3, send_sem.at[6])
    drain(zin.at[pl.ds(1, 15)], send_sem.at[7])
    drain(sums.at[pl.ds(0, 15)], send_sem.at[8])
    drain(squares.at[pl.ds(0, 31)], send_sem.at[9])
    drain(sel_out.at[pl.ds(0, 7)], send_sem.at[11])
    drain(w_part.at[0, pl.ds(0, 3)], send_sem.at[12])
    drain(w_part.at[pl.ds(0, 3)], send_sem.at[13])
    drain(w_part, send_sem.at[14])
    drain(w_part, out_sem.at[1])
    drain(w_all.at[1 - c], out_sem.at[0])


def result_kernel(
    w_all,
    small_hbm,
    step_ref,
    master_hbm,
    first_hbm,
    second_hbm,
    w_out,
    nm_out,
    nf_out,
    ns_out,
    small,
    state_in,
    state_out,
    w_in,
    rows,
    tmp,
    load_sem,
    in_sem,
    out_sem,
):
    inputs = []
    for i, (src, dst) in enumerate(
        (
            (small_hbm, small),
            (master_hbm, state_in.at[0]),
            (first_hbm, state_in.at[1]),
            (second_hbm, state_in.at[2]),
        )
    ):
        inputs.append(pltpu.make_async_copy(src, dst, load_sem.at[i]))
        inputs[i].start()
    loads = {}
    for f in range(4):
        for core in range(2):
            loads[f, core] = pltpu.make_async_copy(
                w_all.at[core, f], w_in.at[core, f], in_sem.at[f, core]
            )
            loads[f, core].start()
    fixes = corrections(step_ref)
    for copy in inputs:
        copy.wait()
    scale = small[8, :1, :1]
    filled = small[9] > 0.5
    for k in range(8):
        cols = slice(128 * k, 128 * k + 128)
        olds = [state_in[a, 0, :, cols] for a in range(3)]
        for a, value in enumerate(adam(small[k], *olds, scale, *fixes)):
            state_out[a, 0, :, cols] = jnp.where(filled, value, 0.0)
    stores = []
    for a, out in enumerate((nm_out, nf_out, ns_out)):
        stores.append(pltpu.make_async_copy(state_out.at[a], out, out_sem.at[8 + a]))
    for f in range(4):
        for core in range(2):
            loads[f, core].wait()
            for k in range(4):
                for r in range(4):
                    i, j = (k, r) if f % 2 == 0 else (r, k)
                    tmp[k, pl.ds(r, 64, stride=4), :] = w_in[core, f, i, j].astype(F32)
                at = 512 * core + 128 * k
                rows[f, :, at : at + 128] = tmp[k].astype(BF16)
            cols = pl.ds(512 * core, 512)
            stores.append(
                pltpu.make_async_copy(
                    rows.at[f, :, cols],
                    w_out.at[pl.ds(256 * f, 256), cols],
                    out_sem.at[2 * f + core],
                )
            )
            stores[-1].start()
            if f == 0 and core == 0:
                for store in stores[:3]:
                    store.start()
    for store in stores:
        store.wait()


def local_step(gradient, owner_list, step_count, master, first_moment, second_moment):
    smem = pl.BlockSpec(memory_space=pltpu.SMEM)
    anywhere = pl.BlockSpec(memory_space=pl.ANY)
    dma = pltpu.SemaphoreType.DMA
    w_all, small = pl.pallas_call(
        reduce_kernel,
        out_shape=(
            jax.ShapeDtypeStruct((2, 4, 4, 4, 64, 128), BF16),
            jax.ShapeDtypeStruct((10, 4, 128), F32),
        ),
        in_specs=[anywhere, anywhere, smem, anywhere, anywhere, anywhere],
        out_specs=(anywhere, anywhere),
        scratch_shapes=[
            pltpu.VMEM((1, owner_list.shape[0]), jnp.int32),
            pltpu.VMEM((3, *master.shape), F32),
            pltpu.VMEM((10, 4, 128), F32),
            pltpu.VMEM((1024, 1024), BF16),
            pltpu.VMEM((2, 4, 2, 4, 64, 128), BF16),
            pltpu.VMEM((2, 256, 128), F32),
            pltpu.VMEM((2, 4, 256, 128), BF16),
            pltpu.VMEM((2, 4, 4, 64, 128), BF16),
            pltpu.VMEM((4, 2, 4, 64, 128), F32),
            pltpu.VMEM((4, 2, 4, 64, 128), F32),
            pltpu.VMEM((4, 4, 4, 64, 128), F32),
            pltpu.VMEM((4, 4, 64, 128), F32),
            pltpu.VMEM((4, 3, 64, 128), F32),
            pltpu.VMEM((NZ, 16, 128), F32),
            pltpu.VMEM((NZ, 16, 128), F32),
            pltpu.VMEM((NZ, 16, 128), F32),
            pltpu.VMEM((32, 1, 128), F32),
            pltpu.VMEM((8, 4, 128), F32),
            pltpu.VMEM((4, 2, 3, 4, 128), F32),
            pltpu.VMEM((8, 2, 3, 4, 128), F32),
            pltpu.VMEM((NZ, 2, 3, 32, 128), F32),
            pltpu.VMEM((256, 512), F32),
            pltpu.VMEM((4, 4, 4, 64, 128), BF16),
            dma((8,)),
            dma((4, 4)),
            dma((4, 2)),
            dma((4,)),
            dma((4,)),
            dma((2,)),
            dma((16,)),
            dma((2,)),
            dma((2,)),
            dma((4, 3)),
            dma((4, 3)),
            dma((3,)),
            dma((15,)),
            pltpu.SemaphoreType.REGULAR((3,)),
        ],
        compiler_params=pltpu.CompilerParams(collective_id=0, has_side_effects=True),
        name="adam_reduce",
    )(
        gradient.reshape(gradient.shape[2:]),
        owner_list.reshape(1, owner_list.shape[0]),
        step_count,
        master,
        first_moment,
        second_moment,
    )
    state = jax.ShapeDtypeStruct(master.shape, F32)
    return pl.pallas_call(
        result_kernel,
        out_shape=(jax.ShapeDtypeStruct((1024, 1024), BF16), state, state, state),
        in_specs=[anywhere, anywhere, smem, anywhere, anywhere, anywhere],
        out_specs=(anywhere, anywhere, anywhere, anywhere),
        scratch_shapes=[
            pltpu.VMEM((10, 4, 128), F32),
            pltpu.VMEM((3, *master.shape), F32),
            pltpu.VMEM((3, *master.shape), F32),
            pltpu.VMEM((2, 4, 4, 4, 64, 128), BF16),
            pltpu.VMEM((4, 256, 1024), BF16),
            pltpu.VMEM((4, 256, 128), F32),
            dma((4,)),
            dma((4, 2)),
            dma((11,)),
        ],
        name="adam_results",
    )(w_all, small, step_count, master, first_moment, second_moment)


def solution(mesh):
    owned = P("dp", None, "rep")
    return jax.shard_map(
        local_step,
        mesh=mesh,
        in_specs=(P("dp", "rep", None, None), P(), P(), owned, owned, owned),
        out_specs=(P(), owned, owned, owned),
        check_vma=False,
    )
```

```python
import jax
import jax.numpy as jnp
from jax import lax
from jax.experimental import pallas as pl
from jax.experimental.pallas import tpu as pltpu
from jax.sharding import PartitionSpec as P

MESH = pl.DeviceIdType.MESH
F32 = jnp.float32
BF16 = jnp.bfloat16
HIGH = lax.Precision.HIGHEST
NZ = 16
FLOWS = (0, 2, 1, 3)
GATHERED = [(d, None) for d in range(-7, 8) if d] + [(-8, 0), (8, 1)]


def flip1(v):
    return v + 1 - 2 * (v % 2)


def flip2(v):
    return (v + 2) % 4


def flip3(v):
    return 3 - v


def integer_power(base, count):
    result = jnp.ones((1, 1), F32)
    factor = jnp.float32(base)
    for bit in range(5):
        result = jnp.where((count // (2**bit)) % 2 == 1, result * factor, result)
        factor = factor * factor
    return result


def corrections(step_ref):
    count = jnp.full((1, 1), step_ref[0], jnp.int32)
    return 1.0 - integer_power(0.9, count), 1.0 - integer_power(0.95, count)


def adam(total, master, first, second, scale, first_fix, second_fix):
    clipped = scale * total
    new_first = 0.9 * first + 0.1 * clipped
    new_second = 0.95 * second + 0.05 * clipped * clipped
    update = new_first / first_fix / (jnp.sqrt(new_second / second_fix) + 1e-08)
    new_master = master * (1.0 - 0.1 * 0.1) - 0.1 * update
    return new_master, new_first, new_second


def reduce_kernel(
    grad,
    owner_hbm,
    step_ref,
    master_hbm,
    first_hbm,
    second_hbm,
    w_all,
    small_hbm,
    owner_ref,
    state_in,
    small,
    g,
    gy,
    tmp,
    in1x,
    in1y,
    core_out,
    core_in,
    part,
    in2,
    in3,
    zsend,
    zin,
    sums,
    squares,
    sel_out,
    opt_out,
    opt_in,
    opt_all,
    onehot,
    w_part,
    load_sem,
    step1_sem,
    core_sem,
    step2_sem,
    dim2_sem,
    opt_sem,
    gather_sem,
    z_sem,
    norm_sem,
    ag2_sem,
    ag1_sem,
    out_sem,
    send_sem,
    token_sem,
):
    d = lax.axis_index("dp")
    y = lax.axis_index("rep")
    z = d // 8
    w = d % 8
    x = w // 2
    c = d % 2
    slab = c * 4 + x
    q = y * 8 + w

    def dev(zz, xx, cc, yy):
        return (zz * 8 + xx * 2 + cc, yy)

    def remote(src, dst, send, recv, device):
        copy = pltpu.make_async_remote_copy(
            src_ref=src,
            dst_ref=dst,
            send_sem=send,
            recv_sem=recv,
            device_id=device,
            device_id_type=MESH,
        )
        copy.start()
        return copy

    def drain(ref, sem):
        pltpu.make_async_copy(ref, ref, sem).wait()

    partner = dev(z, x, 1 - c, y)

    inputs = []
    for i, (src, dst) in enumerate(
        (
            (master_hbm, state_in.at[0]),
            (first_hbm, state_in.at[1]),
            (second_hbm, state_in.at[2]),
            (owner_hbm, owner_ref),
        )
    ):
        inputs.append(pltpu.make_async_copy(src, dst, load_sem.at[4 + i]))
        inputs[i].start()
    loads = {}
    for f in (1, 3, 0, 2):
        loads[f] = pltpu.make_async_copy(
            grad.at[pl.ds(256 * f, 256)], g.at[pl.ds(256 * f, 256)], load_sem.at[f]
        )
        loads[f].start()

    def xc_peer(o):
        t = (w + o) % 8
        return dev(z, t // 2, t % 2, y)

    right = dev((z + 1) % NZ, x, c, y)
    left = dev((z + NZ - 1) % NZ, x, c, y)

    barrier = pltpu.get_barrier_semaphore()
    near = [xc_peer(o) for o in range(1, 8)]
    near += [dev(z, x, c, (y + o) % 4) for o in range(1, 4)] + [right, left]
    for device in near:
        pl.semaphore_signal(barrier, inc=1, device_id=device, device_id_type=MESH)

    for copy in inputs:
        copy.wait()
    for k in range(8):
        for a in range(3):
            opt_out[k % 4, k // 4, a] = state_in[a, 0, :, 128 * k : 128 * k + 128]

    def token(i, distance):
        for to in ((z + distance) % NZ, (z + NZ - distance) % NZ):
            pl.semaphore_signal(
                token_sem.at[i], inc=1, device_id=dev(to, x, c, y), device_id_type=MESH
            )

    pl.semaphore_wait(barrier, len(near))
    token(0, 1)

    for o in range(1, 4):
        xt = (x + o) % 4
        remote(opt_out.at[xt], opt_in.at[w], send_sem.at[0], opt_sem.at[0], dev(z, xt, 1, y))

    @pl.when(c == 0)
    def _():
        remote(opt_out.at[x], opt_in.at[w], send_sem.at[0], opt_sem.at[0], partner)

    @pl.when(c == 1)
    def _():
        opt_in[w] = opt_out[x]

    flows = []
    for f in range(4):
        along_x = f % 2 == 0
        s0, s1 = (flip1, flip3) if f < 2 else (flip3, flip1)
        c1, c2 = (x, y) if along_x else (y, x)
        peer_x = lambda v: dev(z, v, c, y)
        peer_y = lambda v: dev(z, x, c, v)
        peer1, peer2 = (peer_x, peer_y) if along_x else (peer_y, peer_x)
        flows.append((along_x, s0(c1), s1(c1), c1, c2, peer1, peer2))

    def column(core, k):
        return pl.ds(pl.multiple_of(512 * core + 128 * k, 128), 128)

    step1 = {}

    def send_step1(f):
        along_x, p, qq, c1, c2, peer1, peer2 = flows[f]
        h = f // 2
        for k in range(4):
            index = flip2(c1) if k < 2 else p
            core = 1 - c if k % 2 == 0 else c
            if along_x:
                src = grad.at[pl.ds(256 * f, 256), column(core, index)]
                dst = in1x.at[h, k]
            else:
                src = gy.at[h, index, core]
                dst = in1y.at[h, k]
            step1[f, k] = remote(
                src, dst, send_sem.at[1 if along_x else 2], step1_sem.at[f, k], peer1(p)
            )

    send_step1(0)
    send_step1(2)
    for f in (1, 3):
        loads[f].wait()
        for k in range(8):
            tmp[k % 2] = g[256 * f : 256 * f + 256, 128 * k : 128 * k + 128].astype(F32)
            for r in range(4):
                gy[f // 2, r, k // 4, k % 4] = tmp[k % 2, pl.ds(r, 64, stride=4), :].astype(BF16)
        send_step1(f)

    pl.semaphore_wait(token_sem.at[0], 2)
    token(1, 2)

    def pass_state(d, t, side, half=None):
        src = opt_all.at[(z + d + NZ) % NZ, side]
        if half is not None:
            src = src.at[:, pl.ds(16 * half, 16)]
        sem = gather_sem.at[side, GATHERED.index((d - t, half))]
        remote(src, src, send_sem.at[3], sem, dev((z + t + NZ) % NZ, x, c, y))

    def hand_over(d):
        src = opt_all.at[(z + d + NZ) % NZ, 0]
        remote(src, src, send_sem.at[10], opt_sem.at[1], partner)

    def take_state(d, side):
        if d == 8:
            for half in range(2):
                drain(
                    opt_all.at[0, 0, :, pl.ds(0, 16)],
                    gather_sem.at[side, GATHERED.index((16 * half - 8, half))],
                )
        else:
            drain(opt_all.at[0, 0], gather_sem.at[side, GATHERED.index((d, None))])

    def relay(s):
        for side in range(2):
            for d in (-s, s):
                take_state(d, side)
                on = 1 if d < 0 else -1
                pass_state(d, on, side, None if s < 7 else (d + 7) // 14)
                if side == 0:
                    hand_over(d)

    pl.semaphore_wait(token_sem.at[1], 2)
    token(2, 4)

    @pl.when(c == 1)
    def _():
        drain(opt_in.at[pl.ds(0, 7)], opt_sem.at[0])
        for ws in range(8):
            for side in range(2):
                for a in range(3):
                    opt_all[z, side, a, 4 * ws : 4 * ws + 4] = opt_in[ws, side, a]
        for side in range(2):
            for t in (1, -1):
                pass_state(0, t, side)
        hand_over(0)

    loads[0].wait()
    loads[2].wait()

    def pair_sum(f, k, put):
        along_x, p, qq, c1, c2, peer1, peer2 = flows[f]
        h = f // 2
        index = qq if k < 2 else c1
        core = 1 - c if k % 2 == 0 else c
        step1[f, k].wait_recv()
        if along_x:
            own = g[256 * f : 256 * f + 256, column(core, index)]
            tmp[h] = own.astype(F32) + in1x[h, k].astype(F32)
            for r in range(4):
                put(r, tmp[h, pl.ds(r, 64, stride=4), :])
        else:
            for j in range(4):
                put(j, gy[h, index, core, j].astype(F32) + in1y[h, k, j].astype(F32))

    core = {}

    def to_core(f, half):
        def put(j, value):
            core_out[f, half, j] = value

        pair_sum(f, 2 * half, put)
        core[f, half] = remote(
            core_out.at[f, half],
            core_in.at[f, half],
            send_sem.at[4],
            core_sem.at[f, half],
            partner,
        )

    def keep(f, half):
        index = flows[f][2] if half == 0 else flows[f][3]

        def put(j, value):
            part[f, index, j] = value

        pair_sum(f, 2 * half + 1, put)

    step2 = {}
    for f in FLOWS:
        to_core(f, 0)
    for f in FLOWS:
        keep(f, 0)
    for f in FLOWS:
        along_x, p, qq, c1, c2, peer1, peer2 = flows[f]
        core[f, 0].wait_recv()
        part[f, qq] = part[f, qq] + core_in[f, 0]
        step2[f] = remote(
            part.at[f, qq], in2.at[f], send_sem.at[5], step2_sem.at[f], peer1(qq)
        )
    @pl.when(c == 1)
    def _():
        relay(1)

    for f in FLOWS:
        to_core(f, 1)

    row_id = lax.broadcasted_iota(jnp.int32, (256, 256), 0)
    col_id = lax.broadcasted_iota(jnp.int32, (256, 256), 1)
    owner_row = jnp.broadcast_to(owner_ref[...].astype(F32), (256, 256))
    owner_col = jnp.sum(jnp.where(row_id == col_id, owner_row, 0.0), axis=1, keepdims=True)
    same = owner_col == owner_row
    rank_col = jnp.sum(jnp.where(same & (col_id < row_id), 1.0, 0.0), axis=1, keepdims=True)
    rank_row = jnp.sum(jnp.where(same & (row_id < col_id), 1.0, 0.0), axis=0, keepdims=True)
    pos_col = (owner_col * 4.0 + rank_col).astype(jnp.int32)
    pos_row = (owner_ref[...].astype(F32) * 4.0 + rank_row).astype(jnp.int32)
    onehot[...] = (pos_col == lax.broadcasted_iota(jnp.int32, (256, 512), 1)).astype(F32)
    chosen = (pos_row == z * 32 + lax.broadcasted_iota(jnp.int32, (32, 256), 0)).astype(F32)
    mine = (pos_row == d * 4 + lax.broadcasted_iota(jnp.int32, (4, 256), 0)).astype(F32)
    small[9] = jnp.broadcast_to(jnp.sum(mine, axis=1, keepdims=True), (4, 128))

    for f in FLOWS:
        keep(f, 1)
    for f in FLOWS:
        along_x, p, qq, c1, c2, peer1, peer2 = flows[f]
        core[f, 1].wait_recv()
        step2[f].wait_recv()
        part[f, c1] = part[f, c1] + core_in[f, 1] + in2[f]
        for o in (2, 1, 3):
            to = (c2 + o) % 4
            remote(
                part.at[f, c1, to], in3.at[f, o - 1], send_sem.at[6], dim2_sem.at[f], peer2(to)
            )
        if f == 0:

            @pl.when(c == 1)
            def _():
                relay(2)

    for f in FLOWS:
        along_x, p, qq, c1, c2, peer1, peer2 = flows[f]
        drain(in3.at[f], dim2_sem.at[f])
        total = part[f, c1, c2] + in3[f, 0] + in3[f, 1] + in3[f, 2]
        for k in range(4):
            zsend[4 * f + k] = total[16 * k : 16 * k + 16]
        if f == 0:

            @pl.when(c == 1)
            def _():
                relay(3)

    pl.semaphore_wait(token_sem.at[2], 2)

    order = [8, 7, 9, 6, 10, 5, 11, 4, 12, 3, 13, 2, 14, 1, 15]
    for o in order:
        to = (z + o) % NZ
        remote(zsend.at[to], zin.at[o], send_sem.at[7], z_sem.at[0], dev(to, x, c, y))
    zin[0] = zsend[z]

    @pl.when(c == 1)
    def _():
        relay(4)
        relay(5)

    first_fix, second_fix = corrections(step_ref)
    drain(zin.at[pl.ds(1, 15)], z_sem.at[0])
    sums[z] = jnp.sum(zin[...], axis=0)
    for o in order:
        to = (z + o) % NZ
        remote(sums.at[z], sums.at[z], send_sem.at[8], z_sem.at[1], dev(to, x, c, y))

    @pl.when(c == 1)
    def _():
        relay(6)
        relay(7)

    drain(sums.at[pl.ds(0, 15)], z_sem.at[1])

    summed = sums[...].reshape(256, 128)
    squares[q] = jnp.sum(summed * summed, axis=0, keepdims=True)
    for o in range(1, 32):
        t = (q + o) % 32
        remote(
            squares.at[q],
            squares.at[q],
            send_sem.at[9],
            norm_sem.at[0],
            dev(z, (t // 2) % 4, t % 2, t // 8),
        )
    picked = jnp.dot(chosen, summed, precision=HIGH, preferred_element_type=F32)
    for k in range(8):
        sel_out[k] = picked[4 * k : 4 * k + 4]
    for o in range(1, 8):
        remote(
            sel_out.at[(w + o) % 8], small.at[slab], send_sem.at[11], norm_sem.at[1], xc_peer(o)
        )
    small[slab] = sel_out[w]

    @pl.when(c == 1)
    def _():
        take_state(8, 0)
        hand_over(8)
        take_state(8, 1)


    @pl.when(c == 0)
    def _():
        drain(opt_all.at[pl.ds(0, 8)], opt_sem.at[1])

    states = []
    for a in range(3):
        table = opt_all[:, c, a].reshape(512, 128)
        states.append(jnp.dot(onehot[...], table, precision=HIGH, preferred_element_type=F32))
    drain(squares.at[pl.ds(0, 31)], norm_sem.at[0])
    squares_total = jnp.sum(jnp.sum(squares[...], axis=0), keepdims=True)
    limit = jnp.float32(1024.0)
    scale = limit / jnp.maximum(jnp.sqrt(squares_total), limit)
    rounded = adam(summed, *states, scale, first_fix, second_fix)[0].astype(BF16)

    def forward(f, j):
        along_x, p, qq, c1, c2, peer1, peer2 = flows[f]
        piece = w_part.at[f, c1, j]
        remote(piece, piece, send_sem.at[13], ag1_sem.at[f, 0], peer1(qq))
        remote(piece, piece, send_sem.at[13], ag1_sem.at[f, 1], peer1(p))

    ag2 = {}
    for f in FLOWS:
        along_x, p, qq, c1, c2, peer1, peer2 = flows[f]
        w_part[f, c1, c2] = rounded[64 * f : 64 * f + 64]
        own = w_part.at[f, c1, c2]
        for o in (2, 1, 3):
            ag2[f, o] = remote(
                own, own, send_sem.at[12], ag2_sem.at[f, o - 1], peer2((c2 + o) % 4)
            )
    for f in FLOWS:
        forward(f, flows[f][4])
    small[8] = jnp.broadcast_to(scale, (4, 128))

    def give(f, index):
        piece = w_part.at[f, index]
        remote(piece, w_all.at[c, f, index], send_sem.at[14], out_sem.at[0], partner)
        pltpu.make_async_copy(piece, w_all.at[c, f, index], out_sem.at[1]).start()

    for o in (1, 3, 2):
        for f in FLOWS:
            ag2[f, o].wait_recv()
            forward(f, (flows[f][4] + 4 - o) % 4)
    for f in FLOWS:
        give(f, flows[f][3])
    drain(small.at[pl.ds(0, 7)], norm_sem.at[1])
    small_copy = pltpu.make_async_copy(small, small_hbm, out_sem.at[2])
    small_copy.start()
    for f in FLOWS:
        along_x, p, qq, c1, c2, peer1, peer2 = flows[f]
        got = w_part.at[f, qq]
        drain(got, ag1_sem.at[f, 0])
        remote(got, got, send_sem.at[13], ag1_sem.at[f, 2], peer1(p))
        give(f, qq)
    for f in FLOWS:
        got = w_part.at[f, flows[f][1]]
        drain(got, ag1_sem.at[f, 1])
        give(f, flows[f][1])
    for f in FLOWS:
        got = w_part.at[f, flip2(flows[f][3])]
        drain(got, ag1_sem.at[f, 2])
        give(f, flip2(flows[f][3]))

    small_copy.wait()

    @pl.when(c == 0)
    def _():
        drain(opt_out, send_sem.at[0])

    @pl.when(c == 1)
    def _():
        drain(opt_out.at[pl.ds(0, 3)], send_sem.at[0])
        drain(opt_all.at[pl.ds(0, 15)], send_sem.at[3])
        drain(opt_all.at[pl.ds(0, 8)], send_sem.at[10])

    drain(in1x, send_sem.at[1])
    drain(in1y, send_sem.at[2])
    drain(core_out, send_sem.at[4])
    drain(in2, send_sem.at[5])
    drain(in3, send_sem.at[6])
    drain(zin.at[pl.ds(1, 15)], send_sem.at[7])
    drain(sums.at[pl.ds(0, 15)], send_sem.at[8])
    drain(squares.at[pl.ds(0, 31)], send_sem.at[9])
    drain(sel_out.at[pl.ds(0, 7)], send_sem.at[11])
    drain(w_part.at[0, pl.ds(0, 3)], send_sem.at[12])
    drain(w_part.at[pl.ds(0, 3)], send_sem.at[13])
    drain(w_part, send_sem.at[14])
    drain(w_part, out_sem.at[1])
    drain(w_all.at[1 - c], out_sem.at[0])


def result_kernel(
    w_all,
    small_hbm,
    step_ref,
    master_hbm,
    first_hbm,
    second_hbm,
    w_out,
    nm_out,
    nf_out,
    ns_out,
    small,
    state_in,
    state_out,
    w_in,
    rows,
    tmp,
    load_sem,
    in_sem,
    out_sem,
):
    loads = {}
    for f in range(4):
        for core in range(2):
            loads[f, core] = pltpu.make_async_copy(
                w_all.at[core, f], w_in.at[core, f], in_sem.at[f, core]
            )
            loads[f, core].start()
    inputs = []
    for i, (src, dst) in enumerate(
        (
            (small_hbm, small),
            (master_hbm, state_in.at[0]),
            (first_hbm, state_in.at[1]),
            (second_hbm, state_in.at[2]),
        )
    ):
        inputs.append(pltpu.make_async_copy(src, dst, load_sem.at[i]))
        inputs[i].start()
    fixes = corrections(step_ref)
    stores = []

    def store(src, dst):
        stores.append(pltpu.make_async_copy(src, dst, out_sem.at[len(stores)]))
        stores[-1].start()

    for f in range(4):
        if f == 2:
            for copy in inputs:
                copy.wait()
            scale = small[8, :1, :1]
            filled = small[9] > 0.5
            for k in range(8):
                cols = slice(128 * k, 128 * k + 128)
                olds = [state_in[a, 0, :, cols] for a in range(3)]
                for a, value in enumerate(adam(small[k], *olds, scale, *fixes)):
                    state_out[a, 0, :, cols] = jnp.where(filled, value, 0.0)
            for a, out in enumerate((nm_out, nf_out, ns_out)):
                store(state_out.at[a], out)
        for core in range(2):
            loads[f, core].wait()
            for k in range(4):
                for r in range(4):
                    i, j = (k, r) if f % 2 == 0 else (r, k)
                    tmp[k, pl.ds(r, 64, stride=4), :] = w_in[core, f, i, j].astype(F32)
                at = 512 * core + 128 * k
                rows[f, :, at : at + 128] = tmp[k].astype(BF16)
            half = pl.ds(512 * core, 512)
            store(rows.at[f, :, half], w_out.at[pl.ds(256 * f, 256), half])
    for copy in stores:
        copy.wait()


def local_step(gradient, owner_list, step_count, master, first_moment, second_moment):
    smem = pl.BlockSpec(memory_space=pltpu.SMEM)
    anywhere = pl.BlockSpec(memory_space=pl.ANY)
    dma = pltpu.SemaphoreType.DMA
    w_all, small = pl.pallas_call(
        reduce_kernel,
        out_shape=(
            jax.ShapeDtypeStruct((2, 4, 4, 4, 64, 128), BF16),
            jax.ShapeDtypeStruct((10, 4, 128), F32),
        ),
        in_specs=[anywhere, anywhere, smem, anywhere, anywhere, anywhere],
        out_specs=(anywhere, anywhere),
        scratch_shapes=[
            pltpu.VMEM((1, owner_list.shape[0]), jnp.int32),
            pltpu.VMEM((3, *master.shape), F32),
            pltpu.VMEM((10, 4, 128), F32),
            pltpu.VMEM((1024, 1024), BF16),
            pltpu.VMEM((2, 4, 2, 4, 64, 128), BF16),
            pltpu.VMEM((2, 256, 128), F32),
            pltpu.VMEM((2, 4, 256, 128), BF16),
            pltpu.VMEM((2, 4, 4, 64, 128), BF16),
            pltpu.VMEM((4, 2, 4, 64, 128), F32),
            pltpu.VMEM((4, 2, 4, 64, 128), F32),
            pltpu.VMEM((4, 4, 4, 64, 128), F32),
            pltpu.VMEM((4, 4, 64, 128), F32),
            pltpu.VMEM((4, 3, 64, 128), F32),
            pltpu.VMEM((NZ, 16, 128), F32),
            pltpu.VMEM((NZ, 16, 128), F32),
            pltpu.VMEM((NZ, 16, 128), F32),
            pltpu.VMEM((32, 1, 128), F32),
            pltpu.VMEM((8, 4, 128), F32),
            pltpu.VMEM((4, 2, 3, 4, 128), F32),
            pltpu.VMEM((8, 2, 3, 4, 128), F32),
            pltpu.VMEM((NZ, 2, 3, 32, 128), F32),
            pltpu.VMEM((256, 512), F32),
            pltpu.VMEM((4, 4, 4, 64, 128), BF16),
            dma((8,)),
            dma((4, 4)),
            dma((4, 2)),
            dma((4,)),
            dma((4,)),
            dma((2,)),
            dma((2, 16)),
            dma((2,)),
            dma((2,)),
            dma((4, 3)),
            dma((4, 3)),
            dma((3,)),
            dma((15,)),
            pltpu.SemaphoreType.REGULAR((3,)),
        ],
        compiler_params=pltpu.CompilerParams(collective_id=0, has_side_effects=True),
        name="adam_reduce",
    )(
        gradient.reshape(gradient.shape[2:]),
        owner_list.reshape(1, owner_list.shape[0]),
        step_count,
        master,
        first_moment,
        second_moment,
    )
    state = jax.ShapeDtypeStruct(master.shape, F32)
    return pl.pallas_call(
        result_kernel,
        out_shape=(jax.ShapeDtypeStruct((1024, 1024), BF16), state, state, state),
        in_specs=[anywhere, anywhere, smem, anywhere, anywhere, anywhere],
        out_specs=(anywhere, anywhere, anywhere, anywhere),
        scratch_shapes=[
            pltpu.VMEM((10, 4, 128), F32),
            pltpu.VMEM((3, *master.shape), F32),
            pltpu.VMEM((3, *master.shape), F32),
            pltpu.VMEM((2, 4, 4, 4, 64, 128), BF16),
            pltpu.VMEM((4, 256, 1024), BF16),
            pltpu.VMEM((4, 256, 128), F32),
            dma((4,)),
            dma((4, 2)),
            dma((11,)),
        ],
        name="adam_results",
    )(w_all, small, step_count, master, first_moment, second_moment)


def solution(mesh):
    owned = P("dp", None, "rep")
    return jax.shard_map(
        local_step,
        mesh=mesh,
        in_specs=(P("dp", "rep", None, None), P(), P(), owned, owned, owned),
        out_specs=(P(), owned, owned, owned),
        check_vma=False,
    )
```

```python
import jax
import jax.numpy as jnp
from jax import lax
from jax.experimental import pallas as pl
from jax.experimental.pallas import tpu as pltpu
from jax.sharding import PartitionSpec as P

MESH = pl.DeviceIdType.MESH
F32 = jnp.float32
BF16 = jnp.bfloat16
HIGH = lax.Precision.HIGHEST
NZ = 16
FLOWS = (0, 2, 1, 3)
GATHERED = [(d, None) for d in range(-7, 8) if d] + [(-8, 0), (8, 1)]


def flip1(v):
    return v + 1 - 2 * (v % 2)


def flip2(v):
    return (v + 2) % 4


def flip3(v):
    return 3 - v


def integer_power(base, count):
    result = jnp.ones((1, 1), F32)
    factor = jnp.float32(base)
    for bit in range(5):
        result = jnp.where((count // (2**bit)) % 2 == 1, result * factor, result)
        factor = factor * factor
    return result


def corrections(step_ref):
    count = jnp.full((1, 1), step_ref[0], jnp.int32)
    return 1.0 - integer_power(0.9, count), 1.0 - integer_power(0.95, count)


def adam(total, master, first, second, scale, first_fix, second_fix):
    clipped = scale * total
    new_first = 0.9 * first + 0.1 * clipped
    new_second = 0.95 * second + 0.05 * clipped * clipped
    update = new_first / first_fix / (jnp.sqrt(new_second / second_fix) + 1e-08)
    new_master = master * (1.0 - 0.1 * 0.1) - 0.1 * update
    return new_master, new_first, new_second


def reduce_kernel(
    grad,
    owner_hbm,
    step_ref,
    master_hbm,
    first_hbm,
    second_hbm,
    w_all,
    small_hbm,
    owner_ref,
    state_in,
    small,
    g,
    gy,
    tmp,
    in1x,
    in1y,
    core_out,
    core_in,
    part,
    in2,
    in3,
    zsend,
    zin,
    sums,
    squares,
    sel_out,
    opt_out,
    opt_in,
    opt_all,
    onehot,
    w_part,
    load_sem,
    step1_sem,
    core_sem,
    step2_sem,
    dim2_sem,
    opt_sem,
    gather_sem,
    z_sem,
    norm_sem,
    ag2_sem,
    ag1_sem,
    out_sem,
    send_sem,
    token_sem,
):
    d = lax.axis_index("dp")
    y = lax.axis_index("rep")
    z = d // 8
    w = d % 8
    x = w // 2
    c = d % 2
    slab = c * 4 + x
    q = y * 8 + w

    def dev(zz, xx, cc, yy):
        return (zz * 8 + xx * 2 + cc, yy)

    def remote(src, dst, send, recv, device):
        copy = pltpu.make_async_remote_copy(
            src_ref=src,
            dst_ref=dst,
            send_sem=send,
            recv_sem=recv,
            device_id=device,
            device_id_type=MESH,
        )
        copy.start()
        return copy

    def drain(ref, sem):
        pltpu.make_async_copy(ref, ref, sem).wait()

    partner = dev(z, x, 1 - c, y)

    inputs = []
    for i, (src, dst) in enumerate(
        (
            (master_hbm, state_in.at[0]),
            (first_hbm, state_in.at[1]),
            (second_hbm, state_in.at[2]),
            (owner_hbm, owner_ref),
        )
    ):
        inputs.append(pltpu.make_async_copy(src, dst, load_sem.at[4 + i]))
        inputs[i].start()
    loads = {}
    for f in (1, 3, 0, 2):
        loads[f] = pltpu.make_async_copy(
            grad.at[pl.ds(256 * f, 256)], g.at[pl.ds(256 * f, 256)], load_sem.at[f]
        )
        loads[f].start()

    def xc_peer(o):
        t = (w + o) % 8
        return dev(z, t // 2, t % 2, y)

    right = dev((z + 1) % NZ, x, c, y)
    left = dev((z + NZ - 1) % NZ, x, c, y)

    barrier = pltpu.get_barrier_semaphore()
    near = [xc_peer(o) for o in range(1, 8)]
    near += [dev(z, x, c, (y + o) % 4) for o in range(1, 4)] + [right, left]
    for device in near:
        pl.semaphore_signal(barrier, inc=1, device_id=device, device_id_type=MESH)

    for copy in inputs:
        copy.wait()
    for k in range(8):
        for a in range(3):
            opt_out[k % 4, k // 4, a] = state_in[a, 0, :, 128 * k : 128 * k + 128]

    def token(i, distance):
        for to in ((z + distance) % NZ, (z + NZ - distance) % NZ):
            pl.semaphore_signal(
                token_sem.at[i], inc=1, device_id=dev(to, x, c, y), device_id_type=MESH
            )

    pl.semaphore_wait(barrier, len(near))
    token(0, 1)

    for o in range(1, 4):
        xt = (x + o) % 4
        remote(opt_out.at[xt], opt_in.at[w], send_sem.at[0], opt_sem.at[0], dev(z, xt, 1, y))

    @pl.when(c == 0)
    def _():
        remote(opt_out.at[x], opt_in.at[w], send_sem.at[0], opt_sem.at[0], partner)

    @pl.when(c == 1)
    def _():
        opt_in[w] = opt_out[x]

    flows = []
    for f in range(4):
        along_x = f % 2 == 0
        s0, s1 = (flip1, flip3) if f < 2 else (flip3, flip1)
        c1, c2 = (x, y) if along_x else (y, x)
        peer_x = lambda v: dev(z, v, c, y)
        peer_y = lambda v: dev(z, x, c, v)
        peer1, peer2 = (peer_x, peer_y) if along_x else (peer_y, peer_x)
        flows.append((along_x, s0(c1), s1(c1), c1, c2, peer1, peer2))

    def column(core, k):
        return pl.ds(pl.multiple_of(512 * core + 128 * k, 128), 128)

    step1 = {}

    def send_step1(f):
        along_x, p, qq, c1, c2, peer1, peer2 = flows[f]
        h = f // 2
        for k in range(4):
            index = flip2(c1) if k < 2 else p
            core = 1 - c if k % 2 == 0 else c
            if along_x:
                src = grad.at[pl.ds(256 * f, 256), column(core, index)]
                dst = in1x.at[h, k]
            else:
                src = gy.at[h, index, core]
                dst = in1y.at[h, k]
            step1[f, k] = remote(
                src, dst, send_sem.at[1 if along_x else 2], step1_sem.at[f, k], peer1(p)
            )

    send_step1(0)
    send_step1(2)
    for f in (1, 3):
        loads[f].wait()
        for k in range(8):
            tmp[k % 2] = g[256 * f : 256 * f + 256, 128 * k : 128 * k + 128].astype(F32)
            for r in range(4):
                gy[f // 2, r, k // 4, k % 4] = tmp[k % 2, pl.ds(r, 64, stride=4), :].astype(BF16)
        send_step1(f)

    pl.semaphore_wait(token_sem.at[0], 2)
    token(1, 2)

    def pass_state(d, t, side, half=None):
        src = opt_all.at[(z + d + NZ) % NZ, side]
        if half is not None:
            src = src.at[:, pl.ds(16 * half, 16)]
        sem = gather_sem.at[side, GATHERED.index((d - t, half))]
        remote(src, src, send_sem.at[3], sem, dev((z + t + NZ) % NZ, x, c, y))

    def hand_over(d):
        src = opt_all.at[(z + d + NZ) % NZ, 0]
        remote(src, src, send_sem.at[10], opt_sem.at[1], partner)

    def take_state(d, side):
        if d == 8:
            for half in range(2):
                drain(
                    opt_all.at[0, 0, :, pl.ds(0, 16)],
                    gather_sem.at[side, GATHERED.index((16 * half - 8, half))],
                )
        else:
            drain(opt_all.at[0, 0], gather_sem.at[side, GATHERED.index((d, None))])

    def relay(s):
        for side in range(2):
            for d in (-s, s):
                take_state(d, side)
                on = 1 if d < 0 else -1
                pass_state(d, on, side, None if s < 7 else (d + 7) // 14)
                if side == 0:
                    hand_over(d)

    pl.semaphore_wait(token_sem.at[1], 2)
    token(2, 4)

    @pl.when(c == 1)
    def _():
        drain(opt_in.at[pl.ds(0, 7)], opt_sem.at[0])
        for ws in range(8):
            for side in range(2):
                for a in range(3):
                    opt_all[z, side, a, 4 * ws : 4 * ws + 4] = opt_in[ws, side, a]
        for side in range(2):
            for t in (1, -1):
                pass_state(0, t, side)
        hand_over(0)

    loads[0].wait()
    loads[2].wait()

    def pair_sum(f, k, put):
        along_x, p, qq, c1, c2, peer1, peer2 = flows[f]
        h = f // 2
        index = qq if k < 2 else c1
        core = 1 - c if k % 2 == 0 else c
        step1[f, k].wait_recv()
        if along_x:
            own = g[256 * f : 256 * f + 256, column(core, index)]
            tmp[h] = own.astype(F32) + in1x[h, k].astype(F32)
            for r in range(4):
                put(r, tmp[h, pl.ds(r, 64, stride=4), :])
        else:
            for j in range(4):
                put(j, gy[h, index, core, j].astype(F32) + in1y[h, k, j].astype(F32))

    core = {}

    def to_core(f, half):
        def put(j, value):
            core_out[f, half, j] = value

        pair_sum(f, 2 * half, put)
        core[f, half] = remote(
            core_out.at[f, half],
            core_in.at[f, half],
            send_sem.at[4],
            core_sem.at[f, half],
            partner,
        )

    def keep(f, half):
        index = flows[f][2] if half == 0 else flows[f][3]

        def put(j, value):
            part[f, index, j] = value

        pair_sum(f, 2 * half + 1, put)

    step2 = {}
    for f in FLOWS:
        to_core(f, 0)
    for f in FLOWS:
        keep(f, 0)
    for f in FLOWS:
        along_x, p, qq, c1, c2, peer1, peer2 = flows[f]
        core[f, 0].wait_recv()
        part[f, qq] = part[f, qq] + core_in[f, 0]
        step2[f] = remote(
            part.at[f, qq], in2.at[f], send_sem.at[5], step2_sem.at[f], peer1(qq)
        )
    @pl.when(c == 1)
    def _():
        relay(1)

    for f in FLOWS:
        to_core(f, 1)

    row_id = lax.broadcasted_iota(jnp.int32, (256, 256), 0)
    col_id = lax.broadcasted_iota(jnp.int32, (256, 256), 1)
    owner_row = jnp.broadcast_to(owner_ref[...].astype(F32), (256, 256))
    owner_col = jnp.sum(jnp.where(row_id == col_id, owner_row, 0.0), axis=1, keepdims=True)
    same = owner_col == owner_row
    rank_col = jnp.sum(jnp.where(same & (col_id < row_id), 1.0, 0.0), axis=1, keepdims=True)
    rank_row = jnp.sum(jnp.where(same & (row_id < col_id), 1.0, 0.0), axis=0, keepdims=True)
    pos_col = (owner_col * 4.0 + rank_col).astype(jnp.int32)
    pos_row = (owner_ref[...].astype(F32) * 4.0 + rank_row).astype(jnp.int32)
    onehot[...] = (pos_col == lax.broadcasted_iota(jnp.int32, (256, 512), 1)).astype(F32)
    chosen = (pos_row == z * 32 + lax.broadcasted_iota(jnp.int32, (32, 256), 0)).astype(F32)
    mine = (pos_row == d * 4 + lax.broadcasted_iota(jnp.int32, (4, 256), 0)).astype(F32)
    small[9] = jnp.broadcast_to(jnp.sum(mine, axis=1, keepdims=True), (4, 128))

    for f in FLOWS:
        keep(f, 1)
    for f in FLOWS:
        along_x, p, qq, c1, c2, peer1, peer2 = flows[f]
        core[f, 1].wait_recv()
        step2[f].wait_recv()
        part[f, c1] = part[f, c1] + core_in[f, 1] + in2[f]
        for o in (2, 1, 3):
            to = (c2 + o) % 4
            remote(
                part.at[f, c1, to], in3.at[f, o - 1], send_sem.at[6], dim2_sem.at[f], peer2(to)
            )
        if f == 0:

            @pl.when(c == 1)
            def _():
                relay(2)

    for f in FLOWS:
        along_x, p, qq, c1, c2, peer1, peer2 = flows[f]
        drain(in3.at[f], dim2_sem.at[f])
        total = part[f, c1, c2] + in3[f, 0] + in3[f, 1] + in3[f, 2]
        for k in range(4):
            zsend[4 * f + k] = total[16 * k : 16 * k + 16]
        if f == 0:

            @pl.when(c == 1)
            def _():
                relay(3)

    pl.semaphore_wait(token_sem.at[2], 2)

    order = [8, 7, 9, 6, 10, 5, 11, 4, 12, 3, 13, 2, 14, 1, 15]
    for o in order:
        to = (z + o) % NZ
        remote(zsend.at[to], zin.at[o], send_sem.at[7], z_sem.at[0], dev(to, x, c, y))
    zin[0] = zsend[z]

    @pl.when(c == 1)
    def _():
        relay(4)
        relay(5)

    first_fix, second_fix = corrections(step_ref)
    drain(zin.at[pl.ds(1, 15)], z_sem.at[0])
    sums[z] = jnp.sum(zin[...], axis=0)
    for o in order:
        to = (z + o) % NZ
        remote(sums.at[z], sums.at[z], send_sem.at[8], z_sem.at[1], dev(to, x, c, y))

    @pl.when(c == 1)
    def _():
        relay(6)
        relay(7)

    drain(sums.at[pl.ds(0, 15)], z_sem.at[1])

    summed = sums[...].reshape(256, 128)
    squares[q] = jnp.sum(summed * summed, axis=0, keepdims=True)
    for o in range(1, 32):
        t = (q + o) % 32
        remote(
            squares.at[q],
            squares.at[q],
            send_sem.at[9],
            norm_sem.at[0],
            dev(z, (t // 2) % 4, t % 2, t // 8),
        )
    picked = jnp.dot(chosen, summed, precision=HIGH, preferred_element_type=F32)
    for k in range(8):
        sel_out[k] = picked[4 * k : 4 * k + 4]
    for o in range(1, 8):
        remote(
            sel_out.at[(w + o) % 8], small.at[slab], send_sem.at[11], norm_sem.at[1], xc_peer(o)
        )
    small[slab] = sel_out[w]

    @pl.when(c == 1)
    def _():
        take_state(8, 0)
        hand_over(8)
        take_state(8, 1)


    @pl.when(c == 0)
    def _():
        drain(opt_all.at[pl.ds(0, 8)], opt_sem.at[1])

    states = []
    for a in range(3):
        table = opt_all[:, c, a].reshape(512, 128)
        states.append(jnp.dot(onehot[...], table, precision=HIGH, preferred_element_type=F32))
    drain(squares.at[pl.ds(0, 31)], norm_sem.at[0])
    squares_total = jnp.sum(jnp.sum(squares[...], axis=0), keepdims=True)
    limit = jnp.float32(1024.0)
    scale = limit / jnp.maximum(jnp.sqrt(squares_total), limit)
    rounded = adam(summed, *states, scale, first_fix, second_fix)[0].astype(BF16)

    def forward(f, j):
        along_x, p, qq, c1, c2, peer1, peer2 = flows[f]
        piece = w_part.at[f, c1, j]
        remote(piece, piece, send_sem.at[13], ag1_sem.at[f, 2], peer1(flip2(c1)))
        remote(piece, piece, send_sem.at[13], ag1_sem.at[f, 0], peer1(qq))
        remote(piece, piece, send_sem.at[13], ag1_sem.at[f, 1], peer1(p))

    ag2 = {}
    for f in FLOWS:
        along_x, p, qq, c1, c2, peer1, peer2 = flows[f]
        w_part[f, c1, c2] = rounded[64 * f : 64 * f + 64]
        own = w_part.at[f, c1, c2]
        for o in (2, 1, 3):
            ag2[f, o] = remote(
                own, own, send_sem.at[12], ag2_sem.at[f, o - 1], peer2((c2 + o) % 4)
            )
    for f in FLOWS:
        forward(f, flows[f][4])
    small[8] = jnp.broadcast_to(scale, (4, 128))

    def give(f, index):
        piece = w_part.at[f, index]
        remote(piece, w_all.at[c, f, index], send_sem.at[14], out_sem.at[0], partner)
        pltpu.make_async_copy(piece, w_all.at[c, f, index], out_sem.at[1]).start()

    for o in (1, 3, 2):
        for f in FLOWS:
            ag2[f, o].wait_recv()
            forward(f, (flows[f][4] + 4 - o) % 4)
    for f in FLOWS:
        give(f, flows[f][3])
    drain(small.at[pl.ds(0, 7)], norm_sem.at[1])
    small_copy = pltpu.make_async_copy(small, small_hbm, out_sem.at[2])
    small_copy.start()
    for f in FLOWS:
        along_x, p, qq, c1, c2, peer1, peer2 = flows[f]
        got = w_part.at[f, qq]
        drain(got, ag1_sem.at[f, 0])
        give(f, qq)
    for f in FLOWS:
        got = w_part.at[f, flows[f][1]]
        drain(got, ag1_sem.at[f, 1])
        give(f, flows[f][1])
    for f in FLOWS:
        got = w_part.at[f, flip2(flows[f][3])]
        drain(got, ag1_sem.at[f, 2])
        give(f, flip2(flows[f][3]))

    small_copy.wait()

    @pl.when(c == 0)
    def _():
        drain(opt_out, send_sem.at[0])

    @pl.when(c == 1)
    def _():
        drain(opt_out.at[pl.ds(0, 3)], send_sem.at[0])
        drain(opt_all.at[pl.ds(0, 15)], send_sem.at[3])
        drain(opt_all.at[pl.ds(0, 8)], send_sem.at[10])

    drain(in1x, send_sem.at[1])
    drain(in1y, send_sem.at[2])
    drain(core_out, send_sem.at[4])
    drain(in2, send_sem.at[5])
    drain(in3, send_sem.at[6])
    drain(zin.at[pl.ds(1, 15)], send_sem.at[7])
    drain(sums.at[pl.ds(0, 15)], send_sem.at[8])
    drain(squares.at[pl.ds(0, 31)], send_sem.at[9])
    drain(sel_out.at[pl.ds(0, 7)], send_sem.at[11])
    drain(w_part.at[0, pl.ds(0, 3)], send_sem.at[12])
    drain(w_part.at[pl.ds(0, 3)], send_sem.at[13])
    drain(w_part, send_sem.at[14])
    drain(w_part, out_sem.at[1])
    drain(w_all.at[1 - c], out_sem.at[0])


def result_kernel(
    w_all,
    small_hbm,
    step_ref,
    master_hbm,
    first_hbm,
    second_hbm,
    w_out,
    nm_out,
    nf_out,
    ns_out,
    small,
    state_in,
    state_out,
    w_in,
    rows,
    tmp,
    load_sem,
    in_sem,
    out_sem,
):
    loads = {}
    for f in range(4):
        for core in range(2):
            loads[f, core] = pltpu.make_async_copy(
                w_all.at[core, f], w_in.at[core, f], in_sem.at[f, core]
            )
            loads[f, core].start()
    inputs = []
    for i, (src, dst) in enumerate(
        (
            (small_hbm, small),
            (master_hbm, state_in.at[0]),
            (first_hbm, state_in.at[1]),
            (second_hbm, state_in.at[2]),
        )
    ):
        inputs.append(pltpu.make_async_copy(src, dst, load_sem.at[i]))
        inputs[i].start()
    fixes = corrections(step_ref)
    stores = []

    def store(src, dst):
        stores.append(pltpu.make_async_copy(src, dst, out_sem.at[len(stores)]))
        stores[-1].start()

    for f in range(4):
        if f == 2:
            for copy in inputs:
                copy.wait()
            scale = small[8, :1, :1]
            filled = small[9] > 0.5
            for k in range(8):
                cols = slice(128 * k, 128 * k + 128)
                olds = [state_in[a, 0, :, cols] for a in range(3)]
                for a, value in enumerate(adam(small[k], *olds, scale, *fixes)):
                    state_out[a, 0, :, cols] = jnp.where(filled, value, 0.0)
            for a, out in enumerate((nm_out, nf_out, ns_out)):
                store(state_out.at[a], out)
        for core in range(2):
            loads[f, core].wait()
            for k in range(4):
                for r in range(4):
                    i, j = (k, r) if f % 2 == 0 else (r, k)
                    tmp[k, pl.ds(r, 64, stride=4), :] = w_in[core, f, i, j].astype(F32)
                at = 512 * core + 128 * k
                rows[f, :, at : at + 128] = tmp[k].astype(BF16)
            half = pl.ds(512 * core, 512)
            store(rows.at[f, :, half], w_out.at[pl.ds(256 * f, 256), half])
    for copy in stores:
        copy.wait()


def local_step(gradient, owner_list, step_count, master, first_moment, second_moment):
    smem = pl.BlockSpec(memory_space=pltpu.SMEM)
    anywhere = pl.BlockSpec(memory_space=pl.ANY)
    dma = pltpu.SemaphoreType.DMA
    w_all, small = pl.pallas_call(
        reduce_kernel,
        out_shape=(
            jax.ShapeDtypeStruct((2, 4, 4, 4, 64, 128), BF16),
            jax.ShapeDtypeStruct((10, 4, 128), F32),
        ),
        in_specs=[anywhere, anywhere, smem, anywhere, anywhere, anywhere],
        out_specs=(anywhere, anywhere),
        scratch_shapes=[
            pltpu.VMEM((1, owner_list.shape[0]), jnp.int32),
            pltpu.VMEM((3, *master.shape), F32),
            pltpu.VMEM((10, 4, 128), F32),
            pltpu.VMEM((1024, 1024), BF16),
            pltpu.VMEM((2, 4, 2, 4, 64, 128), BF16),
            pltpu.VMEM((2, 256, 128), F32),
            pltpu.VMEM((2, 4, 256, 128), BF16),
            pltpu.VMEM((2, 4, 4, 64, 128), BF16),
            pltpu.VMEM((4, 2, 4, 64, 128), F32),
            pltpu.VMEM((4, 2, 4, 64, 128), F32),
            pltpu.VMEM((4, 4, 4, 64, 128), F32),
            pltpu.VMEM((4, 4, 64, 128), F32),
            pltpu.VMEM((4, 3, 64, 128), F32),
            pltpu.VMEM((NZ, 16, 128), F32),
            pltpu.VMEM((NZ, 16, 128), F32),
            pltpu.VMEM((NZ, 16, 128), F32),
            pltpu.VMEM((32, 1, 128), F32),
            pltpu.VMEM((8, 4, 128), F32),
            pltpu.VMEM((4, 2, 3, 4, 128), F32),
            pltpu.VMEM((8, 2, 3, 4, 128), F32),
            pltpu.VMEM((NZ, 2, 3, 32, 128), F32),
            pltpu.VMEM((256, 512), F32),
            pltpu.VMEM((4, 4, 4, 64, 128), BF16),
            dma((8,)),
            dma((4, 4)),
            dma((4, 2)),
            dma((4,)),
            dma((4,)),
            dma((2,)),
            dma((2, 16)),
            dma((2,)),
            dma((2,)),
            dma((4, 3)),
            dma((4, 3)),
            dma((3,)),
            dma((15,)),
            pltpu.SemaphoreType.REGULAR((3,)),
        ],
        compiler_params=pltpu.CompilerParams(collective_id=0, has_side_effects=True),
        name="adam_reduce",
    )(
        gradient.reshape(gradient.shape[2:]),
        owner_list.reshape(1, owner_list.shape[0]),
        step_count,
        master,
        first_moment,
        second_moment,
    )
    state = jax.ShapeDtypeStruct(master.shape, F32)
    return pl.pallas_call(
        result_kernel,
        out_shape=(jax.ShapeDtypeStruct((1024, 1024), BF16), state, state, state),
        in_specs=[anywhere, anywhere, smem, anywhere, anywhere, anywhere],
        out_specs=(anywhere, anywhere, anywhere, anywhere),
        scratch_shapes=[
            pltpu.VMEM((10, 4, 128), F32),
            pltpu.VMEM((3, *master.shape), F32),
            pltpu.VMEM((3, *master.shape), F32),
            pltpu.VMEM((2, 4, 4, 4, 64, 128), BF16),
            pltpu.VMEM((4, 256, 1024), BF16),
            pltpu.VMEM((4, 256, 128), F32),
            dma((4,)),
            dma((4, 2)),
            dma((11,)),
        ],
        name="adam_results",
    )(w_all, small, step_count, master, first_moment, second_moment)


def solution(mesh):
    owned = P("dp", None, "rep")
    return jax.shard_map(
        local_step,
        mesh=mesh,
        in_specs=(P("dp", "rep", None, None), P(), P(), owned, owned, owned),
        out_specs=(P(), owned, owned, owned),
        check_vma=False,
    )
```

```python
import jax
import jax.numpy as jnp
from jax import lax
from jax.experimental import pallas as pl
from jax.experimental.pallas import tpu as pltpu
from jax.sharding import PartitionSpec as P

MESH = pl.DeviceIdType.MESH
F32 = jnp.float32
BF16 = jnp.bfloat16
HIGH = lax.Precision.HIGHEST
NZ = 16
FLOWS = (0, 2, 1, 3)
GATHERED = [(d, None) for d in range(-7, 8) if d] + [(-8, 0), (8, 1)]


def flip1(v):
    return v + 1 - 2 * (v % 2)


def flip2(v):
    return (v + 2) % 4


def flip3(v):
    return 3 - v


def integer_power(base, count):
    result = jnp.ones((1, 1), F32)
    factor = jnp.float32(base)
    for bit in range(5):
        result = jnp.where((count // (2**bit)) % 2 == 1, result * factor, result)
        factor = factor * factor
    return result


def corrections(step_ref):
    count = jnp.full((1, 1), step_ref[0], jnp.int32)
    return 1.0 - integer_power(0.9, count), 1.0 - integer_power(0.95, count)


def adam(total, master, first, second, scale, first_fix, second_fix):
    clipped = scale * total
    new_first = 0.9 * first + 0.1 * clipped
    new_second = 0.95 * second + 0.05 * clipped * clipped
    update = new_first / first_fix / (jnp.sqrt(new_second / second_fix) + 1e-08)
    new_master = master * (1.0 - 0.1 * 0.1) - 0.1 * update
    return new_master, new_first, new_second


def reduce_kernel(
    grad,
    owner_hbm,
    step_ref,
    master_hbm,
    first_hbm,
    second_hbm,
    w_all,
    small_hbm,
    owner_ref,
    state_in,
    small,
    g,
    gy,
    tmp,
    in1x,
    in1y,
    core_out,
    core_in,
    part,
    in2,
    in3,
    zsend,
    zin,
    sums,
    squares,
    sel_out,
    opt_out,
    opt_in,
    opt_all,
    onehot,
    w_part,
    load_sem,
    step1_sem,
    core_sem,
    step2_sem,
    dim2_sem,
    opt_sem,
    gather_sem,
    z_sem,
    norm_sem,
    ag2_sem,
    ag1_sem,
    out_sem,
    send_sem,
    token_sem,
):
    d = lax.axis_index("dp")
    y = lax.axis_index("rep")
    z = d // 8
    w = d % 8
    x = w // 2
    c = d % 2
    slab = c * 4 + x
    q = y * 8 + w

    def dev(zz, xx, cc, yy):
        return (zz * 8 + xx * 2 + cc, yy)

    def remote(src, dst, send, recv, device):
        copy = pltpu.make_async_remote_copy(
            src_ref=src,
            dst_ref=dst,
            send_sem=send,
            recv_sem=recv,
            device_id=device,
            device_id_type=MESH,
        )
        copy.start()
        return copy

    def drain(ref, sem):
        pltpu.make_async_copy(ref, ref, sem).wait()

    partner = dev(z, x, 1 - c, y)

    inputs = []
    for i, (src, dst) in enumerate(
        (
            (master_hbm, state_in.at[0]),
            (first_hbm, state_in.at[1]),
            (second_hbm, state_in.at[2]),
            (owner_hbm, owner_ref),
        )
    ):
        inputs.append(pltpu.make_async_copy(src, dst, load_sem.at[4 + i]))
        inputs[i].start()
    loads = {}
    for f in (1, 3, 0, 2):
        loads[f] = pltpu.make_async_copy(
            grad.at[pl.ds(256 * f, 256)], g.at[pl.ds(256 * f, 256)], load_sem.at[f]
        )
        loads[f].start()

    def xc_peer(o):
        t = (w + o) % 8
        return dev(z, t // 2, t % 2, y)

    right = dev((z + 1) % NZ, x, c, y)
    left = dev((z + NZ - 1) % NZ, x, c, y)

    barrier = pltpu.get_barrier_semaphore()
    near = [xc_peer(o) for o in range(1, 8)]
    near += [dev(z, x, c, (y + o) % 4) for o in range(1, 4)] + [right, left]
    for device in near:
        pl.semaphore_signal(barrier, inc=1, device_id=device, device_id_type=MESH)

    for copy in inputs:
        copy.wait()
    for k in range(8):
        for a in range(3):
            opt_out[k % 4, k // 4, a] = state_in[a, 0, :, 128 * k : 128 * k + 128]

    def token(i, distance):
        for to in ((z + distance) % NZ, (z + NZ - distance) % NZ):
            pl.semaphore_signal(
                token_sem.at[i], inc=1, device_id=dev(to, x, c, y), device_id_type=MESH
            )

    pl.semaphore_wait(barrier, len(near))
    token(0, 1)

    for o in range(1, 4):
        xt = (x + o) % 4
        remote(opt_out.at[xt], opt_in.at[w], send_sem.at[0], opt_sem.at[0], dev(z, xt, 1, y))

    @pl.when(c == 0)
    def _():
        remote(opt_out.at[x], opt_in.at[w], send_sem.at[0], opt_sem.at[0], partner)

    @pl.when(c == 1)
    def _():
        opt_in[w] = opt_out[x]

    flows = []
    for f in range(4):
        along_x = f % 2 == 0
        s0, s1 = (flip1, flip3) if f < 2 else (flip3, flip1)
        c1, c2 = (x, y) if along_x else (y, x)
        peer_x = lambda v: dev(z, v, c, y)
        peer_y = lambda v: dev(z, x, c, v)
        peer1, peer2 = (peer_x, peer_y) if along_x else (peer_y, peer_x)
        flows.append((along_x, s0(c1), s1(c1), c1, c2, peer1, peer2))

    def column(core, k):
        return pl.ds(pl.multiple_of(512 * core + 128 * k, 128), 128)

    step1 = {}

    def send_step1(f):
        along_x, p, qq, c1, c2, peer1, peer2 = flows[f]
        h = f // 2
        for k in range(4):
            index = flip2(c1) if k < 2 else p
            core = 1 - c if k % 2 == 0 else c
            if along_x:
                src = grad.at[pl.ds(256 * f, 256), column(core, index)]
                dst = in1x.at[h, k]
            else:
                src = gy.at[h, index, core]
                dst = in1y.at[h, k]
            step1[f, k] = remote(
                src, dst, send_sem.at[1 if along_x else 2], step1_sem.at[f, k], peer1(p)
            )

    send_step1(0)
    send_step1(2)
    for f in (1, 3):
        loads[f].wait()
        for k in range(8):
            tmp[k % 2] = g[256 * f : 256 * f + 256, 128 * k : 128 * k + 128].astype(F32)
            for r in range(4):
                gy[f // 2, r, k // 4, k % 4] = tmp[k % 2, pl.ds(r, 64, stride=4), :].astype(BF16)
        send_step1(f)

    pl.semaphore_wait(token_sem.at[0], 2)
    token(1, 2)

    def pass_state(d, t, side, half=None):
        src = opt_all.at[(z + d + NZ) % NZ, side]
        if half is not None:
            src = src.at[:, pl.ds(16 * half, 16)]
        sem = gather_sem.at[side, GATHERED.index((d - t, half))]
        remote(src, src, send_sem.at[3], sem, dev((z + t + NZ) % NZ, x, c, y))

    def hand_over(d):
        src = opt_all.at[(z + d + NZ) % NZ, 0]
        remote(src, src, send_sem.at[10], opt_sem.at[1], partner)

    def take_state(d, side):
        if d == 8:
            for half in range(2):
                drain(
                    opt_all.at[0, 0, :, pl.ds(0, 16)],
                    gather_sem.at[side, GATHERED.index((16 * half - 8, half))],
                )
        else:
            drain(opt_all.at[0, 0], gather_sem.at[side, GATHERED.index((d, None))])

    def relay(s):
        for side in range(2):
            for d in (-s, s):
                take_state(d, side)
                on = 1 if d < 0 else -1
                pass_state(d, on, side, None if s < 7 else (d + 7) // 14)
                if side == 0:
                    hand_over(d)

    pl.semaphore_wait(token_sem.at[1], 2)
    token(2, 4)

    @pl.when(c == 1)
    def _():
        drain(opt_in.at[pl.ds(0, 7)], opt_sem.at[0])
        for ws in range(8):
            for side in range(2):
                for a in range(3):
                    opt_all[z, side, a, 4 * ws : 4 * ws + 4] = opt_in[ws, side, a]
        for side in range(2):
            for t in (1, -1):
                pass_state(0, t, side)
        hand_over(0)

    loads[0].wait()
    loads[2].wait()

    def pair_sum(f, k, put):
        along_x, p, qq, c1, c2, peer1, peer2 = flows[f]
        h = f // 2
        index = qq if k < 2 else c1
        core = 1 - c if k % 2 == 0 else c
        step1[f, k].wait_recv()
        if along_x:
            own = g[256 * f : 256 * f + 256, column(core, index)]
            tmp[h] = own.astype(F32) + in1x[h, k].astype(F32)
            for r in range(4):
                put(r, tmp[h, pl.ds(r, 64, stride=4), :])
        else:
            for j in range(4):
                put(j, gy[h, index, core, j].astype(F32) + in1y[h, k, j].astype(F32))

    core = {}

    def to_core(f, half):
        def put(j, value):
            core_out[f, half, j] = value

        pair_sum(f, 2 * half, put)
        core[f, half] = remote(
            core_out.at[f, half],
            core_in.at[f, half],
            send_sem.at[4],
            core_sem.at[f, half],
            partner,
        )

    def keep(f, half):
        index = flows[f][2] if half == 0 else flows[f][3]

        def put(j, value):
            part[f, index, j] = value

        pair_sum(f, 2 * half + 1, put)

    step2 = {}
    for f in FLOWS:
        to_core(f, 0)
    for f in FLOWS:
        keep(f, 0)
    for f in FLOWS:
        along_x, p, qq, c1, c2, peer1, peer2 = flows[f]
        core[f, 0].wait_recv()
        part[f, qq] = part[f, qq] + core_in[f, 0]
        step2[f] = remote(
            part.at[f, qq], in2.at[f], send_sem.at[5], step2_sem.at[f], peer1(qq)
        )
    @pl.when(c == 1)
    def _():
        relay(1)

    for f in FLOWS:
        to_core(f, 1)

    row_id = lax.broadcasted_iota(jnp.int32, (256, 256), 0)
    col_id = lax.broadcasted_iota(jnp.int32, (256, 256), 1)
    owner_row = jnp.broadcast_to(owner_ref[...].astype(F32), (256, 256))
    owner_col = jnp.sum(jnp.where(row_id == col_id, owner_row, 0.0), axis=1, keepdims=True)
    same = owner_col == owner_row
    rank_col = jnp.sum(jnp.where(same & (col_id < row_id), 1.0, 0.0), axis=1, keepdims=True)
    rank_row = jnp.sum(jnp.where(same & (row_id < col_id), 1.0, 0.0), axis=0, keepdims=True)
    pos_col = (owner_col * 4.0 + rank_col).astype(jnp.int32)
    pos_row = (owner_ref[...].astype(F32) * 4.0 + rank_row).astype(jnp.int32)
    onehot[...] = (pos_col == lax.broadcasted_iota(jnp.int32, (256, 512), 1)).astype(F32).astype(BF16)
    chosen = (pos_row == z * 32 + lax.broadcasted_iota(jnp.int32, (32, 256), 0)).astype(F32)
    mine = (pos_row == d * 4 + lax.broadcasted_iota(jnp.int32, (4, 256), 0)).astype(F32)
    small[9] = jnp.broadcast_to(jnp.sum(mine, axis=1, keepdims=True), (4, 128))

    for f in FLOWS:
        keep(f, 1)
    for f in FLOWS:
        along_x, p, qq, c1, c2, peer1, peer2 = flows[f]
        core[f, 1].wait_recv()
        step2[f].wait_recv()
        part[f, c1] = part[f, c1] + core_in[f, 1] + in2[f]
        for o in (2, 1, 3):
            to = (c2 + o) % 4
            remote(
                part.at[f, c1, to], in3.at[f, o - 1], send_sem.at[6], dim2_sem.at[f], peer2(to)
            )
        if f == 0:

            @pl.when(c == 1)
            def _():
                relay(2)

    pl.semaphore_wait(token_sem.at[2], 2)

    def reduce_z(to):
        @pl.when(z != to)
        def _():
            remote(
                zsend.at[to],
                zin.at[(to - z + NZ) % NZ],
                send_sem.at[7],
                z_sem.at[0],
                dev(to, x, c, y),
            )

    for f in FLOWS:
        along_x, p, qq, c1, c2, peer1, peer2 = flows[f]
        drain(in3.at[f], dim2_sem.at[f])
        total = part[f, c1, c2] + in3[f, 0] + in3[f, 1] + in3[f, 2]
        for k in range(4):
            zsend[4 * f + k] = total[16 * k : 16 * k + 16]
        for k in range(4):
            reduce_z(4 * f + k)
        if f == 0:

            @pl.when(c == 1)
            def _():
                relay(3)

    order = [8, 7, 9, 6, 10, 5, 11, 4, 12, 3, 13, 2, 14, 1, 15]
    zin[0] = zsend[z]

    @pl.when(c == 1)
    def _():
        relay(4)
        relay(5)

    first_fix, second_fix = corrections(step_ref)
    drain(zin.at[pl.ds(1, 15)], z_sem.at[0])
    sums[z] = jnp.sum(zin[...], axis=0)
    for o in order:
        to = (z + o) % NZ
        remote(sums.at[z], sums.at[z], send_sem.at[8], z_sem.at[1], dev(to, x, c, y))

    @pl.when(c == 1)
    def _():
        relay(6)
        relay(7)

    drain(sums.at[pl.ds(0, 15)], z_sem.at[1])

    summed = sums[...].reshape(256, 128)
    squares[q] = jnp.sum(summed * summed, axis=0, keepdims=True)
    for o in range(1, 32):
        t = (q + o) % 32
        remote(
            squares.at[q],
            squares.at[q],
            send_sem.at[9],
            norm_sem.at[0],
            dev(z, (t // 2) % 4, t % 2, t // 8),
        )
    picked = jnp.dot(chosen, summed, precision=HIGH, preferred_element_type=F32)
    for k in range(8):
        sel_out[k] = picked[4 * k : 4 * k + 4]
    for o in range(1, 8):
        remote(
            sel_out.at[(w + o) % 8], small.at[slab], send_sem.at[11], norm_sem.at[1], xc_peer(o)
        )
    small[slab] = sel_out[w]

    @pl.when(c == 1)
    def _():
        take_state(8, 0)
        hand_over(8)
        take_state(8, 1)


    @pl.when(c == 0)
    def _():
        drain(opt_all.at[pl.ds(0, 8)], opt_sem.at[1])

    pieces = []
    for a in range(3):
        table = opt_all[:, c, a].reshape(512, 128)
        for _ in range(3):
            pieces.append(table.astype(BF16))
            table = table - pieces[-1].astype(F32)
    spread = jnp.dot(
        onehot[...], jnp.concatenate(pieces, axis=1), preferred_element_type=F32
    )
    thirds = [spread[:, 128 * i : 128 * i + 128] for i in range(9)]
    states = [thirds[3 * a] + thirds[3 * a + 1] + thirds[3 * a + 2] for a in range(3)]
    drain(squares.at[pl.ds(0, 31)], norm_sem.at[0])
    squares_total = jnp.sum(jnp.sum(squares[...], axis=0), keepdims=True)
    limit = jnp.float32(1024.0)
    scale = limit / jnp.maximum(jnp.sqrt(squares_total), limit)
    rounded = adam(summed, *states, scale, first_fix, second_fix)[0].astype(BF16)

    def forward(f, j):
        along_x, p, qq, c1, c2, peer1, peer2 = flows[f]
        piece = w_part.at[f, c1, j]
        remote(piece, piece, send_sem.at[13], ag1_sem.at[f, 2], peer1(flip2(c1)))
        remote(piece, piece, send_sem.at[13], ag1_sem.at[f, 0], peer1(qq))
        remote(piece, piece, send_sem.at[13], ag1_sem.at[f, 1], peer1(p))

    ag2 = {}
    for f in FLOWS:
        along_x, p, qq, c1, c2, peer1, peer2 = flows[f]
        w_part[f, c1, c2] = rounded[64 * f : 64 * f + 64]
        own = w_part.at[f, c1, c2]
        for o in (2, 1, 3):
            ag2[f, o] = remote(
                own, own, send_sem.at[12], ag2_sem.at[f, o - 1], peer2((c2 + o) % 4)
            )
    for f in FLOWS:
        forward(f, flows[f][4])
    small[8] = jnp.broadcast_to(scale, (4, 128))

    def give(f, index):
        piece = w_part.at[f, index]
        remote(piece, w_all.at[c, f, index], send_sem.at[14], out_sem.at[0], partner)
        pltpu.make_async_copy(piece, w_all.at[c, f, index], out_sem.at[1]).start()

    for o in (1, 3, 2):
        for f in FLOWS:
            ag2[f, o].wait_recv()
            forward(f, (flows[f][4] + 4 - o) % 4)
    for f in FLOWS:
        give(f, flows[f][3])
    drain(small.at[pl.ds(0, 7)], norm_sem.at[1])
    small_copy = pltpu.make_async_copy(small, small_hbm, out_sem.at[2])
    small_copy.start()
    for f in FLOWS:
        along_x, p, qq, c1, c2, peer1, peer2 = flows[f]
        got = w_part.at[f, qq]
        drain(got, ag1_sem.at[f, 0])
        give(f, qq)
    for f in FLOWS:
        got = w_part.at[f, flows[f][1]]
        drain(got, ag1_sem.at[f, 1])
        give(f, flows[f][1])
    for f in FLOWS:
        got = w_part.at[f, flip2(flows[f][3])]
        drain(got, ag1_sem.at[f, 2])
        give(f, flip2(flows[f][3]))

    small_copy.wait()

    @pl.when(c == 0)
    def _():
        drain(opt_out, send_sem.at[0])

    @pl.when(c == 1)
    def _():
        drain(opt_out.at[pl.ds(0, 3)], send_sem.at[0])
        drain(opt_all.at[pl.ds(0, 15)], send_sem.at[3])
        drain(opt_all.at[pl.ds(0, 8)], send_sem.at[10])

    drain(in1x, send_sem.at[1])
    drain(in1y, send_sem.at[2])
    drain(core_out, send_sem.at[4])
    drain(in2, send_sem.at[5])
    drain(in3, send_sem.at[6])
    drain(zin.at[pl.ds(1, 15)], send_sem.at[7])
    drain(sums.at[pl.ds(0, 15)], send_sem.at[8])
    drain(squares.at[pl.ds(0, 31)], send_sem.at[9])
    drain(sel_out.at[pl.ds(0, 7)], send_sem.at[11])
    drain(w_part.at[0, pl.ds(0, 3)], send_sem.at[12])
    drain(w_part.at[pl.ds(0, 3)], send_sem.at[13])
    drain(w_part, send_sem.at[14])
    drain(w_part, out_sem.at[1])
    drain(w_all.at[1 - c], out_sem.at[0])


def result_kernel(
    w_all,
    small_hbm,
    step_ref,
    master_hbm,
    first_hbm,
    second_hbm,
    w_out,
    nm_out,
    nf_out,
    ns_out,
    small,
    state_in,
    state_out,
    w_in,
    rows,
    tmp,
    load_sem,
    in_sem,
    out_sem,
):
    loads = {}
    for f in range(4):
        for core in range(2):
            loads[f, core] = pltpu.make_async_copy(
                w_all.at[core, f], w_in.at[core, f], in_sem.at[f, core]
            )
            loads[f, core].start()
    inputs = []
    for i, (src, dst) in enumerate(
        (
            (small_hbm, small),
            (master_hbm, state_in.at[0]),
            (first_hbm, state_in.at[1]),
            (second_hbm, state_in.at[2]),
        )
    ):
        inputs.append(pltpu.make_async_copy(src, dst, load_sem.at[i]))
        inputs[i].start()
    fixes = corrections(step_ref)
    stores = []

    def store(src, dst):
        stores.append(pltpu.make_async_copy(src, dst, out_sem.at[len(stores)]))
        stores[-1].start()

    for f in range(4):
        if f == 2:
            for copy in inputs:
                copy.wait()
            scale = small[8, :1, :1]
            filled = small[9] > 0.5
            for k in range(8):
                cols = slice(128 * k, 128 * k + 128)
                olds = [state_in[a, 0, :, cols] for a in range(3)]
                for a, value in enumerate(adam(small[k], *olds, scale, *fixes)):
                    state_out[a, 0, :, cols] = jnp.where(filled, value, 0.0)
            for a, out in enumerate((nm_out, nf_out, ns_out)):
                store(state_out.at[a], out)
        for core in range(2):
            loads[f, core].wait()
            for k in range(4):
                for r in range(4):
                    i, j = (k, r) if f % 2 == 0 else (r, k)
                    tmp[k, pl.ds(r, 64, stride=4), :] = w_in[core, f, i, j].astype(F32)
                at = 512 * core + 128 * k
                rows[f, :, at : at + 128] = tmp[k].astype(BF16)
            half = pl.ds(512 * core, 512)
            store(rows.at[f, :, half], w_out.at[pl.ds(256 * f, 256), half])
    for copy in stores:
        copy.wait()


def local_step(gradient, owner_list, step_count, master, first_moment, second_moment):
    smem = pl.BlockSpec(memory_space=pltpu.SMEM)
    anywhere = pl.BlockSpec(memory_space=pl.ANY)
    dma = pltpu.SemaphoreType.DMA
    w_all, small = pl.pallas_call(
        reduce_kernel,
        out_shape=(
            jax.ShapeDtypeStruct((2, 4, 4, 4, 64, 128), BF16),
            jax.ShapeDtypeStruct((10, 4, 128), F32),
        ),
        in_specs=[anywhere, anywhere, smem, anywhere, anywhere, anywhere],
        out_specs=(anywhere, anywhere),
        scratch_shapes=[
            pltpu.VMEM((1, owner_list.shape[0]), jnp.int32),
            pltpu.VMEM((3, *master.shape), F32),
            pltpu.VMEM((10, 4, 128), F32),
            pltpu.VMEM((1024, 1024), BF16),
            pltpu.VMEM((2, 4, 2, 4, 64, 128), BF16),
            pltpu.VMEM((2, 256, 128), F32),
            pltpu.VMEM((2, 4, 256, 128), BF16),
            pltpu.VMEM((2, 4, 4, 64, 128), BF16),
            pltpu.VMEM((4, 2, 4, 64, 128), F32),
            pltpu.VMEM((4, 2, 4, 64, 128), F32),
            pltpu.VMEM((4, 4, 4, 64, 128), F32),
            pltpu.VMEM((4, 4, 64, 128), F32),
            pltpu.VMEM((4, 3, 64, 128), F32),
            pltpu.VMEM((NZ, 16, 128), F32),
            pltpu.VMEM((NZ, 16, 128), F32),
            pltpu.VMEM((NZ, 16, 128), F32),
            pltpu.VMEM((32, 1, 128), F32),
            pltpu.VMEM((8, 4, 128), F32),
            pltpu.VMEM((4, 2, 3, 4, 128), F32),
            pltpu.VMEM((8, 2, 3, 4, 128), F32),
            pltpu.VMEM((NZ, 2, 3, 32, 128), F32),
            pltpu.VMEM((256, 512), BF16),
            pltpu.VMEM((4, 4, 4, 64, 128), BF16),
            dma((8,)),
            dma((4, 4)),
            dma((4, 2)),
            dma((4,)),
            dma((4,)),
            dma((2,)),
            dma((2, 16)),
            dma((2,)),
            dma((2,)),
            dma((4, 3)),
            dma((4, 3)),
            dma((3,)),
            dma((15,)),
            pltpu.SemaphoreType.REGULAR((3,)),
        ],
        compiler_params=pltpu.CompilerParams(collective_id=0, has_side_effects=True),
        name="adam_reduce",
    )(
        gradient.reshape(gradient.shape[2:]),
        owner_list.reshape(1, owner_list.shape[0]),
        step_count,
        master,
        first_moment,
        second_moment,
    )
    state = jax.ShapeDtypeStruct(master.shape, F32)
    return pl.pallas_call(
        result_kernel,
        out_shape=(jax.ShapeDtypeStruct((1024, 1024), BF16), state, state, state),
        in_specs=[anywhere, anywhere, smem, anywhere, anywhere, anywhere],
        out_specs=(anywhere, anywhere, anywhere, anywhere),
        scratch_shapes=[
            pltpu.VMEM((10, 4, 128), F32),
            pltpu.VMEM((3, *master.shape), F32),
            pltpu.VMEM((3, *master.shape), F32),
            pltpu.VMEM((2, 4, 4, 4, 64, 128), BF16),
            pltpu.VMEM((4, 256, 1024), BF16),
            pltpu.VMEM((4, 256, 128), F32),
            dma((4,)),
            dma((4, 2)),
            dma((11,)),
        ],
        name="adam_results",
    )(w_all, small, step_count, master, first_moment, second_moment)


def solution(mesh):
    owned = P("dp", None, "rep")
    return jax.shard_map(
        local_step,
        mesh=mesh,
        in_specs=(P("dp", "rep", None, None), P(), P(), owned, owned, owned),
        out_specs=(P(), owned, owned, owned),
        check_vma=False,
    )
```

```python
import jax
import jax.numpy as jnp
from jax import lax
from jax.experimental import pallas as pl
from jax.experimental.pallas import tpu as pltpu
from jax.sharding import PartitionSpec as P

MESH = pl.DeviceIdType.MESH
F32 = jnp.float32
BF16 = jnp.bfloat16
HIGH = lax.Precision.HIGHEST
NZ = 16
FLOWS = (0, 2, 1, 3)
GATHERED = [(d, None) for d in range(-7, 8) if d] + [(-8, 0), (8, 1)]


def flip1(v):
    return v + 1 - 2 * (v % 2)


def flip2(v):
    return (v + 2) % 4


def flip3(v):
    return 3 - v


def integer_power(base, count):
    result = jnp.ones((1, 1), F32)
    factor = jnp.float32(base)
    for bit in range(5):
        result = jnp.where((count // (2**bit)) % 2 == 1, result * factor, result)
        factor = factor * factor
    return result


def corrections(step_ref):
    count = jnp.full((1, 1), step_ref[0], jnp.int32)
    return 1.0 - integer_power(0.9, count), 1.0 - integer_power(0.95, count)


def adam(total, master, first, second, scale, first_fix, second_fix):
    clipped = scale * total
    new_first = 0.9 * first + 0.1 * clipped
    new_second = 0.95 * second + 0.05 * clipped * clipped
    update = new_first / first_fix / (jnp.sqrt(new_second / second_fix) + 1e-08)
    new_master = master * (1.0 - 0.1 * 0.1) - 0.1 * update
    return new_master, new_first, new_second


def reduce_kernel(
    grad,
    owner_hbm,
    step_ref,
    master_hbm,
    first_hbm,
    second_hbm,
    w_all,
    small_hbm,
    owner_ref,
    state_in,
    small,
    g,
    gy,
    tmp,
    in1x,
    in1y,
    core_out,
    core_in,
    part,
    in2,
    in3,
    zsend,
    zin,
    sums,
    squares,
    sel_out,
    opt_out,
    opt_in,
    opt_all,
    onehot,
    w_part,
    load_sem,
    step1_sem,
    core_sem,
    step2_sem,
    dim2_sem,
    opt_sem,
    gather_sem,
    z_sem,
    norm_sem,
    ag2_sem,
    ag1_sem,
    out_sem,
    send_sem,
    token_sem,
):
    d = lax.axis_index("dp")
    y = lax.axis_index("rep")
    z = d // 8
    w = d % 8
    x = w // 2
    c = d % 2
    slab = c * 4 + x
    q = y * 8 + w

    def dev(zz, xx, cc, yy):
        return (zz * 8 + xx * 2 + cc, yy)

    def remote(src, dst, send, recv, device):
        copy = pltpu.make_async_remote_copy(
            src_ref=src,
            dst_ref=dst,
            send_sem=send,
            recv_sem=recv,
            device_id=device,
            device_id_type=MESH,
        )
        copy.start()
        return copy

    def drain(ref, sem):
        pltpu.make_async_copy(ref, ref, sem).wait()

    partner = dev(z, x, 1 - c, y)

    inputs = []
    for i, (src, dst) in enumerate(
        (
            (master_hbm, state_in.at[0]),
            (first_hbm, state_in.at[1]),
            (second_hbm, state_in.at[2]),
            (owner_hbm, owner_ref),
        )
    ):
        inputs.append(pltpu.make_async_copy(src, dst, load_sem.at[4 + i]))
        inputs[i].start()
    loads = {}
    for f in (1, 3, 0, 2):
        loads[f] = pltpu.make_async_copy(
            grad.at[pl.ds(256 * f, 256)], g.at[pl.ds(256 * f, 256)], load_sem.at[f]
        )
        loads[f].start()

    def xc_peer(o):
        t = (w + o) % 8
        return dev(z, t // 2, t % 2, y)

    right = dev((z + 1) % NZ, x, c, y)
    left = dev((z + NZ - 1) % NZ, x, c, y)

    barrier = pltpu.get_barrier_semaphore()
    near = [xc_peer(o) for o in range(1, 8)]
    near += [dev(z, x, c, (y + o) % 4) for o in range(1, 4)] + [right, left]
    for device in near:
        pl.semaphore_signal(barrier, inc=1, device_id=device, device_id_type=MESH)

    for copy in inputs:
        copy.wait()
    for k in range(8):
        for a in range(3):
            opt_out[k % 4, k // 4, a] = state_in[a, 0, :, 128 * k : 128 * k + 128]

    def token(i, distance):
        for to in ((z + distance) % NZ, (z + NZ - distance) % NZ):
            pl.semaphore_signal(
                token_sem.at[i], inc=1, device_id=dev(to, x, c, y), device_id_type=MESH
            )

    pl.semaphore_wait(barrier, len(near))
    token(0, 1)

    for o in range(1, 4):
        xt = (x + o) % 4
        remote(opt_out.at[xt], opt_in.at[w], send_sem.at[0], opt_sem.at[0], dev(z, xt, 1, y))

    @pl.when(c == 0)
    def _():
        remote(opt_out.at[x], opt_in.at[w], send_sem.at[0], opt_sem.at[0], partner)

    @pl.when(c == 1)
    def _():
        opt_in[w] = opt_out[x]

    flows = []
    for f in range(4):
        along_x = f % 2 == 0
        s0, s1 = (flip1, flip3) if f < 2 else (flip3, flip1)
        c1, c2 = (x, y) if along_x else (y, x)
        peer_x = lambda v: dev(z, v, c, y)
        peer_y = lambda v: dev(z, x, c, v)
        peer1, peer2 = (peer_x, peer_y) if along_x else (peer_y, peer_x)
        flows.append((along_x, s0(c1), s1(c1), c1, c2, peer1, peer2))

    def column(core, k):
        return pl.ds(pl.multiple_of(512 * core + 128 * k, 128), 128)

    step1 = {}

    def send_step1(f):
        along_x, p, qq, c1, c2, peer1, peer2 = flows[f]
        h = f // 2
        for k in range(4):
            index = flip2(c1) if k < 2 else p
            core = 1 - c if k % 2 == 0 else c
            if along_x:
                src = grad.at[pl.ds(256 * f, 256), column(core, index)]
                dst = in1x.at[h, k]
            else:
                src = gy.at[h, index, core]
                dst = in1y.at[h, k]
            step1[f, k] = remote(
                src, dst, send_sem.at[1 if along_x else 2], step1_sem.at[f, k], peer1(p)
            )

    send_step1(0)
    send_step1(2)
    for f in (1, 3):
        loads[f].wait()
        for k in range(8):
            tmp[k % 2] = g[256 * f : 256 * f + 256, 128 * k : 128 * k + 128].astype(F32)
            for r in range(4):
                gy[f // 2, r, k // 4, k % 4] = tmp[k % 2, pl.ds(r, 64, stride=4), :].astype(BF16)
        send_step1(f)

    pl.semaphore_wait(token_sem.at[0], 2)
    token(1, 2)

    def pass_state(d, t, side, half=None):
        src = opt_all.at[(z + d + NZ) % NZ, side]
        if half is not None:
            src = src.at[:, pl.ds(16 * half, 16)]
        sem = gather_sem.at[side, GATHERED.index((d - t, half))]
        remote(src, src, send_sem.at[3], sem, dev((z + t + NZ) % NZ, x, c, y))

    def hand_over(d):
        src = opt_all.at[(z + d + NZ) % NZ, 0]
        remote(src, src, send_sem.at[10], opt_sem.at[1], partner)

    def take_state(d, side):
        if d == 8:
            for half in range(2):
                drain(
                    opt_all.at[0, 0, :, pl.ds(0, 16)],
                    gather_sem.at[side, GATHERED.index((16 * half - 8, half))],
                )
        else:
            drain(opt_all.at[0, 0], gather_sem.at[side, GATHERED.index((d, None))])

    def relay(s):
        for side in range(2):
            for d in (-s, s):
                take_state(d, side)
                on = 1 if d < 0 else -1
                pass_state(d, on, side, None if s < 7 else (d + 7) // 14)
                if side == 0:
                    hand_over(d)

    pl.semaphore_wait(token_sem.at[1], 2)
    token(2, 4)

    @pl.when(c == 1)
    def _():
        drain(opt_in.at[pl.ds(0, 7)], opt_sem.at[0])
        for ws in range(8):
            for side in range(2):
                for a in range(3):
                    opt_all[z, side, a, 4 * ws : 4 * ws + 4] = opt_in[ws, side, a]
        for side in range(2):
            for t in (1, -1):
                pass_state(0, t, side)
        hand_over(0)

    loads[0].wait()
    loads[2].wait()

    def pair_sum(f, k, put):
        along_x, p, qq, c1, c2, peer1, peer2 = flows[f]
        h = f // 2
        index = qq if k < 2 else c1
        core = 1 - c if k % 2 == 0 else c
        step1[f, k].wait_recv()
        if along_x:
            own = g[256 * f : 256 * f + 256, column(core, index)]
            tmp[h] = own.astype(F32) + in1x[h, k].astype(F32)
            for r in range(4):
                put(r, tmp[h, pl.ds(r, 64, stride=4), :])
        else:
            for j in range(4):
                put(j, gy[h, index, core, j].astype(F32) + in1y[h, k, j].astype(F32))

    core = {}

    def to_core(f, half):
        def put(j, value):
            core_out[f, half, j] = value

        pair_sum(f, 2 * half, put)
        core[f, half] = remote(
            core_out.at[f, half],
            core_in.at[f, half],
            send_sem.at[4],
            core_sem.at[f, half],
            partner,
        )

    def keep(f, half):
        index = flows[f][2] if half == 0 else flows[f][3]

        def put(j, value):
            part[f, index, j] = value

        pair_sum(f, 2 * half + 1, put)

    step2 = {}
    for f in FLOWS:
        to_core(f, 0)
    for f in FLOWS:
        keep(f, 0)
    for f in FLOWS:
        along_x, p, qq, c1, c2, peer1, peer2 = flows[f]
        core[f, 0].wait_recv()
        part[f, qq] = part[f, qq] + core_in[f, 0]
        step2[f] = remote(
            part.at[f, qq], in2.at[f], send_sem.at[5], step2_sem.at[f], peer1(qq)
        )
    @pl.when(c == 1)
    def _():
        relay(1)

    for f in FLOWS:
        to_core(f, 1)

    row_id = lax.broadcasted_iota(jnp.int32, (256, 256), 0)
    col_id = lax.broadcasted_iota(jnp.int32, (256, 256), 1)
    owner_row = jnp.broadcast_to(owner_ref[...].astype(F32), (256, 256))
    owner_col = jnp.sum(jnp.where(row_id == col_id, owner_row, 0.0), axis=1, keepdims=True)
    same = owner_col == owner_row
    rank_col = jnp.sum(jnp.where(same & (col_id < row_id), 1.0, 0.0), axis=1, keepdims=True)
    rank_row = jnp.sum(jnp.where(same & (row_id < col_id), 1.0, 0.0), axis=0, keepdims=True)
    pos_col = (owner_col * 4.0 + rank_col).astype(jnp.int32)
    pos_row = (owner_ref[...].astype(F32) * 4.0 + rank_row).astype(jnp.int32)
    onehot[...] = (pos_col == lax.broadcasted_iota(jnp.int32, (256, 512), 1)).astype(F32).astype(BF16)
    chosen = (pos_row == z * 32 + lax.broadcasted_iota(jnp.int32, (32, 256), 0)).astype(F32)
    mine = (pos_row == d * 4 + lax.broadcasted_iota(jnp.int32, (4, 256), 0)).astype(F32)
    small[9] = jnp.broadcast_to(jnp.sum(mine, axis=1, keepdims=True), (4, 128))

    for f in FLOWS:
        keep(f, 1)
    for f in FLOWS:
        along_x, p, qq, c1, c2, peer1, peer2 = flows[f]
        core[f, 1].wait_recv()
        step2[f].wait_recv()
        part[f, c1] = part[f, c1] + core_in[f, 1] + in2[f]
        for o in (2, 1, 3):
            to = (c2 + o) % 4
            remote(
                part.at[f, c1, to], in3.at[f, o - 1], send_sem.at[6], dim2_sem.at[f], peer2(to)
            )
        if f == 0:

            @pl.when(c == 1)
            def _():
                relay(2)

    pl.semaphore_wait(token_sem.at[2], 2)

    def reduce_z(to):
        @pl.when(z != to)
        def _():
            remote(
                zsend.at[to],
                zin.at[(to - z + NZ) % NZ],
                send_sem.at[7],
                z_sem.at[0],
                dev(to, x, c, y),
            )

    for f in FLOWS:
        along_x, p, qq, c1, c2, peer1, peer2 = flows[f]
        drain(in3.at[f], dim2_sem.at[f])
        total = part[f, c1, c2] + in3[f, 0] + in3[f, 1] + in3[f, 2]
        for k in range(4):
            zsend[4 * f + k] = total[16 * k : 16 * k + 16]
        for k in range(4):
            reduce_z(4 * f + k)
        if f == 0:

            @pl.when(c == 1)
            def _():
                relay(3)

    order = [8, 7, 9, 6, 10, 5, 11, 4, 12, 3, 13, 2, 14, 1, 15]
    zin[0] = zsend[z]

    @pl.when(c == 1)
    def _():
        relay(4)
        relay(5)

    first_fix, second_fix = corrections(step_ref)
    drain(zin.at[pl.ds(1, 15)], z_sem.at[0])
    sums[z] = jnp.sum(zin[...], axis=0)
    for o in order:
        to = (z + o) % NZ
        remote(sums.at[z], sums.at[z], send_sem.at[8], z_sem.at[1], dev(to, x, c, y))

    @pl.when(c == 1)
    def _():
        relay(6)
        relay(7)

    drain(sums.at[pl.ds(0, 15)], z_sem.at[1])

    summed = sums[...].reshape(256, 128)
    squares[q] = jnp.sum(summed * summed, axis=0, keepdims=True)
    for o in range(1, 32):
        t = (q + o) % 32
        remote(
            squares.at[q],
            squares.at[q],
            send_sem.at[9],
            norm_sem.at[0],
            dev(z, (t // 2) % 4, t % 2, t // 8),
        )
    picked = jnp.dot(chosen, summed, precision=HIGH, preferred_element_type=F32)
    for k in range(8):
        sel_out[k] = picked[4 * k : 4 * k + 4]
    for o in range(1, 8):
        remote(
            sel_out.at[(w + o) % 8], small.at[slab], send_sem.at[11], norm_sem.at[1], xc_peer(o)
        )
    small[slab] = sel_out[w]

    @pl.when(c == 1)
    def _():
        take_state(8, 0)
        hand_over(8)
        take_state(8, 1)


    @pl.when(c == 0)
    def _():
        drain(opt_all.at[pl.ds(0, 8)], opt_sem.at[1])

    pieces = []
    for a in range(3):
        table = opt_all[:, c, a].reshape(512, 128)
        for _ in range(3):
            pieces.append(table.astype(BF16))
            table = table - pieces[-1].astype(F32)
    spread = jnp.dot(
        onehot[...], jnp.concatenate(pieces, axis=1), preferred_element_type=F32
    )
    thirds = [spread[:, 128 * i : 128 * i + 128] for i in range(9)]
    states = [thirds[3 * a] + thirds[3 * a + 1] + thirds[3 * a + 2] for a in range(3)]
    drain(squares.at[pl.ds(0, 31)], norm_sem.at[0])
    squares_total = jnp.sum(jnp.sum(squares[...], axis=0), keepdims=True)
    limit = jnp.float32(1024.0)
    scale = limit / jnp.maximum(jnp.sqrt(squares_total), limit)
    rounded = adam(summed, *states, scale, first_fix, second_fix)[0].astype(BF16)

    def forward(f, j):
        along_x, p, qq, c1, c2, peer1, peer2 = flows[f]
        piece = w_part.at[f, c1, j]
        remote(piece, piece, send_sem.at[13], ag1_sem.at[f, 0], peer1(qq))
        remote(piece, piece, send_sem.at[13], ag1_sem.at[f, 1], peer1(p))
        remote(piece, piece, send_sem.at[13], ag1_sem.at[f, 2], peer1(flip2(c1)))

    ag2 = {}
    for f in FLOWS:
        along_x, p, qq, c1, c2, peer1, peer2 = flows[f]
        w_part[f, c1, c2] = rounded[64 * f : 64 * f + 64]
        own = w_part.at[f, c1, c2]
        for o in (2, 1, 3):
            ag2[f, o] = remote(
                own, own, send_sem.at[12], ag2_sem.at[f, o - 1], peer2((c2 + o) % 4)
            )
    for f in FLOWS:
        forward(f, flows[f][4])
    small[8] = jnp.broadcast_to(scale, (4, 128))

    def give(f, index):
        piece = w_part.at[f, index]
        remote(piece, w_all.at[c, f, index], send_sem.at[14], out_sem.at[0], partner)
        pltpu.make_async_copy(piece, w_all.at[c, f, index], out_sem.at[1]).start()

    for o in (1, 3, 2):
        for f in FLOWS:
            ag2[f, o].wait_recv()
            forward(f, (flows[f][4] + 4 - o) % 4)
    for f in FLOWS:
        give(f, flows[f][3])
    drain(small.at[pl.ds(0, 7)], norm_sem.at[1])
    small_copy = pltpu.make_async_copy(small, small_hbm, out_sem.at[2])
    small_copy.start()
    for f in FLOWS:
        along_x, p, qq, c1, c2, peer1, peer2 = flows[f]
        got = w_part.at[f, qq]
        drain(got, ag1_sem.at[f, 0])
        give(f, qq)
    for f in FLOWS:
        got = w_part.at[f, flows[f][1]]
        drain(got, ag1_sem.at[f, 1])
        give(f, flows[f][1])
    for f in FLOWS:
        got = w_part.at[f, flip2(flows[f][3])]
        drain(got, ag1_sem.at[f, 2])
        give(f, flip2(flows[f][3]))

    small_copy.wait()

    @pl.when(c == 0)
    def _():
        drain(opt_out, send_sem.at[0])

    @pl.when(c == 1)
    def _():
        drain(opt_out.at[pl.ds(0, 3)], send_sem.at[0])
        drain(opt_all.at[pl.ds(0, 15)], send_sem.at[3])
        drain(opt_all.at[pl.ds(0, 8)], send_sem.at[10])

    drain(in1x, send_sem.at[1])
    drain(in1y, send_sem.at[2])
    drain(core_out, send_sem.at[4])
    drain(in2, send_sem.at[5])
    drain(in3, send_sem.at[6])
    drain(zin.at[pl.ds(1, 15)], send_sem.at[7])
    drain(sums.at[pl.ds(0, 15)], send_sem.at[8])
    drain(squares.at[pl.ds(0, 31)], send_sem.at[9])
    drain(sel_out.at[pl.ds(0, 7)], send_sem.at[11])
    drain(w_part.at[0, pl.ds(0, 3)], send_sem.at[12])
    drain(w_part.at[pl.ds(0, 3)], send_sem.at[13])
    drain(w_part, send_sem.at[14])
    drain(w_part, out_sem.at[1])
    drain(w_all.at[1 - c], out_sem.at[0])


def result_kernel(
    w_all,
    small_hbm,
    step_ref,
    master_hbm,
    first_hbm,
    second_hbm,
    w_out,
    nm_out,
    nf_out,
    ns_out,
    small,
    state_in,
    state_out,
    w_in,
    rows,
    tmp,
    load_sem,
    in_sem,
    out_sem,
):
    loads = {}
    for f in range(4):
        for core in range(2):
            loads[f, core] = pltpu.make_async_copy(
                w_all.at[core, f], w_in.at[core, f], in_sem.at[f, core]
            )
            loads[f, core].start()
    inputs = []
    for i, (src, dst) in enumerate(
        (
            (small_hbm, small),
            (master_hbm, state_in.at[0]),
            (first_hbm, state_in.at[1]),
            (second_hbm, state_in.at[2]),
        )
    ):
        inputs.append(pltpu.make_async_copy(src, dst, load_sem.at[i]))
        inputs[i].start()
    fixes = corrections(step_ref)
    stores = []

    def store(src, dst):
        stores.append(pltpu.make_async_copy(src, dst, out_sem.at[len(stores)]))
        stores[-1].start()

    for f in range(4):
        if f == 2:
            for copy in inputs:
                copy.wait()
            scale = small[8, :1, :1]
            filled = small[9] > 0.5
            for k in range(8):
                cols = slice(128 * k, 128 * k + 128)
                olds = [state_in[a, 0, :, cols] for a in range(3)]
                for a, value in enumerate(adam(small[k], *olds, scale, *fixes)):
                    state_out[a, 0, :, cols] = jnp.where(filled, value, 0.0)
            for a, out in enumerate((nm_out, nf_out, ns_out)):
                store(state_out.at[a], out)
        for core in range(2):
            loads[f, core].wait()
            for k in range(4):
                for r in range(4):
                    i, j = (k, r) if f % 2 == 0 else (r, k)
                    tmp[k, pl.ds(r, 64, stride=4), :] = w_in[core, f, i, j].astype(F32)
                at = 512 * core + 128 * k
                rows[f, :, at : at + 128] = tmp[k].astype(BF16)
            half = pl.ds(512 * core, 512)
            store(rows.at[f, :, half], w_out.at[pl.ds(256 * f, 256), half])
    for copy in stores:
        copy.wait()


def local_step(gradient, owner_list, step_count, master, first_moment, second_moment):
    smem = pl.BlockSpec(memory_space=pltpu.SMEM)
    anywhere = pl.BlockSpec(memory_space=pl.ANY)
    dma = pltpu.SemaphoreType.DMA
    w_all, small = pl.pallas_call(
        reduce_kernel,
        out_shape=(
            jax.ShapeDtypeStruct((2, 4, 4, 4, 64, 128), BF16),
            jax.ShapeDtypeStruct((10, 4, 128), F32),
        ),
        in_specs=[anywhere, anywhere, smem, anywhere, anywhere, anywhere],
        out_specs=(anywhere, anywhere),
        scratch_shapes=[
            pltpu.VMEM((1, owner_list.shape[0]), jnp.int32),
            pltpu.VMEM((3, *master.shape), F32),
            pltpu.VMEM((10, 4, 128), F32),
            pltpu.VMEM((1024, 1024), BF16),
            pltpu.VMEM((2, 4, 2, 4, 64, 128), BF16),
            pltpu.VMEM((2, 256, 128), F32),
            pltpu.VMEM((2, 4, 256, 128), BF16),
            pltpu.VMEM((2, 4, 4, 64, 128), BF16),
            pltpu.VMEM((4, 2, 4, 64, 128), F32),
            pltpu.VMEM((4, 2, 4, 64, 128), F32),
            pltpu.VMEM((4, 4, 4, 64, 128), F32),
            pltpu.VMEM((4, 4, 64, 128), F32),
            pltpu.VMEM((4, 3, 64, 128), F32),
            pltpu.VMEM((NZ, 16, 128), F32),
            pltpu.VMEM((NZ, 16, 128), F32),
            pltpu.VMEM((NZ, 16, 128), F32),
            pltpu.VMEM((32, 1, 128), F32),
            pltpu.VMEM((8, 4, 128), F32),
            pltpu.VMEM((4, 2, 3, 4, 128), F32),
            pltpu.VMEM((8, 2, 3, 4, 128), F32),
            pltpu.VMEM((NZ, 2, 3, 32, 128), F32),
            pltpu.VMEM((256, 512), BF16),
            pltpu.VMEM((4, 4, 4, 64, 128), BF16),
            dma((8,)),
            dma((4, 4)),
            dma((4, 2)),
            dma((4,)),
            dma((4,)),
            dma((2,)),
            dma((2, 16)),
            dma((2,)),
            dma((2,)),
            dma((4, 3)),
            dma((4, 3)),
            dma((3,)),
            dma((15,)),
            pltpu.SemaphoreType.REGULAR((3,)),
        ],
        compiler_params=pltpu.CompilerParams(collective_id=0, has_side_effects=True),
        name="adam_reduce",
    )(
        gradient.reshape(gradient.shape[2:]),
        owner_list.reshape(1, owner_list.shape[0]),
        step_count,
        master,
        first_moment,
        second_moment,
    )
    state = jax.ShapeDtypeStruct(master.shape, F32)
    return pl.pallas_call(
        result_kernel,
        out_shape=(jax.ShapeDtypeStruct((1024, 1024), BF16), state, state, state),
        in_specs=[anywhere, anywhere, smem, anywhere, anywhere, anywhere],
        out_specs=(anywhere, anywhere, anywhere, anywhere),
        scratch_shapes=[
            pltpu.VMEM((10, 4, 128), F32),
            pltpu.VMEM((3, *master.shape), F32),
            pltpu.VMEM((3, *master.shape), F32),
            pltpu.VMEM((2, 4, 4, 4, 64, 128), BF16),
            pltpu.VMEM((4, 256, 1024), BF16),
            pltpu.VMEM((4, 256, 128), F32),
            dma((4,)),
            dma((4, 2)),
            dma((11,)),
        ],
        name="adam_results",
    )(w_all, small, step_count, master, first_moment, second_moment)


def solution(mesh):
    owned = P("dp", None, "rep")
    return jax.shard_map(
        local_step,
        mesh=mesh,
        in_specs=(P("dp", "rep", None, None), P(), P(), owned, owned, owned),
        out_specs=(P(), owned, owned, owned),
        check_vma=False,
    )
```

```python
import jax
import jax.numpy as jnp
from jax import lax
from jax.experimental import pallas as pl
from jax.experimental.pallas import tpu as pltpu
from jax.sharding import PartitionSpec as P

MESH = pl.DeviceIdType.MESH
F32 = jnp.float32
BF16 = jnp.bfloat16
HIGH = lax.Precision.HIGHEST
NZ = 16
FLOWS = (0, 2, 1, 3)
GATHERED = [(d, None) for d in range(-7, 8) if d] + [(-8, 0), (8, 1)]


def flip1(v):
    return v + 1 - 2 * (v % 2)


def flip2(v):
    return (v + 2) % 4


def flip3(v):
    return 3 - v


def integer_power(base, count):
    result = jnp.ones((1, 1), F32)
    factor = jnp.float32(base)
    for bit in range(5):
        result = jnp.where((count // (2**bit)) % 2 == 1, result * factor, result)
        factor = factor * factor
    return result


def corrections(step_ref):
    count = jnp.full((1, 1), step_ref[0], jnp.int32)
    return 1.0 - integer_power(0.9, count), 1.0 - integer_power(0.95, count)


def adam(total, master, first, second, scale, first_fix, second_fix):
    clipped = scale * total
    new_first = 0.9 * first + 0.1 * clipped
    new_second = 0.95 * second + 0.05 * clipped * clipped
    update = new_first / first_fix / (jnp.sqrt(new_second / second_fix) + 1e-08)
    new_master = master * (1.0 - 0.1 * 0.1) - 0.1 * update
    return new_master, new_first, new_second


def reduce_kernel(
    grad,
    owner_hbm,
    step_ref,
    master_hbm,
    first_hbm,
    second_hbm,
    w_all,
    small_hbm,
    owner_ref,
    state_in,
    small,
    g,
    gy,
    tmp,
    in1x,
    in1y,
    core_out,
    core_in,
    part,
    in2,
    in3,
    zsend,
    zin,
    sums,
    squares,
    sel_out,
    opt_out,
    opt_in,
    opt_all,
    onehot,
    w_part,
    load_sem,
    step1_sem,
    core_sem,
    step2_sem,
    dim2_sem,
    opt_sem,
    gather_sem,
    z_sem,
    norm_sem,
    ag2_sem,
    ag1_sem,
    out_sem,
    send_sem,
    token_sem,
):
    d = lax.axis_index("dp")
    y = lax.axis_index("rep")
    z = d // 8
    w = d % 8
    x = w // 2
    c = d % 2
    slab = c * 4 + x
    q = y * 8 + w

    def dev(zz, xx, cc, yy):
        return (zz * 8 + xx * 2 + cc, yy)

    def remote(src, dst, send, recv, device):
        copy = pltpu.make_async_remote_copy(
            src_ref=src,
            dst_ref=dst,
            send_sem=send,
            recv_sem=recv,
            device_id=device,
            device_id_type=MESH,
        )
        copy.start()
        return copy

    def drain(ref, sem):
        pltpu.make_async_copy(ref, ref, sem).wait()

    partner = dev(z, x, 1 - c, y)

    inputs = []
    for i, (src, dst) in enumerate(
        (
            (master_hbm, state_in.at[0]),
            (first_hbm, state_in.at[1]),
            (second_hbm, state_in.at[2]),
            (owner_hbm, owner_ref),
        )
    ):
        inputs.append(pltpu.make_async_copy(src, dst, load_sem.at[4 + i]))
        inputs[i].start()
    loads = {}
    for f in (1, 3, 0, 2):
        loads[f] = pltpu.make_async_copy(
            grad.at[pl.ds(256 * f, 256)], g.at[pl.ds(256 * f, 256)], load_sem.at[f]
        )
        loads[f].start()

    def xc_peer(o):
        t = (w + o) % 8
        return dev(z, t // 2, t % 2, y)

    right = dev((z + 1) % NZ, x, c, y)
    left = dev((z + NZ - 1) % NZ, x, c, y)

    barrier = pltpu.get_barrier_semaphore()
    near = [xc_peer(o) for o in range(1, 8)]
    near += [dev(z, x, c, (y + o) % 4) for o in range(1, 4)] + [right, left]
    for device in near:
        pl.semaphore_signal(barrier, inc=1, device_id=device, device_id_type=MESH)

    for copy in inputs:
        copy.wait()
    for k in range(8):
        for a in range(3):
            opt_out[k % 4, k // 4, a] = state_in[a, 0, :, 128 * k : 128 * k + 128]

    def token(i, distance):
        for to in ((z + distance) % NZ, (z + NZ - distance) % NZ):
            pl.semaphore_signal(
                token_sem.at[i], inc=1, device_id=dev(to, x, c, y), device_id_type=MESH
            )

    pl.semaphore_wait(barrier, len(near))
    token(0, 1)

    for o in range(1, 4):
        xt = (x + o) % 4
        remote(opt_out.at[xt], opt_in.at[w], send_sem.at[0], opt_sem.at[0], dev(z, xt, 1, y))

    @pl.when(c == 0)
    def _():
        remote(opt_out.at[x], opt_in.at[w], send_sem.at[0], opt_sem.at[0], partner)

    @pl.when(c == 1)
    def _():
        opt_in[w] = opt_out[x]

    flows = []
    for f in range(4):
        along_x = f % 2 == 0
        s0, s1 = (flip1, flip3) if f < 2 else (flip3, flip1)
        c1, c2 = (x, y) if along_x else (y, x)
        peer_x = lambda v: dev(z, v, c, y)
        peer_y = lambda v: dev(z, x, c, v)
        peer1, peer2 = (peer_x, peer_y) if along_x else (peer_y, peer_x)
        flows.append((along_x, s0(c1), s1(c1), c1, c2, peer1, peer2))

    def column(core, k):
        return pl.ds(pl.multiple_of(512 * core + 128 * k, 128), 128)

    step1 = {}

    def send_step1(f):
        along_x, p, qq, c1, c2, peer1, peer2 = flows[f]
        h = f // 2
        for k in range(4):
            index = flip2(c1) if k < 2 else p
            core = 1 - c if k % 2 == 0 else c
            if along_x:
                src = grad.at[pl.ds(256 * f, 256), column(core, index)]
                dst = in1x.at[h, k]
            else:
                src = gy.at[h, index, core]
                dst = in1y.at[h, k]
            step1[f, k] = remote(
                src, dst, send_sem.at[1 if along_x else 2], step1_sem.at[f, k], peer1(p)
            )

    send_step1(0)
    send_step1(2)
    for f in (1, 3):
        loads[f].wait()
        for k in range(8):
            tmp[k % 2] = g[256 * f : 256 * f + 256, 128 * k : 128 * k + 128].astype(F32)
            for r in range(4):
                gy[f // 2, r, k // 4, k % 4] = tmp[k % 2, pl.ds(r, 64, stride=4), :].astype(BF16)
        send_step1(f)

    pl.semaphore_wait(token_sem.at[0], 2)
    token(1, 2)

    def pass_state(d, t, side, half=None):
        src = opt_all.at[(z + d + NZ) % NZ, side]
        if half is not None:
            src = src.at[:, pl.ds(16 * half, 16)]
        sem = gather_sem.at[side, GATHERED.index((d - t, half))]
        remote(src, src, send_sem.at[3], sem, dev((z + t + NZ) % NZ, x, c, y))

    def hand_over(d):
        src = opt_all.at[(z + d + NZ) % NZ, 0]
        remote(src, src, send_sem.at[10], opt_sem.at[1], partner)

    def take_state(d, side):
        if d == 8:
            for half in range(2):
                drain(
                    opt_all.at[0, 0, :, pl.ds(0, 16)],
                    gather_sem.at[side, GATHERED.index((16 * half - 8, half))],
                )
        else:
            drain(opt_all.at[0, 0], gather_sem.at[side, GATHERED.index((d, None))])

    def relay(s):
        for side in range(2):
            for d in (-s, s):
                take_state(d, side)
                on = 1 if d < 0 else -1
                pass_state(d, on, side, None if s < 7 else (d + 7) // 14)
                if side == 0:
                    hand_over(d)

    pl.semaphore_wait(token_sem.at[1], 2)
    token(2, 4)

    @pl.when(c == 1)
    def _():
        drain(opt_in.at[pl.ds(0, 7)], opt_sem.at[0])
        for ws in range(8):
            for side in range(2):
                for a in range(3):
                    opt_all[z, side, a, 4 * ws : 4 * ws + 4] = opt_in[ws, side, a]
        for side in range(2):
            for t in (1, -1):
                pass_state(0, t, side)
        hand_over(0)

    loads[0].wait()
    loads[2].wait()

    def pair_sum(f, k, put):
        along_x, p, qq, c1, c2, peer1, peer2 = flows[f]
        h = f // 2
        index = qq if k < 2 else c1
        core = 1 - c if k % 2 == 0 else c
        step1[f, k].wait_recv()
        if along_x:
            own = g[256 * f : 256 * f + 256, column(core, index)]
            tmp[h] = own.astype(F32) + in1x[h, k].astype(F32)
            for r in range(4):
                put(r, tmp[h, pl.ds(r, 64, stride=4), :])
        else:
            for j in range(4):
                put(j, gy[h, index, core, j].astype(F32) + in1y[h, k, j].astype(F32))

    core = {}

    def to_core(f, half):
        def put(j, value):
            core_out[f, half, j] = value

        pair_sum(f, 2 * half, put)
        core[f, half] = remote(
            core_out.at[f, half],
            core_in.at[f, half],
            send_sem.at[4],
            core_sem.at[f, half],
            partner,
        )

    def keep(f, half):
        index = flows[f][2] if half == 0 else flows[f][3]

        def put(j, value):
            part[f, index, j] = value

        pair_sum(f, 2 * half + 1, put)

    step2 = {}
    for f in FLOWS:
        to_core(f, 0)
    for f in FLOWS:
        keep(f, 0)
    for f in FLOWS:
        along_x, p, qq, c1, c2, peer1, peer2 = flows[f]
        core[f, 0].wait_recv()
        part[f, qq] = part[f, qq] + core_in[f, 0]
        step2[f] = remote(
            part.at[f, qq], in2.at[f], send_sem.at[5], step2_sem.at[f], peer1(qq)
        )
    @pl.when(c == 1)
    def _():
        relay(1)

    for f in FLOWS:
        to_core(f, 1)

    row_id = lax.broadcasted_iota(jnp.int32, (256, 256), 0)
    col_id = lax.broadcasted_iota(jnp.int32, (256, 256), 1)
    owner_row = jnp.broadcast_to(owner_ref[...].astype(F32), (256, 256))
    owner_col = jnp.sum(jnp.where(row_id == col_id, owner_row, 0.0), axis=1, keepdims=True)
    same = owner_col == owner_row
    rank_col = jnp.sum(jnp.where(same & (col_id < row_id), 1.0, 0.0), axis=1, keepdims=True)
    rank_row = jnp.sum(jnp.where(same & (row_id < col_id), 1.0, 0.0), axis=0, keepdims=True)
    pos_col = (owner_col * 4.0 + rank_col).astype(jnp.int32)
    pos_row = (owner_ref[...].astype(F32) * 4.0 + rank_row).astype(jnp.int32)
    onehot[...] = (pos_col == lax.broadcasted_iota(jnp.int32, (256, 512), 1)).astype(F32).astype(BF16)
    chosen = (pos_row == z * 32 + lax.broadcasted_iota(jnp.int32, (32, 256), 0)).astype(F32)
    mine = (pos_row == d * 4 + lax.broadcasted_iota(jnp.int32, (4, 256), 0)).astype(F32)
    small[9] = jnp.broadcast_to(jnp.sum(mine, axis=1, keepdims=True), (4, 128))

    for f in FLOWS:
        keep(f, 1)
    for f in FLOWS:
        along_x, p, qq, c1, c2, peer1, peer2 = flows[f]
        core[f, 1].wait_recv()
        step2[f].wait_recv()
        part[f, c1] = part[f, c1] + core_in[f, 1] + in2[f]
        for o in (2, 1, 3):
            to = (c2 + o) % 4
            remote(
                part.at[f, c1, to], in3.at[f, o - 1], send_sem.at[6], dim2_sem.at[f], peer2(to)
            )
        if f == 0:

            @pl.when(c == 1)
            def _():
                relay(2)

    pl.semaphore_wait(token_sem.at[2], 2)

    def reduce_z(to):
        @pl.when(z != to)
        def _():
            remote(
                zsend.at[to],
                zin.at[(to - z + NZ) % NZ],
                send_sem.at[7],
                z_sem.at[0],
                dev(to, x, c, y),
            )

    for f in FLOWS:
        along_x, p, qq, c1, c2, peer1, peer2 = flows[f]
        drain(in3.at[f], dim2_sem.at[f])
        total = part[f, c1, c2] + in3[f, 0] + in3[f, 1] + in3[f, 2]
        for k in range(4):
            zsend[4 * f + k] = total[16 * k : 16 * k + 16]
        for k in range(4):
            reduce_z(4 * f + k)
        if f == 0:

            @pl.when(c == 1)
            def _():
                relay(3)

    order = [8, 7, 9, 6, 10, 5, 11, 4, 12, 3, 13, 2, 14, 1, 15]
    zin[0] = zsend[z]

    @pl.when(c == 1)
    def _():
        relay(4)
        relay(5)

    first_fix, second_fix = corrections(step_ref)
    drain(zin.at[pl.ds(1, 15)], z_sem.at[0])
    sums[z] = jnp.sum(zin[...], axis=0)
    for o in order:
        to = (z + o) % NZ
        remote(sums.at[z], sums.at[z], send_sem.at[8], z_sem.at[1], dev(to, x, c, y))

    @pl.when(c == 1)
    def _():
        relay(6)
        relay(7)

    drain(sums.at[pl.ds(0, 15)], z_sem.at[1])

    summed = sums[...].reshape(256, 128)
    squares[q] = jnp.sum(summed * summed, axis=0, keepdims=True)
    for o in range(1, 32):
        t = (q + o) % 32
        remote(
            squares.at[q],
            squares.at[q],
            send_sem.at[9],
            norm_sem.at[0],
            dev(z, (t // 2) % 4, t % 2, t // 8),
        )
    picked = jnp.dot(chosen, summed, precision=HIGH, preferred_element_type=F32)
    for k in range(8):
        sel_out[k] = picked[4 * k : 4 * k + 4]
    for o in range(1, 8):
        remote(
            sel_out.at[(w + o) % 8], small.at[slab], send_sem.at[11], norm_sem.at[1], xc_peer(o)
        )
    small[slab] = sel_out[w]

    @pl.when(c == 1)
    def _():
        take_state(8, 0)
        hand_over(8)
        take_state(8, 1)


    @pl.when(c == 0)
    def _():
        drain(opt_all.at[pl.ds(0, 8)], opt_sem.at[1])

    pieces = []
    for a in range(3):
        table = opt_all[:, c, a].reshape(512, 128)
        for _ in range(3):
            pieces.append(table.astype(BF16))
            table = table - pieces[-1].astype(F32)
    spread = jnp.dot(
        onehot[...], jnp.concatenate(pieces, axis=1), preferred_element_type=F32
    )
    thirds = [spread[:, 128 * i : 128 * i + 128] for i in range(9)]
    states = [thirds[3 * a] + thirds[3 * a + 1] + thirds[3 * a + 2] for a in range(3)]
    drain(squares.at[pl.ds(0, 31)], norm_sem.at[0])
    squares_total = jnp.sum(jnp.sum(squares[...], axis=0), keepdims=True)
    limit = jnp.float32(1024.0)
    scale = limit / jnp.maximum(jnp.sqrt(squares_total), limit)
    rounded = adam(summed, *states, scale, first_fix, second_fix)[0].astype(BF16)

    def forward(f, j):
        along_x, p, qq, c1, c2, peer1, peer2 = flows[f]
        piece = w_part.at[f, c1, j]
        remote(piece, piece, send_sem.at[13], ag1_sem.at[f, 0], peer1(qq))
        remote(piece, piece, send_sem.at[13], ag1_sem.at[f, 1], peer1(p))
        remote(piece, piece, send_sem.at[13], ag1_sem.at[f, 2], peer1(flip2(c1)))

    ag2 = {}
    for f in FLOWS:
        along_x, p, qq, c1, c2, peer1, peer2 = flows[f]
        w_part[f, c1, c2] = rounded[64 * f : 64 * f + 64]
        own = w_part.at[f, c1, c2]
        for o in (1, 3, 2):
            ag2[f, o] = remote(
                own, own, send_sem.at[12], ag2_sem.at[f, o - 1], peer2((c2 + o) % 4)
            )
    for f in FLOWS:
        forward(f, flows[f][4])
    small[8] = jnp.broadcast_to(scale, (4, 128))

    def give(f, index):
        piece = w_part.at[f, index]
        remote(piece, w_all.at[c, f, index], send_sem.at[14], out_sem.at[0], partner)
        pltpu.make_async_copy(piece, w_all.at[c, f, index], out_sem.at[1]).start()

    for o in (1, 3, 2):
        for f in FLOWS:
            ag2[f, o].wait_recv()
            forward(f, (flows[f][4] + 4 - o) % 4)
    for f in FLOWS:
        give(f, flows[f][3])
    drain(small.at[pl.ds(0, 7)], norm_sem.at[1])
    small_copy = pltpu.make_async_copy(small, small_hbm, out_sem.at[2])
    small_copy.start()
    for f in FLOWS:
        along_x, p, qq, c1, c2, peer1, peer2 = flows[f]
        got = w_part.at[f, qq]
        drain(got, ag1_sem.at[f, 0])
        give(f, qq)
    for f in FLOWS:
        got = w_part.at[f, flows[f][1]]
        drain(got, ag1_sem.at[f, 1])
        give(f, flows[f][1])
    for f in FLOWS:
        got = w_part.at[f, flip2(flows[f][3])]
        drain(got, ag1_sem.at[f, 2])
        give(f, flip2(flows[f][3]))

    small_copy.wait()

    @pl.when(c == 0)
    def _():
        drain(opt_out, send_sem.at[0])

    @pl.when(c == 1)
    def _():
        drain(opt_out.at[pl.ds(0, 3)], send_sem.at[0])
        drain(opt_all.at[pl.ds(0, 15)], send_sem.at[3])
        drain(opt_all.at[pl.ds(0, 8)], send_sem.at[10])

    drain(in1x, send_sem.at[1])
    drain(in1y, send_sem.at[2])
    drain(core_out, send_sem.at[4])
    drain(in2, send_sem.at[5])
    drain(in3, send_sem.at[6])
    drain(zin.at[pl.ds(1, 15)], send_sem.at[7])
    drain(sums.at[pl.ds(0, 15)], send_sem.at[8])
    drain(squares.at[pl.ds(0, 31)], send_sem.at[9])
    drain(sel_out.at[pl.ds(0, 7)], send_sem.at[11])
    drain(w_part.at[0, pl.ds(0, 3)], send_sem.at[12])
    drain(w_part.at[pl.ds(0, 3)], send_sem.at[13])
    drain(w_part, send_sem.at[14])
    drain(w_part, out_sem.at[1])
    drain(w_all.at[1 - c], out_sem.at[0])


def result_kernel(
    w_all,
    small_hbm,
    step_ref,
    master_hbm,
    first_hbm,
    second_hbm,
    w_out,
    nm_out,
    nf_out,
    ns_out,
    small,
    state_in,
    state_out,
    w_in,
    rows,
    tmp,
    load_sem,
    in_sem,
    out_sem,
):
    loads = {}
    for f in range(4):
        for core in range(2):
            loads[f, core] = pltpu.make_async_copy(
                w_all.at[core, f], w_in.at[core, f], in_sem.at[f, core]
            )
            loads[f, core].start()
    inputs = []
    for i, (src, dst) in enumerate(
        (
            (small_hbm, small),
            (master_hbm, state_in.at[0]),
            (first_hbm, state_in.at[1]),
            (second_hbm, state_in.at[2]),
        )
    ):
        inputs.append(pltpu.make_async_copy(src, dst, load_sem.at[i]))
        inputs[i].start()
    fixes = corrections(step_ref)
    stores = []

    def store(src, dst):
        stores.append(pltpu.make_async_copy(src, dst, out_sem.at[len(stores)]))
        stores[-1].start()

    for f in range(4):
        if f == 2:
            for copy in inputs:
                copy.wait()
            scale = small[8, :1, :1]
            filled = small[9] > 0.5
            for k in range(8):
                cols = slice(128 * k, 128 * k + 128)
                olds = [state_in[a, 0, :, cols] for a in range(3)]
                for a, value in enumerate(adam(small[k], *olds, scale, *fixes)):
                    state_out[a, 0, :, cols] = jnp.where(filled, value, 0.0)
            for a, out in enumerate((nm_out, nf_out, ns_out)):
                store(state_out.at[a], out)
        for core in range(2):
            loads[f, core].wait()
            for k in range(4):
                for r in range(4):
                    i, j = (k, r) if f % 2 == 0 else (r, k)
                    tmp[k, pl.ds(r, 64, stride=4), :] = w_in[core, f, i, j].astype(F32)
                at = 512 * core + 128 * k
                rows[f, :, at : at + 128] = tmp[k].astype(BF16)
            half = pl.ds(512 * core, 512)
            store(rows.at[f, :, half], w_out.at[pl.ds(256 * f, 256), half])
    for copy in stores:
        copy.wait()


def local_step(gradient, owner_list, step_count, master, first_moment, second_moment):
    smem = pl.BlockSpec(memory_space=pltpu.SMEM)
    anywhere = pl.BlockSpec(memory_space=pl.ANY)
    dma = pltpu.SemaphoreType.DMA
    w_all, small = pl.pallas_call(
        reduce_kernel,
        out_shape=(
            jax.ShapeDtypeStruct((2, 4, 4, 4, 64, 128), BF16),
            jax.ShapeDtypeStruct((10, 4, 128), F32),
        ),
        in_specs=[anywhere, anywhere, smem, anywhere, anywhere, anywhere],
        out_specs=(anywhere, anywhere),
        scratch_shapes=[
            pltpu.VMEM((1, owner_list.shape[0]), jnp.int32),
            pltpu.VMEM((3, *master.shape), F32),
            pltpu.VMEM((10, 4, 128), F32),
            pltpu.VMEM((1024, 1024), BF16),
            pltpu.VMEM((2, 4, 2, 4, 64, 128), BF16),
            pltpu.VMEM((2, 256, 128), F32),
            pltpu.VMEM((2, 4, 256, 128), BF16),
            pltpu.VMEM((2, 4, 4, 64, 128), BF16),
            pltpu.VMEM((4, 2, 4, 64, 128), F32),
            pltpu.VMEM((4, 2, 4, 64, 128), F32),
            pltpu.VMEM((4, 4, 4, 64, 128), F32),
            pltpu.VMEM((4, 4, 64, 128), F32),
            pltpu.VMEM((4, 3, 64, 128), F32),
            pltpu.VMEM((NZ, 16, 128), F32),
            pltpu.VMEM((NZ, 16, 128), F32),
            pltpu.VMEM((NZ, 16, 128), F32),
            pltpu.VMEM((32, 1, 128), F32),
            pltpu.VMEM((8, 4, 128), F32),
            pltpu.VMEM((4, 2, 3, 4, 128), F32),
            pltpu.VMEM((8, 2, 3, 4, 128), F32),
            pltpu.VMEM((NZ, 2, 3, 32, 128), F32),
            pltpu.VMEM((256, 512), BF16),
            pltpu.VMEM((4, 4, 4, 64, 128), BF16),
            dma((8,)),
            dma((4, 4)),
            dma((4, 2)),
            dma((4,)),
            dma((4,)),
            dma((2,)),
            dma((2, 16)),
            dma((2,)),
            dma((2,)),
            dma((4, 3)),
            dma((4, 3)),
            dma((3,)),
            dma((15,)),
            pltpu.SemaphoreType.REGULAR((3,)),
        ],
        compiler_params=pltpu.CompilerParams(collective_id=0, has_side_effects=True),
        name="adam_reduce",
    )(
        gradient.reshape(gradient.shape[2:]),
        owner_list.reshape(1, owner_list.shape[0]),
        step_count,
        master,
        first_moment,
        second_moment,
    )
    state = jax.ShapeDtypeStruct(master.shape, F32)
    return pl.pallas_call(
        result_kernel,
        out_shape=(jax.ShapeDtypeStruct((1024, 1024), BF16), state, state, state),
        in_specs=[anywhere, anywhere, smem, anywhere, anywhere, anywhere],
        out_specs=(anywhere, anywhere, anywhere, anywhere),
        scratch_shapes=[
            pltpu.VMEM((10, 4, 128), F32),
            pltpu.VMEM((3, *master.shape), F32),
            pltpu.VMEM((3, *master.shape), F32),
            pltpu.VMEM((2, 4, 4, 4, 64, 128), BF16),
            pltpu.VMEM((4, 256, 1024), BF16),
            pltpu.VMEM((4, 256, 128), F32),
            dma((4,)),
            dma((4, 2)),
            dma((11,)),
        ],
        name="adam_results",
    )(w_all, small, step_count, master, first_moment, second_moment)


def solution(mesh):
    owned = P("dp", None, "rep")
    return jax.shard_map(
        local_step,
        mesh=mesh,
        in_specs=(P("dp", "rep", None, None), P(), P(), owned, owned, owned),
        out_specs=(P(), owned, owned, owned),
        check_vma=False,
    )
```
